32 devices in a mesh: grp: 4 (over y, x), seq: 8 (over z, core).
Axes of the slice: x: 2, y: 2, z: 4, core: 2. Of those that a mesh axis runs over, the one named last changes fastest.
Arguments:
- tokens: bfloat16 [32, 832, 1024], P('grp', 'seq'), may hold values from -6 to 6
- counts: int32 [32, 8], P('grp', 'seq'), may hold values from 1 to 104, as said below
- w_qkv: bfloat16 [1024, 3072], P(('grp', 'seq')), may hold values from -0.1875 to 0.1875
- bias_q: bfloat16 [1024], P(('grp', 'seq')), may hold values from -3 to 3
- bias_v: bfloat16 [1024], P(('grp', 'seq')), may hold values from -3 to 3
- w_out: bfloat16 [1024, 1024], P(('grp', 'seq')), may hold values from -3.5 to 3.5
- bias_out: bfloat16 [1024], P(('grp', 'seq')), may hold values from -3 to 3
- w_up: bfloat16 [1024, 4096], P(('grp', 'seq')), may hold values from -0.1875 to 0.1875
- bias_up: bfloat16 [4096], P(('grp', 'seq')), may hold values from -3 to 3
- w_down: bfloat16 [4096, 1024], P(('grp', 'seq')), may hold values from -0.09375 to 0.09375
- bias_down: bfloat16 [1024], P(('grp', 'seq')), may hold values from -3 to 3
- gain_one: bfloat16 [1024], P(('grp', 'seq')), may hold values from 0.099609375 to 1.8984375
- shift_one: bfloat16 [1024], P(('grp', 'seq')), may hold values from -3 to 3
- gain_two: bfloat16 [1024], P(('grp', 'seq')), may hold values from 0.099609375 to 1.8984375
- shift_two: bfloat16 [1024], P(('grp', 'seq')), may hold values from -3 to 3
- cotangent: bfloat16 [32, 832, 1024], P('grp', 'seq'), may hold values from -6 to 6
Outputs:
- result: bfloat16 [32, 832, 1024], P('grp', 'seq')
- grad_tokens: float32 [32, 832, 1024], P('grp', 'seq')
- grad_w_qkv: float32 [1024, 3072], P(('grp', 'seq'))
- grad_bias_q: float32 [1024], P(('grp', 'seq'))
- grad_bias_v: float32 [1024], P(('grp', 'seq'))
- grad_w_out: float32 [1024, 1024], P(('grp', 'seq'))
- grad_bias_out: float32 [1024], P(('grp', 'seq'))
- grad_w_up: float32 [1024, 4096], P(('grp', 'seq'))
- grad_bias_up: float32 [4096], P(('grp', 'seq'))
- grad_w_down: float32 [4096, 1024], P(('grp', 'seq'))
- grad_bias_down: float32 [1024], P(('grp', 'seq'))
- grad_gain_one: float32 [1024], P(('grp', 'seq'))
- grad_shift_one: float32 [1024], P(('grp', 'seq'))
- grad_gain_two: float32 [1024], P(('grp', 'seq'))
- grad_shift_two: float32 [1024], P(('grp', 'seq'))
The draws below stay inside these ranges and needn't reach their ends.
Inputs may be any that keep to these rules, and one draw needn't show every extreme that they name: For each image the counts over the 8 devices of its group sum to 577, and one device holds exactly 104 of its tokens.
All inputs are finite; a program needn't handle non-finite values.
Results may differ from the reference program's by a relative error of at most 0.014.
Values may be sent and summed in bfloat16 or wider, within the bound.
No kernel may reach another device: no remote copies, remote signals or barrier semaphores. Data moves between devices by JAX's collectives and lax.ppermute only.
A program may use at most 264 MiB of HBM per device.

```python
import jax
import jax.numpy as jnp
from jax import lax

D = 1024
FF = 4096
H = 16
HD = 64
LENGTH = 577
MOST = 104
SLOTS = 832
IMAGES = 32
N_SEQ = 8


def draw_counts(key, part):
    rest_total = LENGTH - MOST
    others = N_SEQ - 1
    base = rest_total // others
    extra = rest_total % others
    reach = max(min(MOST - base - 1, base - 1), 0)

    def one_image(image_key):
        first_key, second_key = jax.random.split(image_key)
        lift = jax.random.randint(first_key, (others,), 0, reach + 1)
        spread = lift - jnp.roll(lift, 1)
        drawn = base + (jnp.arange(others) < extra).astype(jnp.int32)
        row_counts = jnp.concatenate([jnp.full((1,), MOST, jnp.int32), (drawn + spread).astype(jnp.int32)])
        order = jax.random.permutation(second_key, N_SEQ)
        return row_counts[order]
    image_keys = jax.random.split(key, IMAGES)
    return jax.vmap(one_image)(image_keys).astype(jnp.int32)


def steps_of(key, shape, pieces, least, largest):
    gain = 1.0
    for dim, parts in pieces:
        draws = jax.random.uniform(jax.random.fold_in(jax.random.fold_in(key, 6), dim), (parts,), jnp.float32, least / len(pieces), largest / len(pieces))
        gain = gain * jnp.repeat(jnp.exp(draws), shape[dim] // parts).reshape((-1,) + (1,) * (len(shape) - 1 - dim))
    return gain


def normal_values(key, extent, deviation, most, cuts=(), held_as=jnp.bfloat16):
    level = steps_of(key, extent, cuts, -0.22, 0.18) if cuts else 1.0
    drawn = jax.random.normal(key, extent, jnp.float32) * deviation * level
    return jnp.minimum(jnp.maximum(drawn, -most), most).astype(held_as)


def setup_inputs(seed: int = 0) -> dict:
    splits = jax.random.split(jax.random.key(seed), 17)
    tokens = normal_values(splits[0], (IMAGES, SLOTS, D), 1.0, 6.0, ((0, 4), (1, 8)))
    counts = draw_counts(jax.random.fold_in(splits[16], 71), 0)
    w_qkv = normal_values(splits[2], (D, 3 * D), D ** -0.5, 0.1875, ((0, 32),))
    bias_q = normal_values(splits[3], (D,), 0.5, 3.0, ((0, 32),))
    bias_v = normal_values(splits[4], (D,), 0.5, 3.0, ((0, 32),))
    w_out = normal_values(splits[5], (D, D), (max(2 * D // LENGTH, 1)) ** -0.5, 3.5, ((0, 32),))
    bias_out = normal_values(splits[6], (D,), 0.5, 3.0, ((0, 32),))
    w_up = normal_values(splits[7], (D, FF), D ** -0.5, 0.1875, ((0, 32),))
    bias_up = normal_values(splits[8], (FF,), 0.5, 3.0, ((0, 32),))
    w_down = normal_values(splits[9], (FF, D), FF ** -0.5, 0.09375, ((0, 32),))
    bias_down = normal_values(splits[10], (D,), 0.5, 3.0, ((0, 32),))
    gain_one = jnp.clip(1.0 + 0.18 * jax.random.normal(splits[11], (D,), jnp.float32), 0.099609375, 1.8984375).astype(jnp.bfloat16)
    shift_one = normal_values(splits[12], (D,), 0.5, 3.0, ((0, 32),))
    gain_two = jnp.clip(1.0 + 0.18 * jax.random.normal(splits[13], (D,), jnp.float32), 0.099609375, 1.8984375).astype(jnp.bfloat16)
    shift_two = normal_values(splits[14], (D,), 0.5, 3.0, ((0, 32),))
    cotangent = normal_values(splits[15], (IMAGES, SLOTS, D), 1.0, 6.0, ((0, 4), (1, 8)))
    return dict(tokens=tokens, counts=counts, w_qkv=w_qkv, bias_q=bias_q, bias_v=bias_v, w_out=w_out, bias_out=bias_out, w_up=w_up, bias_up=bias_up, w_down=w_down, bias_down=bias_down, gain_one=gain_one, shift_one=shift_one, gain_two=gain_two, shift_two=shift_two, cotangent=cotangent)


@jax.custom_vjp
def low(v):
    return lax.optimization_barrier(v.astype(jnp.bfloat16)).astype(jnp.float32)

@jax.custom_vjp
def low_back(v):
    return v

def low_keep(v):
    return (low(v), None)

def low_pass(kept, grad):
    return (grad,)

def back_keep(v):
    return (v, None)

def back_low(kept, grad):
    return (low(grad),)
low.defvjp(low_keep, low_pass)
low_back.defvjp(back_keep, back_low)
EPSILON = 1e-06
NEGATIVE = -1e+30
HIGHEST = lax.Precision.HIGHEST

def norm_rows(values, gain_vec, shift_vec):
    row_mean = lax.optimization_barrier(jnp.mean(values, axis=-1, keepdims=True))
    centred = values - row_mean
    row_var = lax.optimization_barrier(jnp.mean(centred * centred, axis=-1, keepdims=True))
    return centred * lax.rsqrt(row_var + EPSILON) * gain_vec + shift_vec

def product(left, right):
    return jnp.dot(left, right, precision=HIGHEST, preferred_element_type=jnp.float32)

def layer(tokens_f, valid_slots, params):
    w_qkv, bias_q, bias_v, w_out, bias_out, w_up, bias_up, w_down, bias_down, gain_one, shift_one, gain_two, shift_two = params
    slot_total = tokens_f.shape[0]
    score_scale = HD ** (-0.5)
    normed = low(norm_rows(tokens_f, gain_one, shift_one))
    joined = product(normed, w_qkv)
    query_rows = low_back(low(joined[:, :D] + bias_q)).reshape(slot_total, H, HD)
    key_rows = low_back(low(joined[:, D:2 * D])).reshape(slot_total, H, HD)
    value_rows = low_back(low(joined[:, 2 * D:] + bias_v)).reshape(slot_total, H, HD)
    raw_scores = jnp.einsum('qhd,khd->hqk', query_rows, key_rows, precision=HIGHEST) * score_scale
    scores = jnp.where(valid_slots[None, None, :] > 0, low_back(raw_scores), NEGATIVE)
    row_top = lax.optimization_barrier(jnp.max(scores, axis=-1, keepdims=True))
    exponent = jnp.exp(scores - row_top)
    soft_weights = exponent / lax.optimization_barrier(jnp.sum(exponent, axis=-1, keepdims=True))
    mixed_rows = jnp.einsum('hqk,khd->qhd', low(soft_weights), value_rows, precision=HIGHEST)
    mixed_rows = low_back(low(mixed_rows.reshape(slot_total, D)))
    branch = low_back(product(mixed_rows, w_out) + bias_out)
    residual = tokens_f + branch
    normed_two = low(norm_rows(residual, gain_two, shift_two))
    hidden = low_back(product(normed_two, w_up) + bias_up)
    active = low(jax.nn.gelu(hidden, approximate=False))
    output = low_back(product(active, w_down) + bias_down)
    return (residual + output) * valid_slots[:, None]

def reference(tokens, counts, w_qkv, bias_q, bias_v, w_out, bias_out, w_up, bias_up, w_down, bias_down, gain_one, shift_one, gain_two, shift_two, cotangent):
    params = tuple((weight.astype(jnp.float32) for weight in (w_qkv, bias_q, bias_v, w_out, bias_out, w_up, bias_up, w_down, bias_down, gain_one, shift_one, gain_two, shift_two)))
    slot_index = jnp.arange(SLOTS, dtype=jnp.int32)
    owner_index = slot_index // MOST
    local_index = slot_index % MOST

    def one_step(running, inputs):
        image_tokens, count_row, image_back = inputs
        valid_slots = (local_index < count_row[owner_index]).astype(jnp.float32)
        outcome, pull_back = jax.vjp(lambda tokens_f, weights: layer(tokens_f, valid_slots, weights), image_tokens.astype(jnp.float32), params)
        grad_input, grad_params = pull_back(image_back.astype(jnp.float32))
        running = tuple((total + grad for total, grad in zip(running, grad_params)))
        return (running, (outcome.astype(jnp.bfloat16), grad_input))
    start = tuple((jnp.zeros_like(weight) for weight in params))
    grad_sums, (outputs, grad_inputs) = lax.scan(one_step, start, (tokens, counts, cotangent))
    return (outputs, grad_inputs, grad_sums[0], grad_sums[1], grad_sums[2], grad_sums[3], grad_sums[4], grad_sums[5], grad_sums[6], grad_sums[7], grad_sums[8], grad_sums[9], grad_sums[10], grad_sums[11], grad_sums[12])
```

```python
import jax
import jax.numpy as jnp
import numpy as np
from jax import lax
from jax.experimental import pallas as pl
from jax.experimental.pallas import tpu as pltpu
from jax.sharding import Mesh
from jax.sharding import PartitionSpec as P

H = 16
HD = 64
LENGTH = 577
PACKED = 592
EPSILON = 1e-06
NEGATIVE = -1e30
ABSENT = 100.0
SMALL = 128
AXES = ("gy", "gx", "sz", "sc")

bf16 = jnp.bfloat16
f32 = jnp.float32


def norm_rows(values, gain_vec, shift_vec):
    row_mean = jnp.mean(values, axis=-1, keepdims=True)
    centred = values - row_mean
    row_var = jnp.mean(centred * centred, axis=-1, keepdims=True)
    return centred * lax.rsqrt(row_var + EPSILON) * gain_vec + shift_vec


def gelu_exact(values):
    return jax.nn.gelu(values, approximate=False)


def dot_float(left, right):
    return jnp.dot(left, right, preferred_element_type=f32)


def contract_rows(left, right):
    return lax.dot_general(left, right, (((0,), (0,)), ((), ())), preferred_element_type=f32)


def contract_cols(left, right):
    return lax.dot_general(left, right, (((1,), (1,)), ((), ())), preferred_element_type=f32)


def shifted(array, axis, size, step):
    return lax.ppermute(array, axis, [(i, (i + step) % size) for i in range(size)])


def pick(array, index, axis):
    return lax.dynamic_index_in_dim(array, index, axis, keepdims=False)


class Ring:
    def __init__(self, sizes):
        self.sizes = dict(zip(AXES, sizes))
        self.count = int(np.prod(sizes))

    def place(self):
        return {axis: lax.axis_index(axis) for axis in AXES}

    def others(self, array, axis):
        size = self.sizes[axis]
        return [shifted(array, axis, size, step) for step in range(1, size)]

    def gather(self, shard):
        rows, width = shard.shape
        cut = rows // 2
        columns = [shard] + self.others(shard, "sz")
        near, far = [], []
        halves = []
        for part in range(2):
            piece = jnp.stack([c[part * cut : (part + 1) * cut] for c in columns])
            halves.append([piece, ("gx", "gy") if part == 0 else ("gy", "gx")])
        first = [[piece] + self.others(piece, order[0]) for piece, order in halves]
        first = [jnp.stack(group) for group in first]
        first = lax.optimization_barrier(tuple(first))
        second = [self.others(group, order[1]) for group, (_, order) in zip(first, halves)]
        sources = []
        for part in range(2):
            order = halves[part][1]
            plane = [first[part]] + second[part]
            for turn in range(2):
                for step, group in enumerate(plane):
                    if turn:
                        group = shifted(group, "sc", 2, 1)
                    sources.append((group, part, order, turn, step))
        return self.assemble(sources, rows, width)

    def assemble(self, sources, rows, width):
        place = self.place()
        sizes = self.sizes
        cut = rows // 2
        targets = []
        arrays = []
        for group, part, order, turn, step in sources:
            inner, depth = group.shape[:2]
            arrays.append(group.reshape(inner * depth, cut, width))
            for one in range(inner):
                for k in range(depth):
                    at = dict(place)
                    at["sc"] = (place["sc"] - turn) % 2
                    at[order[1]] = (place[order[1]] - step) % sizes[order[1]]
                    at[order[0]] = (place[order[0]] - one) % sizes[order[0]]
                    at["sz"] = (place["sz"] - k) % sizes["sz"]
                    index = at["gy"]
                    for axis in AXES[1:]:
                        index = index * sizes[axis] + at[axis]
                    targets.append(index * 2 + part)
        table = jnp.stack(targets).astype(jnp.int32)
        total = len(targets)
        blocks = [a.shape[0] for a in arrays]

        def body(table_ref, *refs):
            ins, out, sems = refs[: len(blocks)], refs[-2], refs[-1]
            copies = []
            n = 0
            for ref, count in zip(ins, blocks):
                for k in range(count):
                    copies.append(pltpu.make_async_copy(ref.at[k], out.at[table_ref[n]], sems.at[n]))
                    n += 1
            for copy in copies:
                copy.start()
            for copy in copies:
                copy.wait()

        out = pl.pallas_call(
            body,
            out_shape=jax.ShapeDtypeStruct((total, cut, width), bf16),
            grid_spec=pltpu.PrefetchScalarGridSpec(
                num_scalar_prefetch=1,
                grid=(1,),
                in_specs=[pl.BlockSpec(memory_space=pl.ANY)] * len(blocks),
                out_specs=pl.BlockSpec(memory_space=pl.ANY),
                scratch_shapes=[pltpu.SemaphoreType.DMA((total,))],
            ),
            name="assemble",
        )(table, *arrays)
        return out.reshape(total * cut, width)

    def add(self, *arrays):
        total = arrays[0].astype(f32)
        for array in arrays[1:]:
            total = total + array.astype(f32)
        return total

    def fold(self, array, axis, at, low=True):
        size = self.sizes[axis]
        own = pick(array, at[axis], 0)
        came = [shifted(pick(array, (at[axis] + k) % size, 0), axis, size, k) for k in range(1, size)]
        total = self.add(own, *came)
        return total.astype(bf16) if low else total

    def scatter(self, grads):
        width = grads.shape[-1]
        rows = grads.shape[0] // self.count
        cut = rows // 2
        at = self.place()
        sizes = self.sizes
        grads = grads.reshape(sizes["gy"], sizes["gx"], sizes["sz"], 2, rows, width)
        own = pick(grads, at["sc"], 3)
        came = shifted(pick(grads, 1 - at["sc"], 3), "sc", 2, 1)
        total = self.add(own, came).astype(bf16)
        upper = total[:, :, :, :cut]
        lower = jnp.swapaxes(total[:, :, :, cut:], 0, 1)
        upper = self.fold(upper, "gy", at)
        lower = self.fold(lower, "gx", at)
        upper = self.fold(upper, "gx", at)
        lower = self.fold(lower, "gy", at)
        both = jnp.concatenate([upper, lower], axis=1)
        return self.fold(both, "sz", at, low=False)


def head_mask(part):
    lane = lax.broadcasted_iota(jnp.int32, (1, 2 * HD), 1)
    return (lane // HD == part).astype(bf16)


def soft_rows(query, key):
    scores = contract_cols(query, key) * (HD**-0.5)
    lane = lax.broadcasted_iota(jnp.int32, scores.shape, 1)
    scores = jnp.where(lane < LENGTH, scores, NEGATIVE)
    exponent = jnp.exp(scores - jnp.max(scores, axis=-1, keepdims=True))
    return exponent * (1.0 / jnp.sum(exponent, axis=-1, keepdims=True))


def mix_body(q_ref, k_ref, v_ref, o_ref):
    query, key, value = q_ref[...], k_ref[...], v_ref[...]
    total = None
    for part in range(2):
        mask = head_mask(part)
        soft = soft_rows(query * mask, key).astype(bf16)
        mixed = dot_float(soft, value * mask)
        total = mixed if total is None else total + mixed
    o_ref[...] = total.astype(bf16)


def attend(qkv):
    pairs = H // 2
    spec = lambda shift: pl.BlockSpec((PACKED, 2 * HD), lambda i, s=shift: (0, i + s))
    return pl.pallas_call(
        mix_body,
        out_shape=jax.ShapeDtypeStruct((PACKED, H * HD), bf16),
        grid=(pairs,),
        in_specs=[spec(0), spec(pairs), spec(2 * pairs)],
        out_specs=spec(0),
        compiler_params=pltpu.CompilerParams(vmem_limit_bytes=50 * 2**20),
        name="attend",
    )(qkv, qkv, qkv)


def mix_back_body(q_ref, k_ref, v_ref, g_ref, dq_ref, dk_ref, dv_ref):
    query, key, value, grad = q_ref[...], k_ref[...], v_ref[...], g_ref[...]
    scale = HD**-0.5
    sums = None
    for part in range(2):
        mask = head_mask(part)
        soft = soft_rows(query * mask, key)
        grad_part = grad * mask
        grad_soft = contract_cols(grad_part, value)
        delta = jnp.sum(soft * grad_soft, axis=-1, keepdims=True)
        grad_scores = (soft * (grad_soft - delta)).astype(bf16)
        terms = (
            dot_float(grad_scores, key * mask),
            contract_rows(grad_scores, query * mask),
            contract_rows(soft.astype(bf16), grad_part),
        )
        sums = terms if sums is None else tuple(a + b for a, b in zip(sums, terms))
    dq_ref[...] = (sums[0] * scale).astype(bf16)
    dk_ref[...] = (sums[1] * scale).astype(bf16)
    dv_ref[...] = sums[2].astype(bf16)


def attend_back(qkv, grad_mixed):
    pairs = H // 2
    spec = lambda shift: pl.BlockSpec((PACKED, 2 * HD), lambda i, s=shift: (0, i + s))
    return pl.pallas_call(
        mix_back_body,
        out_shape=[jax.ShapeDtypeStruct((PACKED, H * HD), bf16)] * 3,
        grid=(pairs,),
        in_specs=[spec(0), spec(pairs), spec(2 * pairs), spec(0)],
        out_specs=[spec(0)] * 3,
        compiler_params=pltpu.CompilerParams(vmem_limit_bytes=50 * 2**20),
        name="attend_back",
    )(qkv, qkv, qkv, grad_mixed)


def layer(ring, tokens, counts, w_qkv, bias_q, bias_v, w_out, bias_out, w_up, bias_up, w_down, bias_down, gain_one, shift_one, gain_two, shift_two, cotangent):
    images, slots, width = tokens.shape
    group = ring.sizes["sz"] * ring.sizes["sc"]
    twins = group // images
    rows = w_qkv.shape[0]
    wide = w_down.shape[0] // rows
    ff = w_up.shape[1]

    slot = lax.broadcasted_iota(jnp.int32, (images, slots, 1), 1)
    marked = jnp.where(slot < counts[:, :, None], tokens, jnp.asarray(ABSENT, bf16))

    def exchange(array):
        if twins > 1:
            array = jnp.repeat(array, twins, axis=0)
        return lax.all_to_all(array, ("sz", "sc"), 0, 0, tiled=True).reshape(group * slots, width)

    def exchange_back(array):
        array = lax.all_to_all(array.reshape(group, slots, width), ("sz", "sc"), 0, 0, tiled=True)
        return array[::twins] if twins > 1 else array

    image_slots = exchange(marked)
    cot_slots = exchange(cotangent)

    small = [bias_q, bias_v, bias_out, bias_down, gain_one, shift_one, gain_two, shift_two]
    small = jnp.stack(small + list(bias_up.reshape(wide, rows)), axis=1)
    small = jnp.pad(small, ((0, 0), (0, SMALL - small.shape[1])))
    gathered = ring.gather(jnp.concatenate([w_qkv, small], axis=1))
    full_qkv = gathered[:, : 3 * width]
    vectors = gathered[:, 3 * width :].astype(f32)
    bq, bv, bo, bd, g1, s1, g2, s2 = [vectors[:, k] for k in range(8)]
    bu = jnp.swapaxes(vectors[:, 8 : 8 + wide].reshape(ring.count, rows, wide), 1, 2).reshape(ff)
    gathered = ring.gather(jnp.concatenate([w_out, w_up], axis=1))
    full_out, full_up = gathered[:, :width], gathered[:, width:]
    full_down = ring.gather(w_down.reshape(rows, wide * width)).reshape(ff, width)

    here = (image_slots[:, :1].astype(f32) < 0.5 * ABSENT).reshape(group, slots)
    held = jnp.sum(here.astype(f32), axis=1)
    before = jnp.sum(jnp.where(np.tril(np.ones((group, group), bool), -1), held[None, :], 0.0), axis=1)
    rank = before[:, None] + lax.broadcasted_iota(jnp.int32, (group, slots), 1).astype(f32)
    rank = jnp.where(here, rank, -1.0).reshape(1, group * slots).astype(jnp.int32)
    packing = (rank == lax.broadcasted_iota(jnp.int32, (PACKED, group * slots), 0)).astype(bf16)
    tokens_f = dot_float(packing, image_slots)
    grad_low = dot_float(packing, cot_slots).astype(bf16)

    normed_f, norm_one_pull = jax.vjp(norm_rows, tokens_f, g1, s1)
    normed = normed_f.astype(bf16)
    qkv_bias = jnp.concatenate([bq, jnp.zeros((width,), f32), bv])
    qkv = (dot_float(normed, full_qkv) + qkv_bias).astype(bf16)
    mixed = attend(qkv)
    residual = tokens_f + dot_float(mixed, full_out) + bo
    normed_two_f, norm_two_pull = jax.vjp(norm_rows, residual, g2, s2)
    normed_two = normed_two_f.astype(bf16)
    hidden = dot_float(normed_two, full_up) + bu
    active_f, gelu_pull = jax.vjp(gelu_exact, hidden)
    active = active_f.astype(bf16)
    result = (residual + dot_float(active, full_down) + bd).astype(bf16)
    result = exchange_back(contract_rows(packing, result).astype(bf16))

    grad_y = grad_low.astype(f32)
    if twins > 1:
        share = (lax.axis_index(("sz", "sc")) % twins == 0).astype(f32)
    else:
        share = None

    def mine(array):
        return array if share is None else array * share

    grad_w_down = mine(contract_rows(active, grad_low)).astype(bf16).reshape(width, wide * width)
    sum_down = ring.scatter(grad_w_down).reshape(wide * rows, width)
    grad_bd = jnp.sum(grad_y, axis=0)
    (grad_hidden,) = gelu_pull(contract_cols(grad_low, full_down))
    hidden_low = grad_hidden.astype(bf16)
    grad_bu = jnp.sum(hidden_low.astype(f32), axis=0)
    grad_w_up = mine(contract_rows(normed_two, hidden_low)).astype(bf16)
    grad_residual, grad_g2, grad_s2 = norm_two_pull(contract_cols(hidden_low, full_up))
    grad_residual = grad_residual + grad_y
    residual_low = grad_residual.astype(bf16)
    grad_w_out = mine(contract_rows(mixed, residual_low)).astype(bf16)
    sums = ring.scatter(jnp.concatenate([grad_w_out, grad_w_up], axis=1))
    sum_out, sum_up = sums[:, :width], sums[:, width:]
    grad_bo = jnp.sum(residual_low.astype(f32), axis=0)
    grad_mixed = contract_cols(residual_low, full_out).astype(bf16)
    grad_joined = jnp.concatenate(attend_back(qkv, grad_mixed), axis=1)
    grad_w_qkv = mine(contract_rows(normed, grad_joined)).astype(bf16)
    joined_sum = jnp.sum(grad_joined.astype(f32), axis=0)
    grad_bq, grad_bv = joined_sum[:width], joined_sum[2 * width :]
    grad_tokens, grad_g1, grad_s1 = norm_one_pull(contract_cols(grad_joined, full_qkv))
    grad_tokens = (grad_tokens + grad_residual).astype(bf16)
    grad_tokens = exchange_back(contract_rows(packing, grad_tokens).astype(bf16)).astype(f32)

    small = [grad_bq, grad_bv, grad_bo, grad_bd, grad_g1, grad_s1, grad_g2, grad_s2]
    grad_bu = jnp.swapaxes(grad_bu.reshape(ring.count, wide, rows), 1, 2).reshape(width, wide)
    small = jnp.concatenate([jnp.stack(small, axis=1), grad_bu], axis=1)
    small = mine(jnp.pad(small, ((0, 0), (0, SMALL - small.shape[1])))).astype(bf16)
    sums = ring.scatter(jnp.concatenate([grad_w_qkv, small], axis=1))
    sum_qkv = sums[:, : 3 * width]
    vectors = sums[:, 3 * width :]
    sum_bq, sum_bv, sum_bo, sum_bd, sum_g1, sum_s1, sum_g2, sum_s2 = [vectors[:, k] for k in range(8)]
    sum_bu = jnp.swapaxes(vectors[:, 8 : 8 + wide], 0, 1).reshape(wide * rows)
    return (result, grad_tokens, sum_qkv, sum_bq, sum_bv, sum_out, sum_bo, sum_up, sum_bu, sum_down, sum_bd, sum_g1, sum_s1, sum_g2, sum_s2)


def solution(mesh):
    n_grp, n_seq = mesh.shape["grp"], mesh.shape["seq"]
    sizes = (n_grp // 2, 2, n_seq // 2, 2)
    fine = Mesh(mesh.devices.reshape(sizes), AXES)
    ring = Ring(sizes)
    grp, seq = AXES[:2], AXES[2:]
    by_token = P(grp, seq, None)
    rows, vec = P(AXES, None), P(AXES)
    in_specs = (by_token, P(grp, seq), rows, vec, vec, rows, vec, rows, vec, rows, vec, vec, vec, vec, vec, by_token)
    out_specs = (by_token, by_token, rows, vec, vec, rows, vec, rows, vec, rows, vec, vec, vec, vec, vec)

    def shards(*args):
        return layer(ring, *args)

    return jax.shard_map(shards, mesh=fine, in_specs=in_specs, out_specs=out_specs, check_vma=False)
```

```python
import jax
import jax.numpy as jnp
import numpy as np
from jax import lax
from jax.experimental import pallas as pl
from jax.experimental.pallas import tpu as pltpu
from jax.sharding import Mesh
from jax.sharding import PartitionSpec as P

H = 16
HD = 64
LENGTH = 577
PACKED = 592
EPSILON = 1e-06
NEGATIVE = -1e30
ABSENT = 100.0
SMALL = 128
AXES = ("gy", "gx", "sz", "sc")
ORDERS = (("gx", "gy"), ("gy", "gx"))

bf16 = jnp.bfloat16
f32 = jnp.float32


def norm_rows(values, gain_vec, shift_vec):
    row_mean = jnp.mean(values, axis=-1, keepdims=True)
    centred = values - row_mean
    row_var = jnp.mean(centred * centred, axis=-1, keepdims=True)
    return centred * lax.rsqrt(row_var + EPSILON) * gain_vec + shift_vec


def dot_float(left, right):
    return jnp.dot(left, right, preferred_element_type=f32)


def contract_rows(left, right):
    return lax.dot_general(left, right, (((0,), (0,)), ((), ())), preferred_element_type=f32)


def contract_cols(left, right):
    return lax.dot_general(left, right, (((1,), (1,)), ((), ())), preferred_element_type=f32)


def shifted(array, axis, size, step):
    return lax.ppermute(array, axis, [(i, (i + step) % size) for i in range(size)])


def pick(array, index, axis):
    return lax.dynamic_index_in_dim(array, index, axis, keepdims=False)


class Ring:
    def __init__(self, sizes):
        self.sizes = dict(zip(AXES, sizes))
        self.count = int(np.prod(sizes))

    def place(self):
        return {axis: lax.axis_index(axis) for axis in AXES}

    def others(self, array, axis):
        size = self.sizes[axis]
        return [shifted(array, axis, size, step) for step in range(1, size)]

    def along(self, shard):
        cut = shard.shape[0] // 2
        columns = [shard] + self.others(shard, "sz")
        return [jnp.stack([c[:cut] for c in columns]), jnp.stack([c[cut:] for c in columns])]

    def across(self, halves):
        return [jnp.stack([half] + self.others(half, order[0])) for half, order in zip(halves, ORDERS)]

    def plane(self, halves):
        return [[half] + self.others(half, order[1]) for half, order in zip(halves, ORDERS)]

    def cores(self, planes):
        sources = []
        for part, arrays in enumerate(planes):
            for turn in range(2):
                for step, group in enumerate(arrays):
                    if turn:
                        group = shifted(group, "sc", 2, 1)
                    sources.append((group, part, turn, step))
        return sources

    def assemble(self, sources, widths):
        place = self.place()
        sizes = self.sizes
        cut, width = sources[0][0].shape[-2:]
        targets = []
        arrays = []
        for group, part, turn, step in sources:
            order = ORDERS[part]
            inner, depth = group.shape[:2]
            arrays.append(group.reshape(inner * depth, cut, width))
            for one in range(inner):
                for k in range(depth):
                    at = dict(place)
                    at["sc"] = (place["sc"] - turn) % 2
                    at[order[1]] = (place[order[1]] - step) % sizes[order[1]]
                    at[order[0]] = (place[order[0]] - one) % sizes[order[0]]
                    at["sz"] = (place["sz"] - k) % sizes["sz"]
                    index = at["gy"]
                    for axis in AXES[1:]:
                        index = index * sizes[axis] + at[axis]
                    targets.append(index * 2 + part)
        table = jnp.stack(targets).astype(jnp.int32)
        total = len(targets)
        blocks = [a.shape[0] for a in arrays]
        starts = np.concatenate([[0], np.cumsum(widths)])

        def body(table_ref, *refs):
            ins = refs[: len(blocks)]
            outs = refs[len(blocks) : -3]
            held, came, left = refs[-3:]
            arrivals = []
            n = 0
            for ref, count in zip(ins, blocks):
                for k in range(count):
                    arrivals.append(pltpu.make_async_copy(ref.at[k], held.at[n], came.at[n]))
                    n += 1
            for copy in arrivals:
                copy.start()
            departures = []
            for n, copy in enumerate(arrivals):
                copy.wait()
                for i, out in enumerate(outs):
                    window = held.at[n, :, pl.ds(int(starts[i]), widths[i])]
                    leave = pltpu.make_async_copy(window, out.at[table_ref[n]], left.at[n, i])
                    leave.start()
                    departures.append(leave)
            for copy in departures:
                copy.wait()

        outs = pl.pallas_call(
            body,
            out_shape=[jax.ShapeDtypeStruct((total, cut, w), bf16) for w in widths],
            grid_spec=pltpu.PrefetchScalarGridSpec(
                num_scalar_prefetch=1,
                grid=(1,),
                in_specs=[pl.BlockSpec(memory_space=pl.ANY)] * len(blocks),
                out_specs=[pl.BlockSpec(memory_space=pl.ANY)] * len(widths),
                scratch_shapes=[
                    pltpu.VMEM((total, cut, width), bf16),
                    pltpu.SemaphoreType.DMA((total,)),
                    pltpu.SemaphoreType.DMA((total, len(widths))),
                ],
            ),
            compiler_params=pltpu.CompilerParams(vmem_limit_bytes=50 * 2**20),
            name="assemble",
        )(table, *arrays)
        return [out.reshape(total * cut, w) for out, w in zip(outs, widths)]

    def add(self, *arrays):
        total = arrays[0].astype(f32)
        for array in arrays[1:]:
            total = total + array.astype(f32)
        return total

    def fold(self, array, axis, at, low=True):
        size = self.sizes[axis]
        own = pick(array, at[axis], 0)
        came = [shifted(pick(array, (at[axis] + k) % size, 0), axis, size, k) for k in range(1, size)]
        total = self.add(own, *came)
        return total.astype(bf16) if low else total

    def between(self, grads):
        at = self.place()
        sizes = self.sizes
        sums = []
        for array in grads:
            array = array.reshape(sizes["gy"], sizes["gx"], sizes["sz"], 2, array.shape[0] // self.count, array.shape[-1])
            own = pick(array, at["sc"], 3)
            came = shifted(pick(array, 1 - at["sc"], 3), "sc", 2, 1)
            sums.append((own, came))
        return sums

    def halves(self, sums):
        total = [self.add(own, came).astype(bf16) for own, came in sums]
        total = total[0] if len(total) == 1 else jnp.concatenate(total, axis=-1)
        cut = total.shape[3] // 2
        return total[:, :, :, :cut], jnp.swapaxes(total[:, :, :, cut:], 0, 1)

    def inward(self, pair):
        at = self.place()
        return self.fold(pair[0], "gy", at), self.fold(pair[1], "gx", at)

    def inward_more(self, pair):
        at = self.place()
        return self.fold(pair[0], "gx", at), self.fold(pair[1], "gy", at)

    def down(self, pair):
        return self.fold(jnp.concatenate(pair, axis=1), "sz", self.place(), low=False)


def tie(*values):
    return lax.optimization_barrier(values)


def room(mib=50):
    return pltpu.CompilerParams(vmem_limit_bytes=mib * 2**20)


def of_head(part):
    return lax.broadcasted_iota(jnp.int32, (1, 2 * HD), 1) // HD == part


def mask_tail(scores, fill):
    start = LENGTH // 8 * 8
    row = lax.broadcasted_iota(jnp.int32, (PACKED - start, PACKED), 0)
    tail = jnp.where(row < LENGTH - start, scores[start:], fill)
    return jnp.concatenate([scores[:start], tail], axis=0)


def flip(array):
    return array.astype(f32).T.astype(bf16)


def attend_body(q_ref, k_ref, v_ref, o_ref, l_ref):
    query, key = q_ref[...] * jnp.asarray(HD**-0.5, bf16), k_ref[...]
    value_t = flip(v_ref[...])
    mixed, logs = [], []
    for part in range(2):
        scores = contract_cols(jnp.where(of_head(part), key, 0), query)
        scores = mask_tail(scores, NEGATIVE)
        top = jnp.max(scores, axis=0, keepdims=True)
        exponent = jnp.exp(scores - top)
        total = jnp.sum(exponent, axis=0, keepdims=True)
        out = dot_float(value_t[HD * part : HD * (part + 1)], exponent.astype(bf16))
        mixed.append(out * (1.0 / total))
        logs.append(top + jnp.log(total))
    o_ref[...] = jnp.concatenate(mixed, axis=0).T.astype(bf16)
    l_ref[...] = jnp.concatenate(logs + [jnp.zeros((6, PACKED), f32)], axis=0)


PAIR = (PACKED, 2 * HD)
PAIRS = H // 2


def pair_spec(shift=0):
    return pl.BlockSpec(PAIR, lambda i: (0, i + shift))


LOG_SPEC = pl.BlockSpec((8, PACKED), lambda i: (i, 0))


def attend(qkv):
    return pl.pallas_call(
        attend_body,
        out_shape=[
            jax.ShapeDtypeStruct((PACKED, H * HD), bf16),
            jax.ShapeDtypeStruct((8 * PAIRS, PACKED), f32),
        ],
        grid=(PAIRS,),
        in_specs=[pair_spec(), pair_spec(PAIRS), pair_spec(2 * PAIRS)],
        out_specs=[pair_spec(), LOG_SPEC],
        compiler_params=room(),
        name="attend",
    )(qkv, qkv, qkv)


def attend_back_body(q_ref, k_ref, v_ref, o_ref, l_ref, g_ref, dq_ref, dk_ref, dv_ref):
    scale = jnp.asarray(HD**-0.5, bf16)
    query, key, value, grad = q_ref[...] * scale, k_ref[...], v_ref[...], g_ref[...]
    product = (grad.astype(f32) * o_ref[...].astype(f32)).T
    key_t = flip(key)
    grad_query, grad_key, grad_value = [], [], []
    for part in range(2):
        mask = of_head(part)
        delta = jnp.sum(product[HD * part : HD * (part + 1)], axis=0, keepdims=True)
        scores = contract_cols(jnp.where(mask, key, 0), query)
        soft = mask_tail(jnp.exp(scores - l_ref[part : part + 1]), 0.0)
        grad_soft = contract_cols(jnp.where(mask, value, 0), grad)
        grad_scores = (soft * (grad_soft - delta)).astype(bf16)
        grad_value.append(dot_float(soft.astype(bf16), grad))
        grad_key.append(dot_float(grad_scores, query))
        grad_query.append(dot_float(key_t[HD * part : HD * (part + 1)], grad_scores))
    first = of_head(0)
    dq_ref[...] = (jnp.concatenate(grad_query, axis=0).T * HD**-0.5).astype(bf16)
    dk_ref[...] = jnp.where(first, grad_key[0], grad_key[1]).astype(bf16)
    dv_ref[...] = jnp.where(first, grad_value[0], grad_value[1]).astype(bf16)


def attend_back(qkv, mixed, logs, grad_mixed):
    return pl.pallas_call(
        attend_back_body,
        out_shape=[jax.ShapeDtypeStruct((PACKED, H * HD), bf16)] * 3,
        grid=(PAIRS,),
        in_specs=[pair_spec(), pair_spec(PAIRS), pair_spec(2 * PAIRS), pair_spec(), LOG_SPEC, pair_spec()],
        out_specs=[pair_spec()] * 3,
        compiler_params=room(),
        name="attend_back",
    )(qkv, qkv, qkv, mixed, logs, grad_mixed)


def rise_body(x_ref, w_ref, b_ref, active_ref, slope_ref):
    hidden = dot_float(x_ref[...], w_ref[...]) + b_ref[...]
    share = 0.5 * (1.0 + lax.erf(hidden * np.float32(np.sqrt(0.5))))
    active_ref[...] = (hidden * share).astype(bf16)
    bell = jnp.exp(hidden * hidden * -0.5) * np.float32(1.0 / np.sqrt(2.0 * np.pi))
    slope_ref[...] = share + hidden * bell


def rise(normed, weights, bias):
    width, ff = weights.shape
    step = 1024
    return pl.pallas_call(
        rise_body,
        out_shape=[jax.ShapeDtypeStruct((PACKED, ff), bf16), jax.ShapeDtypeStruct((PACKED, ff), f32)],
        grid=(ff // step,),
        in_specs=[
            pl.BlockSpec((PACKED, width), lambda i: (0, 0)),
            pl.BlockSpec((width, step), lambda i: (0, i)),
            pl.BlockSpec((1, step), lambda i: (0, i)),
        ],
        out_specs=[pl.BlockSpec((PACKED, step), lambda i: (0, i))] * 2,
        compiler_params=room(),
        name="rise",
    )(normed, weights, bias.reshape(1, ff))


def layer(ring, tokens, counts, w_qkv, bias_q, bias_v, w_out, bias_out, w_up, bias_up, w_down, bias_down, gain_one, shift_one, gain_two, shift_two, cotangent):
    images, slots, width = tokens.shape
    group = ring.sizes["sz"] * ring.sizes["sc"]
    twins = group // images
    rows = w_qkv.shape[0]
    wide = w_down.shape[0] // rows
    ff = w_up.shape[1]

    slot = lax.broadcasted_iota(jnp.int32, (images, slots, 1), 1)
    marked = jnp.where(slot < counts[:, :, None], tokens, jnp.asarray(ABSENT, bf16))

    def exchange(array):
        if twins > 1:
            array = jnp.repeat(array, twins, axis=0)
        return lax.all_to_all(array, ("sz", "sc"), 0, 0, tiled=True).reshape(group * slots, width)

    def exchange_back(array):
        array = lax.all_to_all(array.reshape(group, slots, width), ("sz", "sc"), 0, 0, tiled=True)
        return array[::twins] if twins > 1 else array

    small = [bias_q, bias_v, bias_out, bias_down, gain_one, shift_one, gain_two, shift_two]
    small = jnp.stack(small + list(bias_up.reshape(wide, rows)), axis=1)
    small = jnp.pad(small, ((0, 0), (0, SMALL - small.shape[1])))

    def arrays_of(sources):
        return [source[0] for source in sources]

    def with_arrays(sources, arrays):
        return [(array,) + source[1:] for array, source in zip(arrays, sources)]

    one = ring.along(jnp.concatenate([w_qkv, small], axis=1))
    two = jnp.concatenate([w_out, w_up], axis=1)
    one, two, marked = tie(one, two, marked)
    one = ring.across(one)
    two = ring.along(two)
    one, two, marked = tie(one, two, marked)
    image_slots = exchange(marked)
    one = ring.plane(one)
    one, two = tie(one, two)
    full_qkv, vectors = ring.assemble(ring.cores(one), [3 * width, SMALL])
    two = ring.across(two)
    image_slots, two, full_qkv, vectors, three = tie(image_slots, two, full_qkv, vectors, w_down)

    two = ring.plane(two)
    three = ring.along(three)
    vectors = vectors.astype(f32)
    bq, bv, bo, bd, g1, s1, g2, s2 = [vectors[:, k] for k in range(8)]
    bu = jnp.swapaxes(vectors[:, 8 : 8 + wide].reshape(ring.count, rows, wide), 1, 2).reshape(ff)
    here = (image_slots[:, :1].astype(f32) < 0.5 * ABSENT).reshape(group, slots)
    held = jnp.sum(here.astype(f32), axis=1)
    before = jnp.sum(jnp.where(np.tril(np.ones((group, group), bool), -1), held[None, :], 0.0), axis=1)
    rank = before[:, None] + lax.broadcasted_iota(jnp.int32, (group, slots), 1).astype(f32)
    rank = jnp.where(here, rank, -1.0).reshape(1, group * slots).astype(jnp.int32)
    packing = (rank == lax.broadcasted_iota(jnp.int32, (PACKED, group * slots), 0)).astype(bf16)
    tokens_f = dot_float(packing, image_slots)
    normed_f, norm_one_pull = jax.vjp(norm_rows, tokens_f, g1, s1)
    normed = normed_f.astype(bf16)
    qkv_bias = jnp.concatenate([bq, jnp.zeros((width,), f32), bv])
    qkv = (dot_float(normed, full_qkv) + qkv_bias).astype(bf16)
    two, three, qkv, cotangent = tie(two, three, qkv, cotangent)

    two = ring.cores(two)
    three = ring.across(three)
    cot_slots = exchange(cotangent)
    mixed, logs = attend(qkv)
    traded, three, mixed = tie(arrays_of(two), three, mixed)

    three = ring.plane(three)
    full_out, full_up = ring.assemble(with_arrays(two, traded), [width, ff])
    residual = tokens_f + dot_float(mixed, full_out) + bo
    normed_two_f, norm_two_pull = jax.vjp(norm_rows, residual, g2, s2)
    normed_two = normed_two_f.astype(bf16)
    active, slope = rise(normed_two, full_up, bu)
    three, active, cot_slots = tie(three, active, cot_slots)

    three = ring.cores(three)
    grad_low = dot_float(packing, cot_slots).astype(bf16)
    grad_y = grad_low.astype(f32)
    if twins > 1:
        share = (lax.axis_index(("sz", "sc")) % twins == 0).astype(f32)
    else:
        share = None

    def mine(array):
        return array if share is None else array * share

    grad_w_down = mine(contract_rows(active, grad_low)).astype(bf16)
    sum_down = ring.between([grad_w_down])
    (full_down,) = ring.assemble(three, [width])
    result = (residual + dot_float(active, full_down) + bd).astype(bf16)
    result = contract_rows(packing, result).astype(bf16)
    grad_bd = jnp.sum(grad_y, axis=0)
    grad_hidden = contract_cols(grad_low, full_down) * slope
    hidden_low = grad_hidden.astype(bf16)
    sum_down, hidden_low, result = tie(sum_down, hidden_low, result)

    result = exchange_back(result)
    sum_down = ring.inward(ring.halves(sum_down))
    grad_bu = jnp.sum(hidden_low.astype(f32), axis=0)
    grad_w_up = mine(contract_rows(normed_two, hidden_low)).astype(bf16)
    grad_residual, grad_g2, grad_s2 = norm_two_pull(contract_cols(hidden_low, full_up))
    grad_residual = grad_residual + grad_y
    residual_low = grad_residual.astype(bf16)
    sum_down, grad_w_up, residual_low = tie(sum_down, grad_w_up, residual_low)

    sum_down = ring.inward_more(sum_down)
    sum_up = ring.between([grad_w_up])
    grad_w_out = mine(contract_rows(mixed, residual_low)).astype(bf16)
    grad_bo = jnp.sum(residual_low.astype(f32), axis=0)
    grad_mixed = contract_cols(residual_low, full_out).astype(bf16)
    sum_out = ring.between([grad_w_out])
    sum_down, sum_up, sum_out, grad_mixed, result = tie(sum_down, sum_up, sum_out, grad_mixed, result)

    sum_up = ring.inward(ring.halves(sum_up))
    sum_down = ring.down(sum_down)
    grads = attend_back(qkv, mixed, logs, grad_mixed)
    sum_down, sum_up, grads = tie(sum_down, sum_up, grads)

    sum_up = ring.inward_more(sum_up)
    sum_out = ring.inward(ring.halves(sum_out))
    grad_joined = jnp.concatenate(grads, axis=1)
    grad_w_qkv = mine(contract_rows(normed, grad_joined)).astype(bf16)
    sum_qkv = ring.between([grad_w_qkv])
    joined_sum = jnp.sum(grad_joined.astype(f32), axis=0)
    grad_bq, grad_bv = joined_sum[:width], joined_sum[2 * width :]
    grad_tokens, grad_g1, grad_s1 = norm_one_pull(contract_cols(grad_joined, full_qkv))
    grad_tokens = (grad_tokens + grad_residual).astype(bf16)
    grad_tokens = contract_rows(packing, grad_tokens).astype(bf16)
    small = [grad_bq, grad_bv, grad_bo, grad_bd, grad_g1, grad_s1, grad_g2, grad_s2]
    grad_bu = jnp.swapaxes(grad_bu.reshape(ring.count, wide, rows), 1, 2).reshape(width, wide)
    small = jnp.concatenate([jnp.stack(small, axis=1), grad_bu], axis=1)
    small = mine(jnp.pad(small, ((0, 0), (0, SMALL - small.shape[1])))).astype(bf16)
    sum_small = ring.between([small])
    sum_qkv, sum_small, sum_up, sum_out, grad_tokens = tie(sum_qkv, sum_small, sum_up, sum_out, grad_tokens)

    sum_qkv = ring.inward(ring.halves(sum_qkv + sum_small))
    sum_up = ring.down(sum_up)
    sum_out = ring.inward_more(sum_out)
    grad_tokens = exchange_back(grad_tokens).astype(f32)
    sum_qkv, sum_out, sum_up = tie(sum_qkv, sum_out, sum_up)

    sum_out = ring.down(sum_out)
    sums = ring.down(ring.inward_more(sum_qkv))
    sum_qkv = sums[:, : 3 * width]
    vectors = sums[:, 3 * width :]
    sum_bq, sum_bv, sum_bo, sum_bd, sum_g1, sum_s1, sum_g2, sum_s2 = [vectors[:, k] for k in range(8)]
    sum_bu = jnp.swapaxes(vectors[:, 8 : 8 + wide], 0, 1).reshape(wide * rows)
    return (result, grad_tokens, sum_qkv, sum_bq, sum_bv, sum_out, sum_bo, sum_up, sum_bu, sum_down, sum_bd, sum_g1, sum_s1, sum_g2, sum_s2)


def solution(mesh):
    n_grp, n_seq = mesh.shape["grp"], mesh.shape["seq"]
    sizes = (n_grp // 2, 2, n_seq // 2, 2)
    fine = Mesh(mesh.devices.reshape(sizes), AXES)
    ring = Ring(sizes)
    grp, seq = AXES[:2], AXES[2:]
    by_token = P(grp, seq, None)
    rows, vec = P(AXES, None), P(AXES)
    in_specs = (by_token, P(grp, seq), rows, vec, vec, rows, vec, rows, vec, rows, vec, vec, vec, vec, vec, by_token)
    out_specs = (by_token, by_token, rows, vec, vec, rows, vec, rows, vec, rows, vec, vec, vec, vec, vec)

    def shards(*args):
        return layer(ring, *args)

    return jax.shard_map(shards, mesh=fine, in_specs=in_specs, out_specs=out_specs, check_vma=False)
```

```python
import jax
import jax.numpy as jnp
import numpy as np
from jax import lax
from jax.experimental import pallas as pl
from jax.experimental.pallas import tpu as pltpu
from jax.sharding import Mesh
from jax.sharding import PartitionSpec as P

H = 16
HD = 64
LENGTH = 577
PACKED = 592
EPSILON = 1e-06
NEGATIVE = -1e30
ABSENT = 100.0
SMALL = 256
AXES = ("gy", "gx", "sz", "sc")
ORDERS = (("gx", "gy"), ("gy", "gx"))

bf16 = jnp.bfloat16
f32 = jnp.float32


def norm_rows(values, gain_vec, shift_vec):
    row_mean = jnp.mean(values, axis=-1, keepdims=True)
    centred = values - row_mean
    row_var = jnp.mean(centred * centred, axis=-1, keepdims=True)
    return centred * lax.rsqrt(row_var + EPSILON) * gain_vec + shift_vec


def dot_float(left, right):
    return jnp.dot(left, right, preferred_element_type=f32)


def contract_rows(left, right):
    return lax.dot_general(left, right, (((0,), (0,)), ((), ())), preferred_element_type=f32)


def contract_cols(left, right):
    return lax.dot_general(left, right, (((1,), (1,)), ((), ())), preferred_element_type=f32)


def room(mib=50):
    return pltpu.CompilerParams(vmem_limit_bytes=mib * 2**20)


HINT = 0.02


def cost(flops, bytes_accessed, transcendentals=0):
    return pl.CostEstimate(
        flops=int(HINT * flops), bytes_accessed=int(HINT * bytes_accessed), transcendentals=int(HINT * transcendentals)
    )


def shifted(array, axis, size, step):
    return lax.ppermute(array, axis, [(i, (i + step) % size) for i in range(size)])


def pick(array, index, axis):
    return lax.dynamic_index_in_dim(array, index, axis, keepdims=False)


class Ring:
    def __init__(self, sizes):
        self.sizes = dict(zip(AXES, sizes))
        self.count = int(np.prod(sizes))

    def place(self):
        return {axis: lax.axis_index(axis) for axis in AXES}

    def others(self, array, axis):
        size = self.sizes[axis]
        return [shifted(array, axis, size, step) for step in range(1, size)]

    def others_from(self, array, axis, steps):
        size = self.sizes[axis]
        return [shifted(array, axis, size, step) for step in steps]

    def along(self, shard, columns):
        cut = shard.shape[0] // 2
        size = self.sizes["sz"]
        columns = [shard] + [columns[k] for k in range(1, size)]
        here = lax.axis_index("sz")
        ordered = [lax.select_n((here - k) % size, *columns) if size > 2 else jnp.where(here == k, *columns) for k in range(size)]
        return [jnp.stack([c[:cut] for c in ordered]), jnp.stack([c[cut:] for c in ordered])]

    def spread(self, shard, steps):
        return {k: shifted(shard, "sz", self.sizes["sz"], k) for k in steps}

    def across(self, halves):
        return [jnp.stack([half] + self.others(half, order[0])) for half, order in zip(halves, ORDERS)]

    def plane(self, halves):
        return [self.others(half, order[1]) for half, order in zip(halves, ORDERS)]

    def to_core(self, groups):
        return [[shifted(group, "sc", 2, 1) for group in part] for part in groups]

    def sources(self, first, traded_first, second, traded_second):
        found = []
        for part in range(2):
            kinds = ([first[part]] + second[part], traded_first[part] + traded_second[part])
            for turn, groups in enumerate(kinds):
                found += [(group, part, turn, step) for step, group in enumerate(groups)]
        return found

    def assemble(self, sources, widths):
        place = self.place()
        sizes = self.sizes
        cut, width = sources[0][0].shape[-2:]
        depth = sizes["sz"]
        planes, kinds, parts, arrays, counts = [], [], [], [], []
        for group, part, turn, step in sources:
            order = ORDERS[part]
            arrays.append(group)
            counts.append(group.shape[0])
            for one in range(group.shape[0]):
                at = {order[1]: (place[order[1]] - step) % sizes[order[1]], order[0]: (place[order[0]] - one) % sizes[order[0]]}
                planes.append(at["gy"] * sizes["gx"] + at["gx"])
                kinds.append((place["sc"] - turn) % 2)
                parts.append(part)
        table = jnp.stack(planes + kinds).astype(jnp.int32)
        many = len(planes)
        starts = np.concatenate([[0], np.cumsum(widths)])

        def body(table_ref, *refs):
            ins = refs[: len(counts)]
            outs = refs[len(counts) : -3]
            held, came, left = refs[-3:]
            arrivals = []
            for ref, count in zip(ins, counts):
                for k in range(count):
                    n = len(arrivals)
                    arrivals.append(pltpu.make_async_copy(ref.at[k], held.at[n], came.at[n]))
            for copy in arrivals:
                copy.start()
            departures = []
            for n, copy in enumerate(arrivals):
                copy.wait()
                for i, out in enumerate(outs):
                    window = held.at[n, :, :, pl.ds(int(starts[i]), widths[i])]
                    target = out.at[table_ref[n], :, table_ref[many + n], parts[n]]
                    leave = pltpu.make_async_copy(window, target, left.at[n, i])
                    leave.start()
                    departures.append(leave)
            for copy in departures:
                copy.wait()

        planes_all = sizes["gy"] * sizes["gx"]
        outs = pl.pallas_call(
            body,
            out_shape=[jax.ShapeDtypeStruct((planes_all, depth, 2, 2, cut, w), bf16) for w in widths],
            grid_spec=pltpu.PrefetchScalarGridSpec(
                num_scalar_prefetch=1,
                grid=(1,),
                in_specs=[pl.BlockSpec(memory_space=pl.ANY)] * len(counts),
                out_specs=[pl.BlockSpec(memory_space=pl.ANY)] * len(widths),
                scratch_shapes=[
                    pltpu.VMEM((many, depth, cut, width), bf16),
                    pltpu.SemaphoreType.DMA((many,)),
                    pltpu.SemaphoreType.DMA((many, len(widths))),
                ],
            ),
            compiler_params=room(),
            cost_estimate=cost(0, 4 * self.count * 2 * cut * width),
            name="assemble",
        )(table, *arrays)
        return [out.reshape(self.count * 2 * cut, w) for out, w in zip(outs, widths)]

    def far(self, device):
        place = self.place()
        sizes = self.sizes
        index, out = device, {}
        for axis in AXES[::-1]:
            out[axis] = (index % sizes[axis] - place[axis]) % sizes[axis]
            index = index // sizes[axis]
        return ((out["sc"] * sizes["gy"] + out["gy"]) * sizes["gx"] + out["gx"]) * sizes["sz"] + out["sz"]

    def by_distance(self, array):
        tokens, width = array.shape
        block = width // self.count
        half = width // 2
        row = lax.broadcasted_iota(jnp.int32, (width, 1), 0)
        target = self.far(row // block) * block + row % block

        def body(x_ref, t_ref, o_ref):
            columns = lax.broadcasted_iota(jnp.int32, (width, half), 1) + half * pl.program_id(0)
            pick_columns = jnp.where(t_ref[...] == columns, 1.0, 0.0).astype(bf16)
            o_ref[0] = dot_float(x_ref[...], pick_columns).astype(bf16)

        return pl.pallas_call(
            body,
            out_shape=jax.ShapeDtypeStruct((2, tokens, half), bf16),
            grid=(2,),
            in_specs=[pl.BlockSpec((tokens, width), lambda i: (0, 0)), pl.BlockSpec((width, 1), lambda i: (0, 0))],
            out_specs=pl.BlockSpec((1, tokens, half), lambda i: (i, 0, 0)),
            compiler_params=room(),
            cost_estimate=cost(2 * tokens * width * width, 4 * tokens * width),
            name="by_distance",
        )(array, target)

    def blocks_for(self, array, twins):
        place = self.place()
        size = self.sizes["sz"]
        out = []
        for turn in range(2):
            found = [((place["sz"] + k) % size * 2 + (place["sc"] + turn) % 2) // twins for k in range(size)]
            out.append(jnp.stack([pick(array, image, 0) for image in found]))
        return out

    def paired(self, stay, came):
        return [jnp.stack([stay[k], came[k]]) for k in range(self.sizes["sz"])]

    def send(self, pieces, steps, sign=1):
        return {k: shifted(pieces[k], "sz", self.sizes["sz"], sign * k) for k in steps}

    def images_of(self, own, came, images, twins):
        place = self.place()
        size = self.sizes["sz"]
        both = jnp.stack([jnp.stack(own), came])
        both = both.reshape((2 * size,) + both.shape[2:])
        out = []
        for image in range(images):
            device = image * twins
            out.append(pick(both, (device % 2 - place["sc"]) % 2 * size + (device // 2 - place["sz"]) % size, 0))
        return jnp.stack(out)

    def swap(self, sent):
        return shifted(sent, "sc", 2, 1)

    def reshaped(self, out):
        sizes = self.sizes
        return out.reshape(sizes["gy"], sizes["gx"], sizes["sz"], out.shape[0] // (self.count // 2), out.shape[1])

    def kept(self, left, right, share, came):
        cut = left.shape[2] // (self.count // 2) // 2
        if cut % 16 == 0:
            return weight_grad(left, 0, right, share, came, self.sizes)
        return self.ready(self.reshaped(weight_grad(left, 0, right, share, came)))

    def toward(self, arrays, axis):
        size = self.sizes[axis]
        return [arrays[0]] + [shifted(arrays[k], axis, size, k) for k in range(1, size)]

    def ready(self, sums):
        cut = sums.shape[3] // 2
        upper = [sums[k, :, :, :cut] for k in range(self.sizes["gy"])]
        lower = [sums[:, k, :, cut:] for k in range(self.sizes["gx"])]
        return upper, lower

    def first(self, pair):
        return self.toward(pair[0], "gy"), self.toward(pair[1], "gx")

    def again(self, pair):
        return tuple(
            [total([t[k] for t in terms]).astype(bf16) for k in range(self.sizes[axis])]
            for terms, axis in zip(pair, ("gx", "gy"))
        )

    def second(self, pair):
        return self.toward(pair[0], "gx"), self.toward(pair[1], "gy")

    def last(self, pair):
        return [
            jnp.concatenate([total([t[k] for t in terms]) for terms in pair], axis=0).astype(bf16)
            for k in range(self.sizes["sz"])
        ]

    def third(self, parts):
        return self.toward(parts, "sz")


def weight_grad(left, kind, right, share, came=None, sizes=None):
    tokens, columns = right.shape
    rows = left.shape[2]
    tiled = rows > 512
    parts = 1
    if sizes is not None:
        ny, nx, nz = sizes["gy"], sizes["gx"], sizes["sz"]
        parts = ny * nx
        block = rows // (parts * nz)
        cut = block // 2
    if tiled:
        tall, broad = rows // (parts if sizes is not None else rows // 512), columns
        steps = rows // tall
        at = lambda i: (i, 0)
        left_at, right_at = (lambda i: (kind, 0, i)), (lambda i: (0, 0))
    else:
        tall, broad = rows, next(w for w in (1024, 768, 512, 128) if columns % w == 0)
        steps = columns // broad
        at = lambda i: (0, i)
        left_at, right_at = (lambda i: (kind, 0, 0)), (lambda i: (0, i))
    others = [] if came is None else [came.reshape(rows, columns)]
    if share is not None:
        others.append(share.reshape(1, 1))
    given = 2 + len(others)

    def body(*refs):
        outs = refs[given:]
        out = contract_rows(refs[0][0], refs[1][...])
        if share is not None:
            out = out * refs[given - 1][...]
        if came is not None:
            out = out + refs[2][...].astype(f32)
        if sizes is None:
            outs[0][...] = out.astype(bf16)
        elif tiled:
            i = pl.program_id(0)
            out = out.astype(bf16).reshape(nz, block, broad)
            for k in range(ny):

                @pl.when(i // nx == k)
                def _(k=k):
                    outs[k][0] = out[:, :cut]

            for k in range(nx):

                @pl.when(i % nx == k)
                def _(k=k):
                    outs[ny + k][0] = out[:, cut:]

        else:
            out = out.astype(bf16).reshape(ny, nx, nz, block, broad)
            for k in range(ny):
                outs[k][...] = out[k, :, :, :cut]
            for k in range(nx):
                outs[ny + k][...] = out[:, k, :, cut:]

    specs = [pl.BlockSpec((1, tokens, tall), left_at), pl.BlockSpec((tokens, broad), right_at)]
    if came is not None:
        specs.append(pl.BlockSpec((tall, broad), at))
    if share is not None:
        specs.append(pl.BlockSpec((1, 1), lambda i: (0, 0)))
    if sizes is None:
        shapes, out_specs = [(rows, columns)], [pl.BlockSpec((tall, broad), at)]
    else:
        shapes = [(nx, nz, cut, columns)] * ny + [(ny, nz, cut, columns)] * nx
        if tiled:
            out_specs = [
                pl.BlockSpec((1, nz, cut, broad), lambda i, k=k: (jnp.clip(i - k * nx, 0, nx - 1), 0, 0, 0)) for k in range(ny)
            ]
            out_specs += [pl.BlockSpec((1, nz, cut, broad), lambda i, k=k: (jnp.maximum(i - k, 0) // nx, 0, 0, 0)) for k in range(nx)]
        else:
            out_specs = [pl.BlockSpec(shape[:3] + (broad,), lambda i: (0, 0, 0, i)) for shape in shapes]
    outs = pl.pallas_call(
        body,
        out_shape=[jax.ShapeDtypeStruct(shape, bf16) for shape in shapes],
        grid=(steps,),
        in_specs=specs,
        out_specs=out_specs,
        compiler_params=room(),
        cost_estimate=cost(2 * tokens * rows * columns, 4 * rows * columns),
        name="weight_grad",
    )(left, right, *others)
    return outs[0] if sizes is None else (outs[:ny], outs[ny:])


def total(arrays):
    out = arrays[0].astype(f32)
    for array in arrays[1:]:
        out = out + array.astype(f32)
    return out


def tie(*values):
    return lax.optimization_barrier(values)


def of_head(part):
    return lax.broadcasted_iota(jnp.int32, (1, 2 * HD), 1) // HD == part


def mask_tail(scores, fill):
    start = LENGTH // 8 * 8
    row = lax.broadcasted_iota(jnp.int32, (PACKED - start, PACKED), 0)
    tail = jnp.where(row < LENGTH - start, scores[start:], fill)
    return jnp.concatenate([scores[:start], tail], axis=0)


def flip(array):
    return array.astype(f32).T.astype(bf16)


def attend_body(q_ref, k_ref, v_ref, o_ref, l_ref):
    query, key = q_ref[...] * jnp.asarray(HD**-0.5, bf16), k_ref[...]
    value_t = flip(v_ref[...])
    mixed, logs = [], []
    for part in range(2):
        scores = contract_cols(jnp.where(of_head(part), key, 0), query)
        scores = mask_tail(scores, NEGATIVE)
        top = jnp.max(scores, axis=0, keepdims=True)
        exponent = jnp.exp(scores - top)
        total = jnp.sum(exponent, axis=0, keepdims=True)
        out = dot_float(value_t[HD * part : HD * (part + 1)], exponent.astype(bf16))
        mixed.append(out * (1.0 / total))
        logs.append(top + jnp.log(total))
    o_ref[...] = jnp.concatenate(mixed, axis=0).T.astype(bf16)
    l_ref[...] = jnp.concatenate(logs + [jnp.zeros((6, PACKED), f32)], axis=0)


PAIR = (PACKED, 2 * HD)
PAIRS = H // 2
CUT = PAIRS // 2


def kind_spec(kind, base=0):
    return pl.BlockSpec(PAIR, lambda i: (0, (i + base) // CUT * 3 * CUT + (i + base) % CUT + kind * CUT))


def pair_spec(base=0):
    return pl.BlockSpec(PAIR, lambda i: (0, i + base))


def log_spec(base=0):
    return pl.BlockSpec((8, PACKED), lambda i: (i + base, 0))


def halved(array):
    return array.reshape(-1, 3, 2, H * HD // 2).swapaxes(1, 2).reshape(array.shape)


def whole(array):
    return array.reshape(-1, 2, 3, H * HD // 2).swapaxes(1, 2).reshape(array.shape)


def attend(qkv):
    return pl.pallas_call(
        attend_body,
        out_shape=[
            jax.ShapeDtypeStruct((PACKED, H * HD), bf16),
            jax.ShapeDtypeStruct((8 * PAIRS, PACKED), f32),
        ],
        grid=(PAIRS,),
        in_specs=[kind_spec(0), kind_spec(1), kind_spec(2)],
        out_specs=[pair_spec(), log_spec()],
        compiler_params=room(),
        cost_estimate=cost(12e9, 8 * qkv.size, PACKED * PACKED * H),
        name="attend",
    )(qkv, qkv, qkv)


def attend_back_body(q_ref, k_ref, v_ref, l_ref, g_ref, d_ref, s_ref):
    scale = jnp.asarray(HD**-0.5, bf16)
    query, key, value, grad = q_ref[...] * scale, k_ref[...], v_ref[...], g_ref[...]
    key_t = flip(key)
    grad_query, grad_key, grad_value = [], [], []
    for part in range(2):
        mask = of_head(part)
        scores = contract_cols(jnp.where(mask, key, 0), query)
        soft = mask_tail(jnp.exp(scores - l_ref[part : part + 1]), 0.0)
        grad_soft = contract_cols(jnp.where(mask, value, 0), grad)
        delta = jnp.sum(soft * grad_soft, axis=0, keepdims=True)
        grad_scores = (soft * (grad_soft - delta)).astype(bf16)
        grad_value.append(dot_float(soft.astype(bf16), grad))
        grad_key.append(dot_float(grad_scores, query))
        grad_query.append(dot_float(key_t[HD * part : HD * (part + 1)], grad_scores))
    first = of_head(0)
    grads = (
        jnp.concatenate(grad_query, axis=0).T * HD**-0.5,
        jnp.where(first, grad_key[0], grad_key[1]),
        jnp.where(first, grad_value[0], grad_value[1]),
    )
    for kind, array in enumerate(grads):
        start = pl.multiple_of((pl.program_id(0) + kind * CUT) * 2 * HD, 2 * HD)
        low = array.astype(bf16)
        d_ref[:, pl.ds(start, 2 * HD)] = low
        s_ref[:, pl.ds(start, 2 * HD)] = jnp.sum(low.astype(f32), axis=0, keepdims=True)


def attend_back(qkv, logs, grad_mixed, half):
    base = half * CUT
    shape = (PACKED, 3 * CUT * 2 * HD)
    return pl.pallas_call(
        attend_back_body,
        out_shape=[jax.ShapeDtypeStruct(shape, bf16), jax.ShapeDtypeStruct((1, shape[1]), f32)],
        grid=(CUT,),
        in_specs=[kind_spec(0, base), kind_spec(1, base), kind_spec(2, base), log_spec(base), pair_spec(base)],
        out_specs=[pl.BlockSpec(shape, lambda i: (0, 0)), pl.BlockSpec((1, shape[1]), lambda i: (0, 0))],
        compiler_params=room(),
        cost_estimate=cost(12e9, 8 * qkv.size, PACKED * PACKED * H // 2),
        name="attend_back",
    )(qkv, qkv, qkv, logs, grad_mixed)


def rise(normed, weights, bias, ranks):
    width, ff = weights.shape
    step = ff // 4
    count = ranks.shape[0]
    block = ff // count
    inside = step // block
    whole_tiles = block % 128 == 0

    def body(rank_ref, x_ref, w_ref, b_ref, active_ref, slope_ref, *rest):
        i = pl.program_id(0)
        hidden = dot_float(x_ref[...], w_ref[...]) + b_ref[...]
        share = 0.5 * (1.0 + lax.erf(hidden * np.float32(np.sqrt(0.5))))
        active = (hidden * share).astype(bf16)
        active_ref[...] = active
        bell = jnp.exp(hidden * hidden * -0.5) * np.float32(1.0 / np.sqrt(2.0 * np.pi))
        slope_ref[...] = share + hidden * bell
        if not whole_tiles:
            return
        far_ref, held, sems = rest
        held[i % 2] = active

        def copies(turn):
            out = []
            for k in range(inside):
                rank = rank_ref[turn * inside + k]
                start = pl.multiple_of(rank % (count // 2) * block, block)
                window = held.at[turn % 2, :, pl.ds(k * block, block)]
                out.append(pltpu.make_async_copy(window, far_ref.at[rank // (count // 2), :, pl.ds(start, block)], sems.at[turn % 2, k]))
            return out

        for copy in copies(i):
            copy.start()

        @pl.when(i > 0)
        def _():
            for copy in copies(i - 1):
                copy.wait()

        @pl.when(i == 3)
        def _():
            for copy in copies(i):
                copy.wait()

    shapes = [jax.ShapeDtypeStruct((PACKED, ff), bf16), jax.ShapeDtypeStruct((PACKED, ff), f32)]
    specs = [pl.BlockSpec((PACKED, step), lambda i, t: (0, i))] * 2
    scratch = []
    if whole_tiles:
        shapes.append(jax.ShapeDtypeStruct((2, PACKED, ff // 2), bf16))
        specs.append(pl.BlockSpec(memory_space=pl.ANY))
        scratch = [pltpu.VMEM((2, PACKED, step), bf16), pltpu.SemaphoreType.DMA((2, inside))]
    outs = pl.pallas_call(
        body,
        out_shape=shapes,
        grid_spec=pltpu.PrefetchScalarGridSpec(
            num_scalar_prefetch=1,
            grid=(4,),
            in_specs=[
                pl.BlockSpec((PACKED, width), lambda i, t: (0, 0)),
                pl.BlockSpec((width, step), lambda i, t: (0, i)),
                pl.BlockSpec((1, step), lambda i, t: (0, i)),
            ],
            out_specs=specs,
            scratch_shapes=scratch,
        ),
        compiler_params=room(),
        cost_estimate=cost(12e9, 30e6, PACKED * ff * 2),
        name="rise",
    )(ranks, normed, weights, bias.reshape(1, ff))
    return outs if whole_tiles else (outs[0], outs[1], None)


def fall_body(g_ref, w_ref, slope_ref, out_ref, sum_ref):
    grad = (contract_cols(g_ref[...], w_ref[...]) * slope_ref[...]).astype(bf16)
    out_ref[...] = grad
    sum_ref[...] = jnp.sum(grad.astype(f32), axis=0, keepdims=True)


def fall(grads, weights, slope):
    ff, width = weights.shape
    step = ff // 4
    return pl.pallas_call(
        fall_body,
        out_shape=[jax.ShapeDtypeStruct((PACKED, ff), bf16), jax.ShapeDtypeStruct((1, ff), f32)],
        grid=(4,),
        in_specs=[
            pl.BlockSpec((PACKED, width), lambda i: (0, 0)),
            pl.BlockSpec((step, width), lambda i: (i, 0)),
            pl.BlockSpec((PACKED, step), lambda i: (0, i)),
        ],
        out_specs=[pl.BlockSpec((PACKED, step), lambda i: (0, i)), pl.BlockSpec((1, step), lambda i: (0, i))],
        compiler_params=room(),
        cost_estimate=cost(10e9, 25e6),
        name="fall",
    )(grads, weights, slope)


def project_body(x_ref, w_ref, b_ref, out_ref):
    out_ref[...] = (dot_float(x_ref[...], w_ref[...]) + b_ref[...]).astype(bf16)


def project(left, weights, bias):
    width, columns = weights.shape
    step = columns // 3
    return pl.pallas_call(
        project_body,
        out_shape=jax.ShapeDtypeStruct((PACKED, columns), bf16),
        grid=(3,),
        in_specs=[
            pl.BlockSpec((PACKED, width), lambda i: (0, 0)),
            pl.BlockSpec((width, step), lambda i: (0, i)),
            pl.BlockSpec((1, step), lambda i: (0, i)),
        ],
        out_specs=pl.BlockSpec((PACKED, step), lambda i: (0, i)),
        compiler_params=room(),
        cost_estimate=cost(6e9, 12e6),
        name="project",
    )(left, weights, bias.reshape(1, columns))


def row(vector):
    return vector.reshape(1, -1)


def fixed(shape):
    return pl.BlockSpec(shape, lambda i: (0,) * len(shape))


def seed(weights, vectors, long):
    rows, width = weights.shape
    half = width // 6

    def body(w_ref, *refs):
        out_ref = refs[-1]
        for k in range(6):
            out_ref[:, k * half : (k + 1) * half] = w_ref[:, pl.ds((k % 3 * 2 + k // 3) * half, half)]
        out_ref[:, width:] = jnp.zeros((rows, SMALL), bf16)
        for k in range(len(vectors)):
            out_ref[k : k + 1, width : width + rows] = refs[k][...]
        out_ref[0:1, width + 128 : width + 128 + long.shape[0]] = refs[len(vectors)][...]

    return pl.pallas_call(
        body,
        out_shape=jax.ShapeDtypeStruct((rows, width + SMALL), bf16),
        cost_estimate=cost(0, 1e6),
        name="seed",
    )(weights, *[row(v) for v in vectors], row(long))


def pack_norm_body(p_ref, x_ref, g_ref, s_ref, t_ref, n_ref):
    tokens = dot_float(p_ref[...], x_ref[...])
    t_ref[...] = tokens
    n_ref[...] = norm_rows(tokens, g_ref[...], s_ref[...]).astype(bf16)


def pack_norm(packing, slots, gain, shift):
    count, width = slots.shape
    half = PACKED // 2
    by_row = pl.BlockSpec((half, width), lambda i: (i, 0))
    return pl.pallas_call(
        pack_norm_body,
        out_shape=[jax.ShapeDtypeStruct((PACKED, width), f32), jax.ShapeDtypeStruct((PACKED, width), bf16)],
        grid=(2,),
        in_specs=[pl.BlockSpec((half, count), lambda i: (i, 0)), fixed((count, width)), fixed((1, width)), fixed((1, width))],
        out_specs=[by_row, by_row],
        compiler_params=room(),
        cost_estimate=cost(1e9, 8e6),
        name="pack_norm",
    )(packing, slots, row(gain), row(shift))


def pack_body(p_ref, x_ref, o_ref, s_ref):
    low = dot_float(p_ref[...], x_ref[...]).astype(bf16)
    o_ref[...] = low
    s_ref[...] = jnp.sum(low.astype(f32), axis=0, keepdims=True)


def pack(packing, slots):
    count, width = slots.shape
    half = width // 2
    return pl.pallas_call(
        pack_body,
        out_shape=[jax.ShapeDtypeStruct((PACKED, width), bf16), jax.ShapeDtypeStruct((1, width), f32)],
        grid=(2,),
        in_specs=[fixed((PACKED, count)), pl.BlockSpec((count, half), lambda i: (0, i))],
        out_specs=[pl.BlockSpec((PACKED, half), lambda i: (0, i)), pl.BlockSpec((1, half), lambda i: (0, i))],
        compiler_params=room(),
        cost_estimate=cost(1e9, 4e6),
        name="pack",
    )(packing, slots)


def out_norm_body(m_ref, w_ref, t_ref, b_ref, g_ref, s_ref, r_ref, n_ref):
    residual = t_ref[...] + dot_float(m_ref[...], w_ref[...]) + b_ref[...]
    r_ref[...] = residual
    n_ref[...] = norm_rows(residual, g_ref[...], s_ref[...]).astype(bf16)


def out_norm(mixed, weights, tokens, bias, gain, shift):
    width = weights.shape[1]
    half = PACKED // 2
    by_row = pl.BlockSpec((half, width), lambda i: (i, 0))
    vec = fixed((1, width))
    return pl.pallas_call(
        out_norm_body,
        out_shape=[jax.ShapeDtypeStruct((PACKED, width), f32), jax.ShapeDtypeStruct((PACKED, width), bf16)],
        grid=(2,),
        in_specs=[by_row, fixed(weights.shape), by_row, vec, vec, vec],
        out_specs=[by_row, by_row],
        compiler_params=room(),
        cost_estimate=cost(2e9, 8e6),
        name="out_norm",
    )(mixed, weights, tokens, row(bias), row(gain), row(shift))


def land_body(a_ref, w_ref, r_ref, b_ref, p_ref, o_ref, sum_ref):
    i = pl.program_id(0)
    part = dot_float(a_ref[...], w_ref[...])

    @pl.when(i == 0)
    def _():
        sum_ref[...] = part + r_ref[...] + b_ref[...]

    @pl.when(i > 0)
    def _():
        sum_ref[...] += part

    @pl.when(i == pl.num_programs(0) - 1)
    def _():
        o_ref[...] = contract_rows(p_ref[...], sum_ref[...].astype(bf16)).astype(bf16)


def land(active, weights, residual, bias, packing):
    ff, width = weights.shape
    step = ff // 4
    count = packing.shape[1]
    return pl.pallas_call(
        land_body,
        out_shape=jax.ShapeDtypeStruct((count, width), bf16),
        grid=(4,),
        in_specs=[
            pl.BlockSpec((PACKED, step), lambda i: (0, i)),
            pl.BlockSpec((step, width), lambda i: (i, 0)),
            fixed((PACKED, width)),
            fixed((1, width)),
            fixed((PACKED, count)),
        ],
        out_specs=fixed((count, width)),
        scratch_shapes=[pltpu.VMEM((PACKED, width), f32)],
        compiler_params=room(),
        cost_estimate=cost(6e9, 14e6),
        name="land",
    )(active, weights, residual, row(bias), packing)


def back_norm(grads, weights, values, gain, added, packing=None):
    width = weights.shape[0]
    step = weights.shape[1] // (4 if len(grads) == 1 else len(grads))
    steps = weights.shape[1] // step
    count = len(grads)

    def body(*refs):
        g_refs, (w_ref, x_ref, gain_ref, add_ref), rest = refs[:count], refs[count : count + 4], refs[count + 4 :]
        sum_ref = rest[-1]
        i = pl.program_id(0)
        for k, g_ref in enumerate(g_refs):

            @pl.when((i == k) if count > 1 else (i >= 0))
            def _(g_ref=g_ref, k=k):
                part = contract_cols(g_ref[...], w_ref[...])

                @pl.when(i == 0)
                def _():
                    sum_ref[...] = part

                @pl.when(i > 0)
                def _():
                    sum_ref[...] += part

        @pl.when(i == steps - 1)
        def _():
            back = sum_ref[...]
            values = x_ref[...]
            centred = values - jnp.mean(values, axis=-1, keepdims=True)
            scale = lax.rsqrt(jnp.mean(centred * centred, axis=-1, keepdims=True) + EPSILON)
            normed = centred * scale
            scaled = back * gain_ref[...]
            inner = jnp.mean(scaled * normed, axis=-1, keepdims=True)
            out = (scaled - jnp.mean(scaled, axis=-1, keepdims=True) - normed * inner) * scale + add_ref[...].astype(f32)
            low = out.astype(bf16)
            if packing is None:
                out_ref, low_ref, sums_ref = rest[:3]
                out_ref[...] = out
                low_ref[...] = low
            else:
                p_ref, low_ref, sums_ref = rest[:3]
                low_ref[...] = contract_rows(p_ref[...], low).astype(bf16)
            sums = [jnp.sum(a, axis=0, keepdims=True) for a in (back * normed, back, low.astype(f32))]
            sums_ref[...] = jnp.concatenate(sums + [jnp.zeros((5, width), f32)], axis=0)

    full = fixed((PACKED, width))
    if packing is None:
        shapes = [jax.ShapeDtypeStruct((PACKED, width), f32), jax.ShapeDtypeStruct((PACKED, width), bf16)]
        out_specs, more_specs, more = [full, full], [], []
    else:
        shapes = [jax.ShapeDtypeStruct((packing.shape[1], width), bf16)]
        out_specs, more_specs, more = [fixed(shapes[0].shape)], [fixed(packing.shape)], [packing]
    g_spec = fixed((PACKED, step)) if count > 1 else pl.BlockSpec((PACKED, step), lambda i: (0, i))
    return pl.pallas_call(
        body,
        out_shape=shapes + [jax.ShapeDtypeStruct((8, width), f32)],
        grid=(steps,),
        in_specs=[g_spec] * count + [pl.BlockSpec((width, step), lambda i: (0, i)), full, fixed((1, width)), full] + more_specs,
        out_specs=out_specs + [fixed((8, width))],
        scratch_shapes=[pltpu.VMEM((PACKED, width), f32)],
        compiler_params=room(),
        cost_estimate=cost(6e9, 20e6),
        name="back_norm",
    )(*grads, weights, values, row(gain), added, *more)


def back_project_body(g_ref, w_ref, o_ref):
    o_ref[...] = contract_cols(g_ref[...], w_ref[...]).astype(bf16)


def back_project(grads, weights):
    rows, width = weights.shape
    half = rows // 2
    return pl.pallas_call(
        back_project_body,
        out_shape=jax.ShapeDtypeStruct((PACKED, rows), bf16),
        grid=(2,),
        in_specs=[fixed((PACKED, width)), pl.BlockSpec((half, width), lambda i: (i, 0))],
        out_specs=pl.BlockSpec((PACKED, half), lambda i: (0, i)),
        compiler_params=room(),
        cost_estimate=cost(2e9, 5e6),
        name="back_project",
    )(grads, weights)


def layer(ring, tokens, counts, w_qkv, bias_q, bias_v, w_out, bias_out, w_up, bias_up, w_down, bias_down, gain_one, shift_one, gain_two, shift_two, cotangent):
    images, slots, width = tokens.shape
    group = ring.sizes["sz"] * ring.sizes["sc"]
    twins = group // images
    rows = w_qkv.shape[0]
    wide = w_down.shape[0] // rows
    ff = w_up.shape[1]

    slot = lax.broadcasted_iota(jnp.int32, (images, slots, 1), 1)
    marked = jnp.where(slot < counts[:, :, None], tokens, jnp.asarray(ABSENT, bf16))

    def back_on_device(pieces, own):
        pieces = [own] + [pieces[k] for k in range(1, depth)]
        came = ring.swap(jnp.stack([piece[1] for piece in pieces]))
        return ring.images_of([piece[0] for piece in pieces], came, images, twins)

    def slots_of(array):
        return array.reshape(depth, 2, slots, width)

    depth = ring.sizes["sz"]
    outer = [k for k in range(1, depth) if k in (1, depth - 1)]
    inner = [k for k in range(1, depth) if k not in outer]
    everything = list(range(1, depth))

    small = [bias_q, bias_v, bias_out, bias_down, gain_one, shift_one, gain_two, shift_two]

    def arrays_of(sources):
        return [source[0] for source in sources]

    def with_arrays(sources, arrays):
        return [(array,) + source[1:] for array, source in zip(arrays, sources)]

    one = seed(w_qkv, small, bias_up)
    column = ring.spread(one, everything)
    one = ring.along(one, column)
    two = jnp.concatenate([w_out, w_up], axis=1)
    one, two = tie(one, two)

    one = ring.across(one)
    column = ring.spread(two, outer)
    stay, go = ring.blocks_for(marked, twins)
    came = ring.swap(go)
    one, two, column, stay, came = tie(one, two, column, stay, came)

    one_more = ring.plane(one)
    one_core = ring.to_core([[half] for half in one])
    column.update(ring.spread(two, inner))
    two = ring.along(two, column)
    pieces = ring.paired(stay, came)
    one, one_more, one_core, two, pieces = tie(one, one_more, one_core, two, pieces)

    one_more_core = ring.to_core(one_more)
    two = ring.across(two)
    rest = ring.send(pieces, outer[:1])
    one, one_more, one_core, one_more_core, two, pieces = tie(one, one_more, one_core, one_more_core, two, pieces)

    two_more = ring.plane(two)
    rest.update(ring.send(pieces, everything[1:]))
    full_qkv, vectors = ring.assemble(ring.sources(one, one_core, one_more, one_more_core), [3 * width, SMALL])
    two, two_more, rest, full_qkv, vectors, three = tie(two, two_more, rest, full_qkv, vectors, w_down)

    column = ring.spread(three, outer)
    two_core = ring.to_core([[half] for half in two])
    image_slots = jnp.concatenate([pieces[0]] + [rest[k] for k in everything]).reshape(group * slots, width)
    vectors = vectors.reshape(ring.count, rows, SMALL).astype(f32)
    bu = vectors[:, 0, 128 : 128 + wide * rows].reshape(ff)
    bq, bv, bo, bd, g1, s1, g2, s2 = [vectors[:, k, :rows].reshape(width) for k in range(8)]
    here = (image_slots[:, :1].astype(f32) < 0.5 * ABSENT).reshape(group, slots)
    held = jnp.sum(here.astype(f32), axis=1)
    before = jnp.sum(jnp.where(np.tril(np.ones((group, group), bool), -1), held[None, :], 0.0), axis=1)
    rank = before[:, None] + lax.broadcasted_iota(jnp.int32, (group, slots), 1).astype(f32)
    rank = jnp.where(here, rank, -1.0).reshape(1, group * slots).astype(jnp.int32)
    packing = (rank == lax.broadcasted_iota(jnp.int32, (PACKED, group * slots), 0)).astype(bf16)
    tokens_f, normed = pack_norm(packing, image_slots, g1, s1)
    qkv_bias = halved(jnp.concatenate([bq, jnp.zeros((width,), f32), bv]))
    qkv = project(normed, full_qkv, qkv_bias)
    two_core, column, three, qkv = tie(two_core, column, three, qkv)

    column.update(ring.spread(three, inner))
    two_more_core = ring.to_core(two_more)
    stay, go = ring.blocks_for(cotangent, twins)
    came = ring.swap(go)
    mixed, logs = attend(qkv)
    three = ring.along(three, column)
    two_more_core, three, mixed, stay, came = tie(two_more_core, three, mixed, stay, came)

    three = ring.across(three)
    cot_pieces = ring.paired(stay, came)
    cot_rest = ring.send(cot_pieces, outer)
    full_out, full_up = ring.assemble(ring.sources(two, two_core, two_more, two_more_core), [width, ff])
    residual, normed_two = out_norm(mixed, full_out, tokens_f, bo, g2, s2)
    three, normed_two, cot_pieces, cot_rest = tie(three, normed_two, cot_pieces, cot_rest)

    three_more = ring.plane(three)
    three_core = ring.to_core([[half] for half in three])
    cot_rest.update(ring.send(cot_pieces, inner))
    ranks = ring.far(lax.broadcasted_iota(jnp.int32, (ring.count,), 0))
    active, slope, active_far = rise(normed_two, full_up, bu, ranks)
    if active_far is None:
        active_far = ring.by_distance(active)
    mixed_far = ring.by_distance(mixed)
    normed_far = ring.by_distance(normed)
    three_more, three_core, active, active_far, cot_rest = tie(three_more, three_core, active, active_far, cot_rest)

    three_more_core = ring.to_core(three_more)
    share = (lax.axis_index(("sz", "sc")) % twins == 0).astype(f32) if twins > 1 else None
    cot_slots = jnp.concatenate([cot_pieces[0]] + [cot_rest[k] for k in everything]).reshape(group * slots, width)
    grad_low, grad_bd = pack(packing, cot_slots)
    sent = weight_grad(active_far, 1, grad_low, share)
    three_more_core, sent, grad_low = tie(three_more_core, sent, grad_low)

    d = ring.swap(sent)
    (full_down,) = ring.assemble(ring.sources(three, three_core, three_more, three_more_core), [width])
    two_far = ring.by_distance(normed_two)
    d, full_down, two_far = tie(d, full_down, two_far)

    d = ring.kept(active_far, grad_low, share, d)
    result = slots_of(land(active, full_down, residual, bd, packing))
    d, result = tie(d, result)

    d = ring.first(d)
    back = ring.send(result, outer, -1)
    hidden_low, grad_bu = fall(grad_low, full_down, slope)
    sent = weight_grad(two_far, 1, hidden_low, share)
    d, sent, back = tie(d, sent, back)

    d = ring.again(d)
    d, sent = tie(d, sent)

    d = ring.second(d)
    u = ring.swap(sent)
    back.update(ring.send(result, inner, -1))
    grad_residual, residual_low, sums_two = back_norm([hidden_low], full_up, residual, g2, grad_low)
    d, u, residual_low, back = tie(d, u, residual_low, back)

    d = ring.last(d)
    u = ring.kept(two_far, hidden_low, share, u)
    sent = weight_grad(mixed_far, 1, residual_low, share)
    d, u, sent, residual_low = tie(d, u, sent, residual_low)

    u = ring.first(u)
    sent_out = sent
    d = ring.third(d)
    grad_mixed = back_project(residual_low, full_out)
    first_half, first_sums = attend_back(qkv, logs, grad_mixed, 0)
    sent = weight_grad(normed_far, 1, first_half, share)
    u, sent_out, sent, d, grad_mixed = tie(u, sent_out, sent, d, grad_mixed)

    u = ring.again(u)
    u, sent, sent_out, grad_mixed, back = tie(u, sent, sent_out, grad_mixed, back)

    u = ring.second(u)
    q = ring.swap(sent)
    o = ring.swap(sent_out)
    second_half, second_sums = attend_back(qkv, logs, grad_mixed, 1)
    u, q, o, second_half, back = tie(u, q, o, second_half, back)

    u = ring.last(u)
    u, q, o, second_half, back = tie(u, q, o, second_half, back)

    u = ring.third(u)
    result = back_on_device(back, result[0])
    q = ring.reshaped(weight_grad(normed_far, 0, first_half, share, q))
    o = ring.reshaped(weight_grad(mixed_far, 0, residual_low, share, o))
    q = ring.ready(jnp.concatenate([q, o], axis=-1))
    sent = weight_grad(normed_far, 1, second_half, share)
    q, sent, result, u = tie(q, sent, result, u)

    q = ring.first(q)
    r = ring.swap(sent)
    grad_tokens, sums_one = back_norm([first_half, second_half], full_qkv, tokens_f, g1, grad_residual, packing)
    grad_tokens = slots_of(grad_tokens)
    q, r, grad_tokens, sums_one = tie(q, r, grad_tokens, sums_one)

    q = ring.again(q)
    q, r, grad_tokens, sums_one = tie(q, r, grad_tokens, sums_one)

    back = ring.send(grad_tokens, everything, -1)
    q = ring.second(q)
    joined_sum = whole(jnp.concatenate([first_sums[0], second_sums[0]]))
    grad_bq, grad_bv = joined_sum[:width], joined_sum[2 * width :]
    small = [grad_bq, grad_bv, sums_two[2], grad_bd, sums_one[0], sums_one[1], sums_two[0], sums_two[1]]
    small = [array.reshape(ring.count, rows) for array in small] + [grad_bu.reshape(ring.count, wide * rows)]
    small = jnp.concatenate(small, axis=1)
    small = (small if share is None else small * share).astype(bf16)
    near_first = (ranks[None, :] == lax.broadcasted_iota(jnp.int32, (ring.count, 1), 0)).astype(bf16)
    small = dot_float(near_first, small).astype(bf16)
    small = jnp.pad(small, ((0, 0), (0, rows * SMALL - small.shape[1]))).reshape(2, ring.count // 2 * rows, SMALL)
    r = ring.reshaped(weight_grad(normed_far, 0, second_half, share, r))
    result = jnp.where(slot < counts[:, :, None], result, jnp.asarray(0, bf16))
    q, r, small, result = tie(q, r, small, result)

    came = ring.swap(small[1])
    q = ring.last(q)
    came, q, r = tie(came, q, r)

    small = ring.reshaped(total([small[0], came]).astype(bf16))
    r = ring.first(ring.ready(jnp.concatenate([r, small], axis=-1)))
    (r,) = tie(r)
    r = ring.second(ring.again(r))
    r, q, back = tie(r, q, back)

    r = ring.last(r)
    q = ring.third([jnp.concatenate(pair, axis=-1) for pair in zip(q, r)])
    grad_tokens = back_on_device(back, grad_tokens[0]).astype(f32)

    sum_down, sum_up = total(d), total(u)
    q = total(q)
    first_end, second_start, small_start = 3 * width // 2, 5 * width // 2, 4 * width
    sum_out = q[:, first_end:second_start]
    sum_qkv = whole(jnp.concatenate([q[:, :first_end], q[:, second_start:small_start]], axis=1))
    small = q[:, small_start:].reshape(rows * SMALL)
    sum_bq, sum_bv, sum_bo, sum_bd, sum_g1, sum_s1, sum_g2, sum_s2 = [small[k * rows : (k + 1) * rows] for k in range(8)]
    sum_bu = small[8 * rows : (8 + wide) * rows]
    return (result, grad_tokens, sum_qkv, sum_bq, sum_bv, sum_out, sum_bo, sum_up, sum_bu, sum_down, sum_bd, sum_g1, sum_s1, sum_g2, sum_s2)


def solution(mesh):
    n_grp, n_seq = mesh.shape["grp"], mesh.shape["seq"]
    sizes = (n_grp // 2, 2, n_seq // 2, 2)
    fine = Mesh(mesh.devices.reshape(sizes), AXES)
    ring = Ring(sizes)
    grp, seq = AXES[:2], AXES[2:]
    by_token = P(grp, seq, None)
    rows, vec = P(AXES, None), P(AXES)
    in_specs = (by_token, P(grp, seq), rows, vec, vec, rows, vec, rows, vec, rows, vec, vec, vec, vec, vec, by_token)
    out_specs = (by_token, by_token, rows, vec, vec, rows, vec, rows, vec, rows, vec, vec, vec, vec, vec)

    def shards(*args):
        return layer(ring, *args)

    return jax.shard_map(shards, mesh=fine, in_specs=in_specs, out_specs=out_specs, check_vma=False)
```

```python
import jax
import jax.numpy as jnp
import numpy as np
from jax import lax
from jax.experimental import pallas as pl
from jax.experimental.pallas import tpu as pltpu
from jax.sharding import Mesh
from jax.sharding import PartitionSpec as P

H = 16
HD = 64
LENGTH = 577
PACKED = 592
EPSILON = 1e-06
NEGATIVE = -1e30
ABSENT = 100.0
SMALL = 256
AXES = ("gy", "gx", "sz", "sc")
ORDERS = (("gx", "gy"), ("gy", "gx"))

bf16 = jnp.bfloat16
f32 = jnp.float32


def norm_rows(values, gain_vec, shift_vec):
    row_mean = jnp.mean(values, axis=-1, keepdims=True)
    centred = values - row_mean
    row_var = jnp.mean(centred * centred, axis=-1, keepdims=True)
    return centred * lax.rsqrt(row_var + EPSILON) * gain_vec + shift_vec


def dot_float(left, right):
    return jnp.dot(left, right, preferred_element_type=f32)


def contract_rows(left, right):
    return lax.dot_general(left, right, (((0,), (0,)), ((), ())), preferred_element_type=f32)


def contract_cols(left, right):
    return lax.dot_general(left, right, (((1,), (1,)), ((), ())), preferred_element_type=f32)


def room(mib=50):
    return pltpu.CompilerParams(vmem_limit_bytes=mib * 2**20)


HINT = 0.02


def cost(flops, bytes_accessed, transcendentals=0):
    return pl.CostEstimate(
        flops=int(HINT * flops), bytes_accessed=int(HINT * bytes_accessed), transcendentals=int(HINT * transcendentals)
    )


def shifted(array, axis, size, step):
    return lax.ppermute(array, axis, [(i, (i + step) % size) for i in range(size)])


def pick(array, index, axis):
    return lax.dynamic_index_in_dim(array, index, axis, keepdims=False)


class Ring:
    def __init__(self, sizes):
        self.sizes = dict(zip(AXES, sizes))
        self.count = int(np.prod(sizes))

    def place(self):
        return {axis: lax.axis_index(axis) for axis in AXES}

    def others(self, array, axis):
        size = self.sizes[axis]
        return [shifted(array, axis, size, step) for step in range(1, size)]

    def others_from(self, array, axis, steps):
        size = self.sizes[axis]
        return [shifted(array, axis, size, step) for step in steps]

    def along(self, shard, columns):
        cut = shard.shape[0] // 2
        size = self.sizes["sz"]
        columns = [shard] + [columns[k] for k in range(1, size)]
        here = lax.axis_index("sz")
        ordered = [lax.select_n((here - k) % size, *columns) if size > 2 else jnp.where(here == k, *columns) for k in range(size)]
        return [jnp.stack([c[:cut] for c in ordered]), jnp.stack([c[cut:] for c in ordered])]

    def spread(self, shard, steps):
        return {k: shifted(shard, "sz", self.sizes["sz"], k) for k in steps}

    def across(self, halves):
        return [jnp.stack([half] + self.others(half, order[0])) for half, order in zip(halves, ORDERS)]

    def plane(self, halves):
        return [self.others(half, order[1]) for half, order in zip(halves, ORDERS)]

    def to_core(self, groups):
        return [[shifted(group, "sc", 2, 1) for group in part] for part in groups]

    def sources(self, first, traded_first, second, traded_second):
        found = []
        for part in range(2):
            kinds = ([first[part]] + second[part], traded_first[part] + traded_second[part])
            for turn, groups in enumerate(kinds):
                found += [(g, turn, [(part, step, one) for one in range(g.shape[0])]) for step, g in enumerate(groups)]
        return found

    def flat(self, groups):
        return jnp.concatenate([group for part in groups for group in part], axis=0)

    def labels(self, far):
        sizes = self.sizes
        found = []
        for part in range(2):
            for step in range(1, sizes[ORDERS[part][1]]) if far else [0]:
                found += [(part, step, one) for one in range(sizes[ORDERS[part][0]])]
        return found

    def flat_sources(self, near, near_core, far, far_core):
        return [(near, 0, self.labels(False)), (far, 0, self.labels(True)), (near_core, 1, self.labels(False)), (far_core, 1, self.labels(True))]

    def assemble(self, sources, widths):
        place = self.place()
        sizes = self.sizes
        cut, width = sources[0][0].shape[-2:]
        depth = sizes["sz"]
        planes, kinds, parts, arrays, counts = [], [], [], [], []
        for group, turn, labels in sources:
            arrays.append(group)
            counts.append(len(labels))
            for part, step, one in labels:
                order = ORDERS[part]
                at = {order[1]: (place[order[1]] - step) % sizes[order[1]], order[0]: (place[order[0]] - one) % sizes[order[0]]}
                planes.append(at["gy"] * sizes["gx"] + at["gx"])
                kinds.append((place["sc"] - turn) % 2)
                parts.append(part)
        table = jnp.stack(planes + kinds).astype(jnp.int32)
        many = len(planes)
        starts = np.concatenate([[0], np.cumsum(widths)])

        def body(table_ref, *refs):
            ins = refs[: len(counts)]
            outs = refs[len(counts) : -3]
            held, came, left = refs[-3:]
            arrivals = []
            for ref, count in zip(ins, counts):
                for k in range(count):
                    n = len(arrivals)
                    arrivals.append(pltpu.make_async_copy(ref.at[k], held.at[n], came.at[n]))
            for copy in arrivals:
                copy.start()
            departures = []
            for n, copy in enumerate(arrivals):
                copy.wait()
                for i, out in enumerate(outs):
                    window = held.at[n, :, :, pl.ds(int(starts[i]), widths[i])]
                    target = out.at[table_ref[n], :, table_ref[many + n], parts[n]]
                    leave = pltpu.make_async_copy(window, target, left.at[n, i])
                    leave.start()
                    departures.append(leave)
            for copy in departures:
                copy.wait()

        planes_all = sizes["gy"] * sizes["gx"]
        outs = pl.pallas_call(
            body,
            out_shape=[jax.ShapeDtypeStruct((planes_all, depth, 2, 2, cut, w), bf16) for w in widths],
            grid_spec=pltpu.PrefetchScalarGridSpec(
                num_scalar_prefetch=1,
                grid=(1,),
                in_specs=[pl.BlockSpec(memory_space=pl.ANY)] * len(counts),
                out_specs=[pl.BlockSpec(memory_space=pl.ANY)] * len(widths),
                scratch_shapes=[
                    pltpu.VMEM((many, depth, cut, width), bf16),
                    pltpu.SemaphoreType.DMA((many,)),
                    pltpu.SemaphoreType.DMA((many, len(widths))),
                ],
            ),
            compiler_params=room(),
            cost_estimate=cost(0, 4 * self.count * 2 * cut * width),
            name="assemble",
        )(table, *arrays)
        return [out.reshape(self.count * 2 * cut, w) for out, w in zip(outs, widths)]

    def far(self, device):
        place = self.place()
        sizes = self.sizes
        index, out = device, {}
        for axis in AXES[::-1]:
            out[axis] = (index % sizes[axis] - place[axis]) % sizes[axis]
            index = index // sizes[axis]
        return ((out["sc"] * sizes["gy"] + out["gy"]) * sizes["gx"] + out["gx"]) * sizes["sz"] + out["sz"]

    def by_distance(self, array):
        tokens, width = array.shape
        block = width // self.count
        half = width // 2
        row = lax.broadcasted_iota(jnp.int32, (width, 1), 0)
        target = self.far(row // block) * block + row % block

        def body(x_ref, t_ref, o_ref):
            columns = lax.broadcasted_iota(jnp.int32, (width, half), 1) + half * pl.program_id(0)
            pick_columns = jnp.where(t_ref[...] == columns, 1.0, 0.0).astype(bf16)
            o_ref[0] = dot_float(x_ref[...], pick_columns).astype(bf16)

        return pl.pallas_call(
            body,
            out_shape=jax.ShapeDtypeStruct((2, tokens, half), bf16),
            grid=(2,),
            in_specs=[pl.BlockSpec((tokens, width), lambda i: (0, 0)), pl.BlockSpec((width, 1), lambda i: (0, 0))],
            out_specs=pl.BlockSpec((1, tokens, half), lambda i: (i, 0, 0)),
            compiler_params=room(),
            cost_estimate=cost(2 * tokens * width * width, 4 * tokens * width),
            name="by_distance",
        )(array, target)

    def blocks_for(self, array, twins):
        place = self.place()
        size = self.sizes["sz"]
        out = []
        for turn in range(2):
            found = [((place["sz"] + k) % size * 2 + (place["sc"] + turn) % 2) // twins for k in range(size)]
            out.append(jnp.stack([pick(array, image, 0) for image in found]))
        return out

    def paired(self, stay, came):
        return [jnp.stack([stay[k], came[k]]) for k in range(self.sizes["sz"])]

    def send(self, pieces, steps, sign=1):
        return {k: shifted(pieces[k], "sz", self.sizes["sz"], sign * k) for k in steps}

    def images_of(self, own, came, images, twins):
        place = self.place()
        size = self.sizes["sz"]
        both = jnp.stack([own, came])
        both = both.reshape((2 * size,) + both.shape[2:])
        out = []
        for image in range(images):
            device = image * twins
            out.append(pick(both, (device % 2 - place["sc"]) % 2 * size + (device // 2 - place["sz"]) % size, 0))
        return jnp.stack(out)

    def swap(self, sent):
        return shifted(sent, "sc", 2, 1)

    def reshaped(self, out):
        sizes = self.sizes
        return out.reshape(sizes["gy"], sizes["gx"], sizes["sz"], out.shape[0] // (self.count // 2), out.shape[1])

    def kept(self, left, right, share, came):
        cut = left.shape[2] // (self.count // 2) // 2
        if cut % 16 == 0:
            return weight_grad(left, 0, right, share, came, self.sizes)
        return self.ready(self.reshaped(weight_grad(left, 0, right, share, came)))

    def toward(self, arrays, axis):
        size = self.sizes[axis]
        return [arrays[0]] + [shifted(arrays[k], axis, size, k) for k in range(1, size)]

    def toward_some(self, parts, steps):
        return {k: shifted(parts[k], "sz", self.sizes["sz"], k) for k in steps}

    def ready(self, sums):
        cut = sums.shape[3] // 2
        upper = [sums[k, :, :, :cut] for k in range(self.sizes["gy"])]
        lower = [sums[:, k, :, cut:] for k in range(self.sizes["gx"])]
        return upper, lower

    def first(self, pair):
        return self.toward(pair[0], "gy"), self.toward(pair[1], "gx")

    def again(self, pair):
        return tuple(
            [total([t[k] for t in terms]).astype(bf16) for k in range(self.sizes[axis])]
            for terms, axis in zip(pair, ("gx", "gy"))
        )

    def second(self, pair):
        return self.toward(pair[0], "gx"), self.toward(pair[1], "gy")

    def last(self, pair):
        return [
            jnp.concatenate([total([t[k] for t in terms]) for terms in pair], axis=0).astype(bf16)
            for k in range(self.sizes["sz"])
        ]

    def third(self, parts):
        return self.toward(parts, "sz")


def weight_grad(left, kind, right, share, came=None, sizes=None):
    tokens, columns = right.shape
    rows = left.shape[2]
    tiled = rows > 512
    parts = 1
    if sizes is not None:
        ny, nx, nz = sizes["gy"], sizes["gx"], sizes["sz"]
        parts = ny * nx
        block = rows // (parts * nz)
        cut = block // 2
    if tiled:
        tall, broad = rows // (parts if sizes is not None else rows // 512), columns
        steps = rows // tall
        at = lambda i: (i, 0)
        left_at, right_at = (lambda i: (kind, 0, i)), (lambda i: (0, 0))
    else:
        tall, broad = rows, next(w for w in (1024, 768, 512, 128) if columns % w == 0)
        steps = columns // broad
        at = lambda i: (0, i)
        left_at, right_at = (lambda i: (kind, 0, 0)), (lambda i: (0, i))
    others = [] if came is None else [came.reshape(rows, columns)]
    if share is not None:
        others.append(share.reshape(1, 1))
    given = 2 + len(others)

    def body(*refs):
        outs = refs[given:]
        out = contract_rows(refs[0][0], refs[1][...])
        if share is not None:
            out = out * refs[given - 1][...]
        if came is not None:
            out = out + refs[2][...].astype(f32)
        if sizes is None:
            outs[0][...] = out.astype(bf16)
        elif tiled:
            i = pl.program_id(0)
            out = out.astype(bf16).reshape(nz, block, broad)
            for k in range(ny):

                @pl.when(i // nx == k)
                def _(k=k):
                    outs[k][0] = out[:, :cut]

            for k in range(nx):

                @pl.when(i % nx == k)
                def _(k=k):
                    outs[ny + k][0] = out[:, cut:]

        else:
            out = out.astype(bf16).reshape(ny, nx, nz, block, broad)
            for k in range(ny):
                outs[k][...] = out[k, :, :, :cut]
            for k in range(nx):
                outs[ny + k][...] = out[:, k, :, cut:]

    specs = [pl.BlockSpec((1, tokens, tall), left_at), pl.BlockSpec((tokens, broad), right_at)]
    if came is not None:
        specs.append(pl.BlockSpec((tall, broad), at))
    if share is not None:
        specs.append(pl.BlockSpec((1, 1), lambda i: (0, 0)))
    if sizes is None:
        shapes, out_specs = [(rows, columns)], [pl.BlockSpec((tall, broad), at)]
    else:
        shapes = [(nx, nz, cut, columns)] * ny + [(ny, nz, cut, columns)] * nx
        if tiled:
            out_specs = [
                pl.BlockSpec((1, nz, cut, broad), lambda i, k=k: (jnp.clip(i - k * nx, 0, nx - 1), 0, 0, 0)) for k in range(ny)
            ]
            out_specs += [pl.BlockSpec((1, nz, cut, broad), lambda i, k=k: (jnp.maximum(i - k, 0) // nx, 0, 0, 0)) for k in range(nx)]
        else:
            out_specs = [pl.BlockSpec(shape[:3] + (broad,), lambda i: (0, 0, 0, i)) for shape in shapes]
    outs = pl.pallas_call(
        body,
        out_shape=[jax.ShapeDtypeStruct(shape, bf16) for shape in shapes],
        grid=(steps,),
        in_specs=specs,
        out_specs=out_specs,
        compiler_params=room(),
        cost_estimate=cost(2 * tokens * rows * columns, 4 * rows * columns),
        name="weight_grad",
    )(left, right, *others)
    return outs[0] if sizes is None else (outs[:ny], outs[ny:])


def total(arrays):
    out = arrays[0].astype(f32)
    for array in arrays[1:]:
        out = out + array.astype(f32)
    return out


def tie(*values):
    return lax.optimization_barrier(values)


def of_head(part):
    return lax.broadcasted_iota(jnp.int32, (1, 2 * HD), 1) // HD == part


def mask_tail(scores, fill):
    start = LENGTH // 8 * 8
    row = lax.broadcasted_iota(jnp.int32, (PACKED - start, PACKED), 0)
    tail = jnp.where(row < LENGTH - start, scores[start:], fill)
    return jnp.concatenate([scores[:start], tail], axis=0)


def flip(array):
    return array.astype(f32).T.astype(bf16)


def attend_body(q_ref, k_ref, v_ref, o_ref, l_ref):
    query, key = q_ref[...] * jnp.asarray(HD**-0.5, bf16), k_ref[...]
    value_t = flip(v_ref[...])
    mixed, logs = [], []
    for part in range(2):
        scores = contract_cols(jnp.where(of_head(part), key, 0), query)
        scores = mask_tail(scores, NEGATIVE)
        top = jnp.max(scores, axis=0, keepdims=True)
        exponent = jnp.exp(scores - top)
        total = jnp.sum(exponent, axis=0, keepdims=True)
        out = dot_float(value_t[HD * part : HD * (part + 1)], exponent.astype(bf16))
        mixed.append(out * (1.0 / total))
        logs.append(top + jnp.log(total))
    o_ref[...] = jnp.concatenate(mixed, axis=0).T.astype(bf16)
    l_ref[...] = jnp.concatenate(logs + [jnp.zeros((6, PACKED), f32)], axis=0)


PAIR = (PACKED, 2 * HD)
PAIRS = H // 2
CUT = PAIRS // 2


def kind_spec(kind, base=0):
    return pl.BlockSpec(PAIR, lambda i: (0, (i + base) // CUT * 3 * CUT + (i + base) % CUT + kind * CUT))


def pair_spec(base=0):
    return pl.BlockSpec(PAIR, lambda i: (0, i + base))


def log_spec(base=0):
    return pl.BlockSpec((8, PACKED), lambda i: (i + base, 0))


def halved(array):
    return array.reshape(-1, 3, 2, H * HD // 2).swapaxes(1, 2).reshape(array.shape)


def whole(array):
    return array.reshape(-1, 2, 3, H * HD // 2).swapaxes(1, 2).reshape(array.shape)


def attend(qkv):
    return pl.pallas_call(
        attend_body,
        out_shape=[
            jax.ShapeDtypeStruct((PACKED, H * HD), bf16),
            jax.ShapeDtypeStruct((8 * PAIRS, PACKED), f32),
        ],
        grid=(PAIRS,),
        in_specs=[kind_spec(0), kind_spec(1), kind_spec(2)],
        out_specs=[pair_spec(), log_spec()],
        compiler_params=room(),
        cost_estimate=cost(12e9, 8 * qkv.size, PACKED * PACKED * H),
        name="attend",
    )(qkv, qkv, qkv)


def attend_back_body(q_ref, k_ref, v_ref, l_ref, g_ref, d_ref, s_ref):
    scale = jnp.asarray(HD**-0.5, bf16)
    query, key, value, grad = q_ref[...] * scale, k_ref[...], v_ref[...], g_ref[...]
    key_t = flip(key)
    grad_query, grad_key, grad_value = [], [], []
    for part in range(2):
        mask = of_head(part)
        scores = contract_cols(jnp.where(mask, key, 0), query)
        soft = mask_tail(jnp.exp(scores - l_ref[part : part + 1]), 0.0)
        grad_soft = contract_cols(jnp.where(mask, value, 0), grad)
        delta = jnp.sum(soft * grad_soft, axis=0, keepdims=True)
        grad_scores = (soft * (grad_soft - delta)).astype(bf16)
        grad_value.append(dot_float(soft.astype(bf16), grad))
        grad_key.append(dot_float(grad_scores, query))
        grad_query.append(dot_float(key_t[HD * part : HD * (part + 1)], grad_scores))
    first = of_head(0)
    grads = (
        jnp.concatenate(grad_query, axis=0).T * HD**-0.5,
        jnp.where(first, grad_key[0], grad_key[1]),
        jnp.where(first, grad_value[0], grad_value[1]),
    )
    for kind, array in enumerate(grads):
        i = pl.program_id(0)
        start = pl.multiple_of((i // CUT * 3 * CUT + i % CUT + kind * CUT) * 2 * HD, 2 * HD)
        low = array.astype(bf16)
        d_ref[:, pl.ds(start, 2 * HD)] = low
        s_ref[:, pl.ds(start, 2 * HD)] = jnp.sum(low.astype(f32), axis=0, keepdims=True)


def attend_back(qkv, logs, grad_mixed):
    shape = qkv.shape
    return pl.pallas_call(
        attend_back_body,
        out_shape=[jax.ShapeDtypeStruct(shape, bf16), jax.ShapeDtypeStruct((1, shape[1]), f32)],
        grid=(PAIRS,),
        in_specs=[kind_spec(0), kind_spec(1), kind_spec(2), log_spec(), pair_spec()],
        out_specs=[pl.BlockSpec(shape, lambda i: (0, 0)), pl.BlockSpec((1, shape[1]), lambda i: (0, 0))],
        compiler_params=room(),
        cost_estimate=cost(12e9, 8 * qkv.size, PACKED * PACKED * H // 2),
        name="attend_back",
    )(qkv, qkv, qkv, logs, grad_mixed)


def rise(normed, weights, bias, ranks):
    width, ff = weights.shape
    step = ff // 4
    count = ranks.shape[0]
    block = ff // count
    inside = step // block
    whole_tiles = block % 128 == 0

    def body(rank_ref, x_ref, w_ref, b_ref, active_ref, slope_ref, *rest):
        i = pl.program_id(0)
        hidden = dot_float(x_ref[...], w_ref[...]) + b_ref[...]
        share = 0.5 * (1.0 + lax.erf(hidden * np.float32(np.sqrt(0.5))))
        active = (hidden * share).astype(bf16)
        active_ref[...] = active
        bell = jnp.exp(hidden * hidden * -0.5) * np.float32(1.0 / np.sqrt(2.0 * np.pi))
        slope_ref[...] = share + hidden * bell
        if not whole_tiles:
            return
        far_ref, held, sems = rest
        held[i % 2] = active

        def copies(turn):
            out = []
            for k in range(inside):
                rank = rank_ref[turn * inside + k]
                start = pl.multiple_of(rank % (count // 2) * block, block)
                window = held.at[turn % 2, :, pl.ds(k * block, block)]
                out.append(pltpu.make_async_copy(window, far_ref.at[rank // (count // 2), :, pl.ds(start, block)], sems.at[turn % 2, k]))
            return out

        for copy in copies(i):
            copy.start()

        @pl.when(i > 0)
        def _():
            for copy in copies(i - 1):
                copy.wait()

        @pl.when(i == 3)
        def _():
            for copy in copies(i):
                copy.wait()

    shapes = [jax.ShapeDtypeStruct((PACKED, ff), bf16), jax.ShapeDtypeStruct((PACKED, ff), f32)]
    specs = [pl.BlockSpec((PACKED, step), lambda i, t: (0, i))] * 2
    scratch = []
    if whole_tiles:
        shapes.append(jax.ShapeDtypeStruct((2, PACKED, ff // 2), bf16))
        specs.append(pl.BlockSpec(memory_space=pl.ANY))
        scratch = [pltpu.VMEM((2, PACKED, step), bf16), pltpu.SemaphoreType.DMA((2, inside))]
    outs = pl.pallas_call(
        body,
        out_shape=shapes,
        grid_spec=pltpu.PrefetchScalarGridSpec(
            num_scalar_prefetch=1,
            grid=(4,),
            in_specs=[
                pl.BlockSpec((PACKED, width), lambda i, t: (0, 0)),
                pl.BlockSpec((width, step), lambda i, t: (0, i)),
                pl.BlockSpec((1, step), lambda i, t: (0, i)),
            ],
            out_specs=specs,
            scratch_shapes=scratch,
        ),
        compiler_params=room(),
        cost_estimate=cost(12e9, 30e6, PACKED * ff * 2),
        name="rise",
    )(ranks, normed, weights, bias.reshape(1, ff))
    return outs if whole_tiles else (outs[0], outs[1], None)


def fall_body(g_ref, w_ref, slope_ref, out_ref, sum_ref):
    grad = (contract_cols(g_ref[...], w_ref[...]) * slope_ref[...]).astype(bf16)
    out_ref[...] = grad
    sum_ref[...] = jnp.sum(grad.astype(f32), axis=0, keepdims=True)


def fall(grads, weights, slope):
    ff, width = weights.shape
    step = ff // 4
    return pl.pallas_call(
        fall_body,
        out_shape=[jax.ShapeDtypeStruct((PACKED, ff), bf16), jax.ShapeDtypeStruct((1, ff), f32)],
        grid=(4,),
        in_specs=[
            pl.BlockSpec((PACKED, width), lambda i: (0, 0)),
            pl.BlockSpec((step, width), lambda i: (i, 0)),
            pl.BlockSpec((PACKED, step), lambda i: (0, i)),
        ],
        out_specs=[pl.BlockSpec((PACKED, step), lambda i: (0, i)), pl.BlockSpec((1, step), lambda i: (0, i))],
        compiler_params=room(),
        cost_estimate=cost(10e9, 25e6),
        name="fall",
    )(grads, weights, slope)


def project_body(x_ref, w_ref, b_ref, out_ref):
    out_ref[...] = (dot_float(x_ref[...], w_ref[...]) + b_ref[...]).astype(bf16)


def project(left, weights, bias):
    width, columns = weights.shape
    step = columns // 3
    return pl.pallas_call(
        project_body,
        out_shape=jax.ShapeDtypeStruct((PACKED, columns), bf16),
        grid=(3,),
        in_specs=[
            pl.BlockSpec((PACKED, width), lambda i: (0, 0)),
            pl.BlockSpec((width, step), lambda i: (0, i)),
            pl.BlockSpec((1, step), lambda i: (0, i)),
        ],
        out_specs=pl.BlockSpec((PACKED, step), lambda i: (0, i)),
        compiler_params=room(),
        cost_estimate=cost(6e9, 12e6),
        name="project",
    )(left, weights, bias.reshape(1, columns))


def row(vector):
    return vector.reshape(1, -1)


def fixed(shape):
    return pl.BlockSpec(shape, lambda i: (0,) * len(shape))


def seed(weights, vectors, long):
    rows, width = weights.shape
    half = width // 6

    def body(w_ref, *refs):
        out_ref = refs[-1]
        for k in range(6):
            out_ref[:, k * half : (k + 1) * half] = w_ref[:, pl.ds((k % 3 * 2 + k // 3) * half, half)]
        out_ref[:, width:] = jnp.zeros((rows, SMALL), bf16)
        for k in range(len(vectors)):
            out_ref[k : k + 1, width : width + rows] = refs[k][...]
        out_ref[0:1, width + 128 : width + 128 + long.shape[0]] = refs[len(vectors)][...]

    return pl.pallas_call(
        body,
        out_shape=jax.ShapeDtypeStruct((rows, width + SMALL), bf16),
        cost_estimate=cost(0, 1e6),
        name="seed",
    )(weights, *[row(v) for v in vectors], row(long))


def pack_norm_body(p_ref, x_ref, g_ref, s_ref, t_ref, n_ref):
    tokens = dot_float(p_ref[...], x_ref[...])
    t_ref[...] = tokens
    n_ref[...] = norm_rows(tokens, g_ref[...], s_ref[...]).astype(bf16)


def pack_norm(packing, slots, gain, shift):
    count, width = slots.shape
    half = PACKED // 2
    by_row = pl.BlockSpec((half, width), lambda i: (i, 0))
    return pl.pallas_call(
        pack_norm_body,
        out_shape=[jax.ShapeDtypeStruct((PACKED, width), f32), jax.ShapeDtypeStruct((PACKED, width), bf16)],
        grid=(2,),
        in_specs=[pl.BlockSpec((half, count), lambda i: (i, 0)), fixed((count, width)), fixed((1, width)), fixed((1, width))],
        out_specs=[by_row, by_row],
        compiler_params=room(),
        cost_estimate=cost(1e9, 8e6),
        name="pack_norm",
    )(packing, slots, row(gain), row(shift))


def pack_body(p_ref, x_ref, o_ref, s_ref):
    low = dot_float(p_ref[...], x_ref[...]).astype(bf16)
    o_ref[...] = low
    s_ref[...] = jnp.sum(low.astype(f32), axis=0, keepdims=True)


def pack(packing, slots):
    count, width = slots.shape
    half = width // 2
    return pl.pallas_call(
        pack_body,
        out_shape=[jax.ShapeDtypeStruct((PACKED, width), bf16), jax.ShapeDtypeStruct((1, width), f32)],
        grid=(2,),
        in_specs=[fixed((PACKED, count)), pl.BlockSpec((count, half), lambda i: (0, i))],
        out_specs=[pl.BlockSpec((PACKED, half), lambda i: (0, i)), pl.BlockSpec((1, half), lambda i: (0, i))],
        compiler_params=room(),
        cost_estimate=cost(1e9, 4e6),
        name="pack",
    )(packing, slots)


def out_norm_body(m_ref, w_ref, t_ref, b_ref, g_ref, s_ref, r_ref, n_ref):
    residual = t_ref[...] + dot_float(m_ref[...], w_ref[...]) + b_ref[...]
    r_ref[...] = residual
    n_ref[...] = norm_rows(residual, g_ref[...], s_ref[...]).astype(bf16)


def out_norm(mixed, weights, tokens, bias, gain, shift):
    width = weights.shape[1]
    half = PACKED // 2
    by_row = pl.BlockSpec((half, width), lambda i: (i, 0))
    vec = fixed((1, width))
    return pl.pallas_call(
        out_norm_body,
        out_shape=[jax.ShapeDtypeStruct((PACKED, width), f32), jax.ShapeDtypeStruct((PACKED, width), bf16)],
        grid=(2,),
        in_specs=[by_row, fixed(weights.shape), by_row, vec, vec, vec],
        out_specs=[by_row, by_row],
        compiler_params=room(),
        cost_estimate=cost(2e9, 8e6),
        name="out_norm",
    )(mixed, weights, tokens, row(bias), row(gain), row(shift))


def land_body(a_ref, w_ref, r_ref, b_ref, p_ref, o_ref, sum_ref):
    i = pl.program_id(0)
    part = dot_float(a_ref[...], w_ref[...])

    @pl.when(i == 0)
    def _():
        sum_ref[...] = part + r_ref[...] + b_ref[...]

    @pl.when(i > 0)
    def _():
        sum_ref[...] += part

    @pl.when(i == pl.num_programs(0) - 1)
    def _():
        o_ref[...] = contract_rows(p_ref[...], sum_ref[...].astype(bf16)).astype(bf16)


def land(active, weights, residual, bias, packing):
    ff, width = weights.shape
    step = ff // 4
    count = packing.shape[1]
    return pl.pallas_call(
        land_body,
        out_shape=jax.ShapeDtypeStruct((count, width), bf16),
        grid=(4,),
        in_specs=[
            pl.BlockSpec((PACKED, step), lambda i: (0, i)),
            pl.BlockSpec((step, width), lambda i: (i, 0)),
            fixed((PACKED, width)),
            fixed((1, width)),
            fixed((PACKED, count)),
        ],
        out_specs=fixed((count, width)),
        scratch_shapes=[pltpu.VMEM((PACKED, width), f32)],
        compiler_params=room(),
        cost_estimate=cost(6e9, 14e6),
        name="land",
    )(active, weights, residual, row(bias), packing)


def back_norm(grads, weights, values, gain, added, packing=None):
    width = weights.shape[0]
    step = weights.shape[1] // (4 if len(grads) == 1 else len(grads))
    steps = weights.shape[1] // step
    count = len(grads)

    def body(*refs):
        g_refs, (w_ref, x_ref, gain_ref, add_ref), rest = refs[:count], refs[count : count + 4], refs[count + 4 :]
        sum_ref = rest[-1]
        i = pl.program_id(0)
        for k, g_ref in enumerate(g_refs):

            @pl.when((i == k) if count > 1 else (i >= 0))
            def _(g_ref=g_ref, k=k):
                part = contract_cols(g_ref[...], w_ref[...])

                @pl.when(i == 0)
                def _():
                    sum_ref[...] = part

                @pl.when(i > 0)
                def _():
                    sum_ref[...] += part

        @pl.when(i == steps - 1)
        def _():
            back = sum_ref[...]
            values = x_ref[...]
            centred = values - jnp.mean(values, axis=-1, keepdims=True)
            scale = lax.rsqrt(jnp.mean(centred * centred, axis=-1, keepdims=True) + EPSILON)
            normed = centred * scale
            scaled = back * gain_ref[...]
            inner = jnp.mean(scaled * normed, axis=-1, keepdims=True)
            out = (scaled - jnp.mean(scaled, axis=-1, keepdims=True) - normed * inner) * scale + add_ref[...].astype(f32)
            low = out.astype(bf16)
            if packing is None:
                out_ref, low_ref, sums_ref = rest[:3]
                out_ref[...] = out
                low_ref[...] = low
            else:
                p_ref, low_ref, sums_ref = rest[:3]
                low_ref[...] = contract_rows(p_ref[...], low).astype(bf16)
            sums = [jnp.sum(a, axis=0, keepdims=True) for a in (back * normed, back, low.astype(f32))]
            sums_ref[...] = jnp.concatenate(sums + [jnp.zeros((5, width), f32)], axis=0)

    full = fixed((PACKED, width))
    if packing is None:
        shapes = [jax.ShapeDtypeStruct((PACKED, width), f32), jax.ShapeDtypeStruct((PACKED, width), bf16)]
        out_specs, more_specs, more = [full, full], [], []
    else:
        shapes = [jax.ShapeDtypeStruct((packing.shape[1], width), bf16)]
        out_specs, more_specs, more = [fixed(shapes[0].shape)], [fixed(packing.shape)], [packing]
    g_spec = fixed((PACKED, step)) if count > 1 else pl.BlockSpec((PACKED, step), lambda i: (0, i))
    return pl.pallas_call(
        body,
        out_shape=shapes + [jax.ShapeDtypeStruct((8, width), f32)],
        grid=(steps,),
        in_specs=[g_spec] * count + [pl.BlockSpec((width, step), lambda i: (0, i)), full, fixed((1, width)), full] + more_specs,
        out_specs=out_specs + [fixed((8, width))],
        scratch_shapes=[pltpu.VMEM((PACKED, width), f32)],
        compiler_params=room(),
        cost_estimate=cost(6e9, 20e6),
        name="back_norm",
    )(*grads, weights, values, row(gain), added, *more)


def back_project_body(g_ref, w_ref, o_ref):
    o_ref[...] = contract_cols(g_ref[...], w_ref[...]).astype(bf16)


def back_project(grads, weights):
    rows, width = weights.shape
    half = rows // 2
    return pl.pallas_call(
        back_project_body,
        out_shape=jax.ShapeDtypeStruct((PACKED, rows), bf16),
        grid=(2,),
        in_specs=[fixed((PACKED, width)), pl.BlockSpec((half, width), lambda i: (i, 0))],
        out_specs=pl.BlockSpec((PACKED, half), lambda i: (0, i)),
        compiler_params=room(),
        cost_estimate=cost(2e9, 5e6),
        name="back_project",
    )(grads, weights)


def layer(ring, tokens, counts, w_qkv, bias_q, bias_v, w_out, bias_out, w_up, bias_up, w_down, bias_down, gain_one, shift_one, gain_two, shift_two, cotangent):
    images, slots, width = tokens.shape
    group = ring.sizes["sz"] * ring.sizes["sc"]
    twins = group // images
    rows = w_qkv.shape[0]
    wide = w_down.shape[0] // rows
    ff = w_up.shape[1]

    slot = lax.broadcasted_iota(jnp.int32, (images, slots, 1), 1)
    marked = jnp.where(slot < counts[:, :, None], tokens, jnp.asarray(ABSENT, bf16))

    def back_pieces(pieces, own):
        pieces = jnp.stack([own] + [pieces[k] for k in everything])
        return pieces[:, 0], ring.swap(pieces[:, 1])

    def slots_of(array):
        return array.reshape(depth, 2, slots, width)

    depth = ring.sizes["sz"]
    outer = [k for k in range(1, depth) if k in (1, depth - 1)]
    inner = [k for k in range(1, depth) if k not in outer]
    everything = list(range(1, depth))

    small = [bias_q, bias_v, bias_out, bias_down, gain_one, shift_one, gain_two, shift_two]

    def arrays_of(sources):
        return [source[0] for source in sources]

    def with_arrays(sources, arrays):
        return [(array,) + source[1:] for array, source in zip(arrays, sources)]

    one = seed(w_qkv, small, bias_up)
    column = ring.spread(one, everything)
    stay, go = ring.blocks_for(marked, twins)
    came = ring.swap(go)
    cot_stay, go = ring.blocks_for(cotangent, twins)
    cot_came = ring.swap(go)
    one = ring.along(one, column)
    two = jnp.concatenate([w_out, w_up], axis=1)
    one, two, stay, came, cot_stay, cot_came = tie(one, two, stay, came, cot_stay, cot_came)

    one = ring.across(one)
    column = ring.spread(two, outer)
    pieces = ring.paired(stay, came)
    cot_pieces = ring.paired(cot_stay, cot_came)
    one, two, column, pieces, cot_pieces = tie(one, two, column, pieces, cot_pieces)

    one_more = ring.plane(one)
    one_core = ring.to_core([[half] for half in one])
    column.update(ring.spread(two, inner))
    two = ring.along(two, column)
    one, one_more, one_core, two, pieces, cot_pieces = tie(one, one_more, one_core, two, pieces, cot_pieces)

    one_more_core = ring.to_core(one_more)
    two = ring.across(two)
    rest = ring.send(pieces, outer[:1])
    one, one_more, one_core, one_more_core, two, pieces, three = tie(one, one_more, one_core, one_more_core, two, pieces, w_down)

    two_near = ring.flat([[half] for half in two])
    two_more = ring.plane(two)
    rest.update(ring.send(pieces, everything[1:]))
    full_qkv, vectors = ring.assemble(ring.sources(one, one_core, one_more, one_more_core), [3 * width, SMALL])
    two_more = ring.flat(two_more)
    two_near, two_more, rest, full_qkv, vectors, three = tie(two_near, two_more, rest, full_qkv, vectors, three)

    column = ring.spread(three, everything)
    two_core = ring.swap(two_near)
    two_more_core = ring.swap(two_more)
    image_slots = jnp.concatenate([pieces[0]] + [rest[k] for k in everything]).reshape(group * slots, width)
    vectors = vectors.reshape(ring.count, rows, SMALL).astype(f32)
    bu = vectors[:, 0, 128 : 128 + wide * rows].reshape(ff)
    bq, bv, bo, bd, g1, s1, g2, s2 = [vectors[:, k, :rows].reshape(width) for k in range(8)]
    here = (image_slots[:, :1].astype(f32) < 0.5 * ABSENT).reshape(group, slots)
    held = jnp.sum(here.astype(f32), axis=1)
    before = jnp.sum(jnp.where(np.tril(np.ones((group, group), bool), -1), held[None, :], 0.0), axis=1)
    rank = before[:, None] + lax.broadcasted_iota(jnp.int32, (group, slots), 1).astype(f32)
    rank = jnp.where(here, rank, -1.0).reshape(1, group * slots).astype(jnp.int32)
    packing = (rank == lax.broadcasted_iota(jnp.int32, (PACKED, group * slots), 0)).astype(bf16)
    tokens_f, normed = pack_norm(packing, image_slots, g1, s1)
    qkv_bias = halved(jnp.concatenate([bq, jnp.zeros((width,), f32), bv]))
    qkv = project(normed, full_qkv, qkv_bias)
    mixed, logs = attend(qkv)
    three = ring.along(three, column)
    two_core, two_more_core, three, mixed = tie(two_core, two_more_core, three, mixed)

    three = ring.across(three)
    cot_rest = ring.send(cot_pieces, outer)
    full_out, full_up = ring.assemble(ring.flat_sources(two_near, two_core, two_more, two_more_core), [width, ff])
    residual, normed_two = out_norm(mixed, full_out, tokens_f, bo, g2, s2)
    normed_far = ring.by_distance(normed)
    three, normed_two, normed_far, cot_rest = tie(three, normed_two, normed_far, cot_rest)

    three_more = ring.plane(three)
    three_core = ring.to_core([[half] for half in three])
    cot_rest.update(ring.send(cot_pieces, inner))
    ranks = ring.far(lax.broadcasted_iota(jnp.int32, (ring.count,), 0))
    active, slope, active_far = rise(normed_two, full_up, bu, ranks)
    if active_far is None:
        active_far = ring.by_distance(active)
    mixed_far = ring.by_distance(mixed)
    two_far = ring.by_distance(normed_two)
    three, three_more, three_core, active, active_far, mixed_far, two_far, cot_rest = tie(
        three, three_more, three_core, active, active_far, mixed_far, two_far, cot_rest
    )

    three_more_core = ring.to_core(three_more)
    share = (lax.axis_index(("sz", "sc")) % twins == 0).astype(f32) if twins > 1 else None
    cot_slots = jnp.concatenate([cot_pieces[0]] + [cot_rest[k] for k in everything]).reshape(group * slots, width)
    grad_low, grad_bd = pack(packing, cot_slots)
    sent = weight_grad(active_far, 1, grad_low, share)
    three_more_core, sent, grad_low = tie(three_more_core, sent, grad_low)

    d = ring.swap(sent)
    (full_down,) = ring.assemble(ring.sources(three, three_core, three_more, three_more_core), [width])
    d, full_down = tie(d, full_down)

    d = ring.kept(active_far, grad_low, share, d)
    result = slots_of(land(active, full_down, residual, bd, packing))
    d, result = tie(d, result)

    d = ring.first(d)
    back = ring.send(result, outer, -1)
    hidden_low, grad_bu = fall(grad_low, full_down, slope)
    sent = weight_grad(two_far, 1, hidden_low, share)
    d, sent, back = tie(d, sent, back)

    d = ring.again(d)
    d, sent = tie(d, sent)

    d = ring.second(d)
    u = ring.swap(sent)
    back.update(ring.send(result, inner, -1))
    grad_residual, residual_low, sums_two = back_norm([hidden_low], full_up, residual, g2, grad_low)
    d, u, residual_low, back = tie(d, u, residual_low, back)

    d = ring.last(d)
    u = ring.kept(two_far, hidden_low, share, u)
    sent = weight_grad(mixed_far, 1, residual_low, share)
    d, u, sent, residual_low = tie(d, u, sent, residual_low)

    u = ring.first(u)
    d = ring.third(d)
    grad_mixed = back_project(residual_low, full_out)
    sent_out = sent
    grads, grad_sums = attend_back(qkv, logs, grad_mixed)
    sent = weight_grad(normed_far, 1, grads, share)
    u, sent_out, sent, d, grads = tie(u, sent_out, sent, d, grads)

    u = ring.again(u)
    u, sent_out, sent, grads, back = tie(u, sent_out, sent, grads, back)

    u = ring.second(u)
    o = ring.swap(sent_out)
    q = ring.swap(sent)
    grad_tokens, sums_one = back_norm([grads], full_qkv, tokens_f, g1, grad_residual, packing)
    grad_tokens = slots_of(grad_tokens)
    u, o, q, grads, grad_tokens, sums_one, back, d = tie(u, o, q, grads, grad_tokens, sums_one, back, d)

    sent_back = ring.send(grad_tokens, outer, -1)
    q = ring.kept(normed_far, grads, share, q)
    o = ring.reshaped(weight_grad(mixed_far, 0, residual_low, share, o))
    u = ring.last(u)
    joined_sum = whole(grad_sums[0])
    grad_bq, grad_bv = joined_sum[:width], joined_sum[2 * width :]
    small = [grad_bq, grad_bv, sums_two[2], grad_bd, sums_one[0], sums_one[1], sums_two[0], sums_two[1]]
    small = [array.reshape(ring.count, rows) for array in small] + [grad_bu.reshape(ring.count, wide * rows)]
    small = jnp.concatenate(small, axis=1)
    small = (small if share is None else small * share).astype(bf16)
    near_first = (ranks[None, :] == lax.broadcasted_iota(jnp.int32, (ring.count, 1), 0)).astype(bf16)
    small = dot_float(near_first, small).astype(bf16)
    small = jnp.pad(small, ((0, 0), (0, rows * SMALL - small.shape[1]))).reshape(2, ring.count // 2 * rows, SMALL)
    q, o, small, u, sent_back, grad_tokens, back, d = tie(q, o, small, u, sent_back, grad_tokens, back, d)

    q = ring.first(q)
    sent_back.update(ring.send(grad_tokens, inner, -1))
    came = ring.swap(small[1])
    own = jnp.stack([result[0]] + [back[k] for k in everything])
    q, came, sent_back, u, back, d, own = tie(q, came, sent_back, u, back, d, own)

    q = ring.again(q)
    q, u, own, d = tie(q, u, own, d)

    q = ring.second(q)
    later = ring.toward_some(u, outer)
    other = ring.swap(own[:, 1])
    small = ring.reshaped(total([small[0], came]).astype(bf16))
    o = ring.ready(jnp.concatenate([o, small], axis=-1))
    q, later, other, o, u, own, d = tie(q, later, other, o, u, own, d)

    q = ring.last(q)
    q, o, u, d = tie(q, o, u, d)

    o = ring.first(o)
    later.update(ring.toward_some(u, inner))
    result = ring.images_of(own[:, 0], other, images, twins)
    result = jnp.where(slot < counts[:, :, None], result, jnp.asarray(0, bf16))
    o, later, result, q, d = tie(o, later, result, q, d)

    o = ring.again(o)
    o, q, d = tie(o, q, d)

    q = ring.third(q)
    o = ring.second(o)
    u = [u[0]] + [later[k] for k in everything]
    grad_tokens, came = back_pieces(sent_back, grad_tokens[0])
    q, o, grad_tokens, came = tie(q, o, grad_tokens, came)

    o = ring.third(ring.last(o))
    grad_tokens = ring.images_of(grad_tokens, came, images, twins).astype(f32)

    sum_down, sum_up = total(d), total(u)
    o = total(o)
    sum_out = o[:, :width]
    sum_qkv = whole(total(q))
    small = o[:, width:].reshape(rows * SMALL)
    sum_bq, sum_bv, sum_bo, sum_bd, sum_g1, sum_s1, sum_g2, sum_s2 = [small[k * rows : (k + 1) * rows] for k in range(8)]
    sum_bu = small[8 * rows : (8 + wide) * rows]
    return (result, grad_tokens, sum_qkv, sum_bq, sum_bv, sum_out, sum_bo, sum_up, sum_bu, sum_down, sum_bd, sum_g1, sum_s1, sum_g2, sum_s2)


def solution(mesh):
    n_grp, n_seq = mesh.shape["grp"], mesh.shape["seq"]
    sizes = (n_grp // 2, 2, n_seq // 2, 2)
    fine = Mesh(mesh.devices.reshape(sizes), AXES)
    ring = Ring(sizes)
    grp, seq = AXES[:2], AXES[2:]
    by_token = P(grp, seq, None)
    rows, vec = P(AXES, None), P(AXES)
    in_specs = (by_token, P(grp, seq), rows, vec, vec, rows, vec, rows, vec, rows, vec, vec, vec, vec, vec, by_token)
    out_specs = (by_token, by_token, rows, vec, vec, rows, vec, rows, vec, rows, vec, vec, vec, vec, vec)

    def shards(*args):
        return layer(ring, *args)

    return jax.shard_map(shards, mesh=fine, in_specs=in_specs, out_specs=out_specs, check_vma=False)
```

```python
import jax
import jax.numpy as jnp
import numpy as np
from jax import lax
from jax.experimental import pallas as pl
from jax.experimental.pallas import tpu as pltpu
from jax.sharding import Mesh
from jax.sharding import PartitionSpec as P

H = 16
HD = 64
LENGTH = 577
PACKED = 592
EPSILON = 1e-06
NEGATIVE = -1e30
ABSENT = 100.0
SMALL = 256
AXES = ("gy", "gx", "sz", "sc")
ORDERS = (("gx", "gy"), ("gy", "gx"))

bf16 = jnp.bfloat16
f32 = jnp.float32


def norm_rows(values, gain_vec, shift_vec):
    row_mean = jnp.mean(values, axis=-1, keepdims=True)
    centred = values - row_mean
    row_var = jnp.mean(centred * centred, axis=-1, keepdims=True)
    return centred * lax.rsqrt(row_var + EPSILON) * gain_vec + shift_vec


def dot_float(left, right):
    return jnp.dot(left, right, preferred_element_type=f32)


def contract_rows(left, right):
    return lax.dot_general(left, right, (((0,), (0,)), ((), ())), preferred_element_type=f32)


def contract_cols(left, right):
    return lax.dot_general(left, right, (((1,), (1,)), ((), ())), preferred_element_type=f32)


def room(mib=50):
    return pltpu.CompilerParams(vmem_limit_bytes=mib * 2**20)


HINT = 0.02


def cost(flops, bytes_accessed, transcendentals=0):
    return pl.CostEstimate(
        flops=int(HINT * flops), bytes_accessed=int(HINT * bytes_accessed), transcendentals=int(HINT * transcendentals)
    )


def shifted(array, axis, size, step):
    return lax.ppermute(array, axis, [(i, (i + step) % size) for i in range(size)])


def pick(array, index, axis):
    return lax.dynamic_index_in_dim(array, index, axis, keepdims=False)


class Ring:
    def __init__(self, sizes):
        self.sizes = dict(zip(AXES, sizes))
        self.count = int(np.prod(sizes))

    def place(self):
        return {axis: lax.axis_index(axis) for axis in AXES}

    def others(self, array, axis):
        size = self.sizes[axis]
        return [shifted(array, axis, size, step) for step in range(1, size)]

    def others_from(self, array, axis, steps):
        size = self.sizes[axis]
        return [shifted(array, axis, size, step) for step in steps]

    def along(self, shard, columns):
        cut = shard.shape[0] // 2
        size = self.sizes["sz"]
        columns = [shard] + [columns[k] for k in range(1, size)]
        here = lax.axis_index("sz")
        ordered = [lax.select_n((here - k) % size, *columns) if size > 2 else jnp.where(here == k, *columns) for k in range(size)]
        return [jnp.stack([c[:cut] for c in ordered]), jnp.stack([c[cut:] for c in ordered])]

    def spread(self, shard, steps):
        return {k: shifted(shard, "sz", self.sizes["sz"], k) for k in steps}

    def across(self, halves):
        return [jnp.stack([half] + self.others(half, order[0])) for half, order in zip(halves, ORDERS)]

    def plane(self, halves):
        return [self.others(half, order[1]) for half, order in zip(halves, ORDERS)]

    def to_core(self, groups):
        return [[shifted(group, "sc", 2, 1) for group in part] for part in groups]

    def sources(self, first, traded_first, second, traded_second):
        found = []
        for part in range(2):
            kinds = ([first[part]] + second[part], traded_first[part] + traded_second[part])
            for turn, groups in enumerate(kinds):
                found += [(g, turn, [(part, step, one) for one in range(g.shape[0])]) for step, g in enumerate(groups)]
        return found

    def flat(self, groups):
        return jnp.concatenate([group for part in groups for group in part], axis=0)

    def labels(self, far):
        sizes = self.sizes
        found = []
        for part in range(2):
            for step in range(1, sizes[ORDERS[part][1]]) if far else [0]:
                found += [(part, step, one) for one in range(sizes[ORDERS[part][0]])]
        return found

    def near_flat_sources(self, near, near_core, second, traded_second):
        found = [(near, 0, self.labels(False)), (near_core, 1, self.labels(False))]
        for turn, groups in enumerate((second, traded_second)):
            for part in range(2):
                for step, g in enumerate(groups[part]):
                    found.append((g, turn, [(part, step + 1, one) for one in range(g.shape[0])]))
        return found

    def assemble(self, sources, widths):
        place = self.place()
        sizes = self.sizes
        cut, width = sources[0][0].shape[-2:]
        depth = sizes["sz"]
        planes, kinds, parts, arrays, counts = [], [], [], [], []
        for group, turn, labels in sources:
            arrays.append(group)
            counts.append(len(labels))
            for part, step, one in labels:
                order = ORDERS[part]
                at = {order[1]: (place[order[1]] - step) % sizes[order[1]], order[0]: (place[order[0]] - one) % sizes[order[0]]}
                planes.append(at["gy"] * sizes["gx"] + at["gx"])
                kinds.append((place["sc"] - turn) % 2)
                parts.append(part)
        table = jnp.stack(planes + kinds).astype(jnp.int32)
        many = len(planes)
        starts = np.concatenate([[0], np.cumsum(widths)])

        def body(table_ref, *refs):
            ins = refs[: len(counts)]
            outs = refs[len(counts) : -3]
            held, came, left = refs[-3:]
            arrivals = []
            for ref, count in zip(ins, counts):
                for k in range(count):
                    n = len(arrivals)
                    arrivals.append(pltpu.make_async_copy(ref.at[k], held.at[n], came.at[n]))
            for copy in arrivals:
                copy.start()
            departures = []
            for n, copy in enumerate(arrivals):
                copy.wait()
                for i, out in enumerate(outs):
                    window = held.at[n, :, :, pl.ds(int(starts[i]), widths[i])]
                    target = out.at[table_ref[n], :, table_ref[many + n], parts[n]]
                    leave = pltpu.make_async_copy(window, target, left.at[n, i])
                    leave.start()
                    departures.append(leave)
            for copy in departures:
                copy.wait()

        planes_all = sizes["gy"] * sizes["gx"]
        outs = pl.pallas_call(
            body,
            out_shape=[jax.ShapeDtypeStruct((planes_all, depth, 2, 2, cut, w), bf16) for w in widths],
            grid_spec=pltpu.PrefetchScalarGridSpec(
                num_scalar_prefetch=1,
                grid=(1,),
                in_specs=[pl.BlockSpec(memory_space=pl.ANY)] * len(counts),
                out_specs=[pl.BlockSpec(memory_space=pl.ANY)] * len(widths),
                scratch_shapes=[
                    pltpu.VMEM((many, depth, cut, width), bf16),
                    pltpu.SemaphoreType.DMA((many,)),
                    pltpu.SemaphoreType.DMA((many, len(widths))),
                ],
            ),
            compiler_params=room(),
            cost_estimate=cost(0, 4 * self.count * 2 * cut * width),
            name="assemble",
        )(table, *arrays)
        return [out.reshape(self.count * 2 * cut, w) for out, w in zip(outs, widths)]

    def far(self, device):
        place = self.place()
        sizes = self.sizes
        index, out = device, {}
        for axis in AXES[::-1]:
            out[axis] = (index % sizes[axis] - place[axis]) % sizes[axis]
            index = index // sizes[axis]
        return ((out["sc"] * sizes["gy"] + out["gy"]) * sizes["gx"] + out["gx"]) * sizes["sz"] + out["sz"]

    def target(self, width):
        block = width // self.count
        row = lax.broadcasted_iota(jnp.int32, (width, 1), 0)
        return self.far(row // block) * block + row % block

    def by_distance(self, array, target):
        tokens, width = array.shape
        half = width // 2

        def body(x_ref, t_ref, o_ref):
            columns = lax.broadcasted_iota(jnp.int32, (width, half), 1) + half * pl.program_id(0)
            pick_columns = jnp.where(t_ref[...] == columns, 1.0, 0.0).astype(bf16)
            o_ref[0] = dot_float(x_ref[...], pick_columns).astype(bf16)

        return pl.pallas_call(
            body,
            out_shape=jax.ShapeDtypeStruct((2, tokens, half), bf16),
            grid=(2,),
            in_specs=[pl.BlockSpec((tokens, width), lambda i: (0, 0)), pl.BlockSpec((width, 1), lambda i: (0, 0))],
            out_specs=pl.BlockSpec((1, tokens, half), lambda i: (i, 0, 0)),
            compiler_params=room(),
            cost_estimate=cost(2 * tokens * width * width, 4 * tokens * width),
            name="by_distance",
        )(array, target)

    def blocks_for(self, array, twins):
        place = self.place()
        size = self.sizes["sz"]
        out = []
        for turn in range(2):
            found = [((place["sz"] + k) % size * 2 + (place["sc"] + turn) % 2) // twins for k in range(size)]
            out.append(jnp.stack([pick(array, image, 0) for image in found]))
        return out

    def paired(self, stay, came):
        return [jnp.stack([stay[k], came[k]]) for k in range(self.sizes["sz"])]

    def send(self, pieces, steps, sign=1):
        return {k: shifted(pieces[k], "sz", self.sizes["sz"], sign * k) for k in steps}

    def images_of(self, own, came, images, twins):
        place = self.place()
        size = self.sizes["sz"]
        both = jnp.stack([own, came])
        both = both.reshape((2 * size,) + both.shape[2:])
        out = []
        for image in range(images):
            device = image * twins
            out.append(pick(both, (device % 2 - place["sc"]) % 2 * size + (device // 2 - place["sz"]) % size, 0))
        return jnp.stack(out)

    def swap(self, sent):
        return shifted(sent, "sc", 2, 1)

    def reshaped(self, out):
        sizes = self.sizes
        return out.reshape(sizes["gy"], sizes["gx"], sizes["sz"], out.shape[0] // (self.count // 2), out.shape[1])

    def kept(self, left, right, share, came):
        cut = left.shape[2] // (self.count // 2) // 2
        if cut % 16 == 0:
            return weight_grad(left, 0, right, share, came, self.sizes)
        return self.ready(self.reshaped(weight_grad(left, 0, right, share, came)))

    def toward(self, arrays, axis):
        size = self.sizes[axis]
        return [arrays[0]] + [shifted(arrays[k], axis, size, k) for k in range(1, size)]

    def toward_some(self, parts, steps):
        return {k: shifted(parts[k], "sz", self.sizes["sz"], k) for k in steps}

    def ready(self, sums):
        cut = sums.shape[3] // 2
        upper = [sums[k, :, :, :cut] for k in range(self.sizes["gy"])]
        lower = [sums[:, k, :, cut:] for k in range(self.sizes["gx"])]
        return upper, lower

    def first(self, pair):
        return self.toward(pair[0], "gy"), self.toward(pair[1], "gx")

    def again(self, pair):
        return tuple(
            [total([t[k] for t in terms]).astype(bf16) for k in range(self.sizes[axis])]
            for terms, axis in zip(pair, ("gx", "gy"))
        )

    def second(self, pair):
        return self.toward(pair[0], "gx"), self.toward(pair[1], "gy")

    def last(self, pair):
        return [
            jnp.concatenate([total([t[k] for t in terms]) for terms in pair], axis=0).astype(bf16)
            for k in range(self.sizes["sz"])
        ]

    def third(self, parts):
        return self.toward(parts, "sz")


def weight_grad(left, kind, right, share, came=None, sizes=None):
    tokens, columns = right.shape
    rows = left.shape[2]
    tiled = rows > 512
    parts = 1
    if sizes is not None:
        ny, nx, nz = sizes["gy"], sizes["gx"], sizes["sz"]
        parts = ny * nx
        block = rows // (parts * nz)
        cut = block // 2
    if tiled:
        tall, broad = rows // (parts if sizes is not None else rows // 512), columns
        steps = rows // tall
        at = lambda i: (i, 0)
        left_at, right_at = (lambda i: (kind, 0, i)), (lambda i: (0, 0))
    else:
        tall, broad = rows, next(w for w in (1024, 768, 512, 128) if columns % w == 0)
        steps = columns // broad
        at = lambda i: (0, i)
        left_at, right_at = (lambda i: (kind, 0, 0)), (lambda i: (0, i))
    others = [] if came is None else [came.reshape(rows, columns)]
    if share is not None:
        others.append(share.reshape(1, 1))
    given = 2 + len(others)

    def body(*refs):
        outs = refs[given:]
        out = contract_rows(refs[0][0], refs[1][...])
        if share is not None:
            out = out * refs[given - 1][...]
        if came is not None:
            out = out + refs[2][...].astype(f32)
        if sizes is None:
            outs[0][...] = out.astype(bf16)
        elif tiled:
            i = pl.program_id(0)
            out = out.astype(bf16).reshape(nz, block, broad)
            for k in range(ny):

                @pl.when(i // nx == k)
                def _(k=k):
                    outs[k][0] = out[:, :cut]

            for k in range(nx):

                @pl.when(i % nx == k)
                def _(k=k):
                    outs[ny + k][0] = out[:, cut:]

        else:
            out = out.astype(bf16).reshape(ny, nx, nz, block, broad)
            for k in range(ny):
                outs[k][...] = out[k, :, :, :cut]
            for k in range(nx):
                outs[ny + k][...] = out[:, k, :, cut:]

    specs = [pl.BlockSpec((1, tokens, tall), left_at), pl.BlockSpec((tokens, broad), right_at)]
    if came is not None:
        specs.append(pl.BlockSpec((tall, broad), at))
    if share is not None:
        specs.append(pl.BlockSpec((1, 1), lambda i: (0, 0)))
    if sizes is None:
        shapes, out_specs = [(rows, columns)], [pl.BlockSpec((tall, broad), at)]
    else:
        shapes = [(nx, nz, cut, columns)] * ny + [(ny, nz, cut, columns)] * nx
        if tiled:
            out_specs = [
                pl.BlockSpec((1, nz, cut, broad), lambda i, k=k: (jnp.clip(i - k * nx, 0, nx - 1), 0, 0, 0)) for k in range(ny)
            ]
            out_specs += [pl.BlockSpec((1, nz, cut, broad), lambda i, k=k: (jnp.maximum(i - k, 0) // nx, 0, 0, 0)) for k in range(nx)]
        else:
            out_specs = [pl.BlockSpec(shape[:3] + (broad,), lambda i: (0, 0, 0, i)) for shape in shapes]
    outs = pl.pallas_call(
        body,
        out_shape=[jax.ShapeDtypeStruct(shape, bf16) for shape in shapes],
        grid=(steps,),
        in_specs=specs,
        out_specs=out_specs,
        compiler_params=room(),
        cost_estimate=cost(2 * tokens * rows * columns, 4 * rows * columns),
        name="weight_grad",
    )(left, right, *others)
    return outs[0] if sizes is None else (outs[:ny], outs[ny:])


def total(arrays):
    out = arrays[0].astype(f32)
    for array in arrays[1:]:
        out = out + array.astype(f32)
    return out


def tie(*values):
    return lax.optimization_barrier(values)


def of_head(part):
    return lax.broadcasted_iota(jnp.int32, (1, 2 * HD), 1) // HD == part


def mask_tail(scores, fill):
    start = LENGTH // 8 * 8
    row = lax.broadcasted_iota(jnp.int32, (PACKED - start, PACKED), 0)
    tail = jnp.where(row < LENGTH - start, scores[start:], fill)
    return jnp.concatenate([scores[:start], tail], axis=0)


def flip(array):
    return array.astype(f32).T.astype(bf16)


def attend_body(q_ref, k_ref, v_ref, o_ref, l_ref):
    query, key = q_ref[...] * jnp.asarray(HD**-0.5, bf16), k_ref[...]
    value_t = flip(v_ref[...])
    mixed, logs = [], []
    for part in range(2):
        scores = contract_cols(jnp.where(of_head(part), key, 0), query)
        scores = mask_tail(scores, NEGATIVE)
        top = jnp.max(scores, axis=0, keepdims=True)
        exponent = jnp.exp(scores - top)
        total = jnp.sum(exponent, axis=0, keepdims=True)
        out = dot_float(value_t[HD * part : HD * (part + 1)], exponent.astype(bf16))
        mixed.append(out * (1.0 / total))
        logs.append(top + jnp.log(total))
    o_ref[...] = jnp.concatenate(mixed, axis=0).T.astype(bf16)
    l_ref[...] = jnp.concatenate(logs + [jnp.zeros((6, PACKED), f32)], axis=0)


PAIR = (PACKED, 2 * HD)
PAIRS = H // 2
CUT = PAIRS // 2


def kind_spec(kind, base=0):
    return pl.BlockSpec(PAIR, lambda i: (0, (i + base) // CUT * 3 * CUT + (i + base) % CUT + kind * CUT))


def pair_spec(base=0):
    return pl.BlockSpec(PAIR, lambda i: (0, i + base))


def log_spec(base=0):
    return pl.BlockSpec((8, PACKED), lambda i: (i + base, 0))


def halved(array):
    return array.reshape(-1, 3, 2, H * HD // 2).swapaxes(1, 2).reshape(array.shape)


def whole(array):
    return array.reshape(-1, 2, 3, H * HD // 2).swapaxes(1, 2).reshape(array.shape)


def attend(qkv):
    return pl.pallas_call(
        attend_body,
        out_shape=[
            jax.ShapeDtypeStruct((PACKED, H * HD), bf16),
            jax.ShapeDtypeStruct((8 * PAIRS, PACKED), f32),
        ],
        grid=(PAIRS,),
        in_specs=[kind_spec(0), kind_spec(1), kind_spec(2)],
        out_specs=[pair_spec(), log_spec()],
        compiler_params=room(),
        cost_estimate=cost(12e9, 8 * qkv.size, PACKED * PACKED * H),
        name="attend",
    )(qkv, qkv, qkv)


def attend_back_body(q_ref, k_ref, v_ref, l_ref, g_ref, *rest):
    d_ref, s_ref = rest[-2:]
    base = 0
    if len(rest) == 4:
        base = rest[0].shape[1]

        @pl.when(pl.program_id(0) == 0)
        def _():
            d_ref[:, :base] = rest[0][...]
            s_ref[:, :base] = rest[1][...]

    scale = jnp.asarray(HD**-0.5, bf16)
    query, key, value, grad = q_ref[...] * scale, k_ref[...], v_ref[...], g_ref[...]
    key_t = flip(key)
    grad_query, grad_key, grad_value = [], [], []
    for part in range(2):
        mask = of_head(part)
        scores = contract_cols(jnp.where(mask, key, 0), query)
        soft = mask_tail(jnp.exp(scores - l_ref[part : part + 1]), 0.0)
        grad_soft = contract_cols(jnp.where(mask, value, 0), grad)
        delta = jnp.sum(soft * grad_soft, axis=0, keepdims=True)
        grad_scores = (soft * (grad_soft - delta)).astype(bf16)
        grad_value.append(dot_float(soft.astype(bf16), grad))
        grad_key.append(dot_float(grad_scores, query))
        grad_query.append(dot_float(key_t[HD * part : HD * (part + 1)], grad_scores))
    first = of_head(0)
    grads = (
        jnp.concatenate(grad_query, axis=0).T * HD**-0.5,
        jnp.where(first, grad_key[0], grad_key[1]),
        jnp.where(first, grad_value[0], grad_value[1]),
    )
    for kind, array in enumerate(grads):
        start = pl.multiple_of(base + (pl.program_id(0) + kind * CUT) * 2 * HD, 2 * HD)
        low = array.astype(bf16)
        d_ref[:, pl.ds(start, 2 * HD)] = low
        s_ref[:, pl.ds(start, 2 * HD)] = jnp.sum(low.astype(f32), axis=0, keepdims=True)


def attend_back(qkv, logs, grad_mixed, before=()):
    base = CUT if before else 0
    width = qkv.shape[1] // (1 if before else 2)
    return pl.pallas_call(
        attend_back_body,
        out_shape=[jax.ShapeDtypeStruct((PACKED, width), bf16), jax.ShapeDtypeStruct((1, width), f32)],
        grid=(CUT,),
        in_specs=[kind_spec(0, base), kind_spec(1, base), kind_spec(2, base), log_spec(base), pair_spec(base)]
        + [pl.BlockSpec(array.shape, lambda i: (0, 0)) for array in before],
        out_specs=[pl.BlockSpec((PACKED, width), lambda i: (0, 0)), pl.BlockSpec((1, width), lambda i: (0, 0))],
        compiler_params=room(),
        cost_estimate=cost(12e9, 8 * qkv.size, PACKED * PACKED * H // 2),
        name="attend_back",
    )(qkv, qkv, qkv, logs, grad_mixed, *before)


def rise(normed, weights, bias, ranks):
    width, ff = weights.shape
    step = ff // 4
    count = ranks.shape[0]
    block = ff // count
    inside = step // block
    whole_tiles = block % 128 == 0

    def body(rank_ref, x_ref, w_ref, b_ref, active_ref, slope_ref, *rest):
        i = pl.program_id(0)
        hidden = dot_float(x_ref[...], w_ref[...]) + b_ref[...]
        share = 0.5 * (1.0 + lax.erf(hidden * np.float32(np.sqrt(0.5))))
        active = (hidden * share).astype(bf16)
        active_ref[...] = active
        bell = jnp.exp(hidden * hidden * -0.5) * np.float32(1.0 / np.sqrt(2.0 * np.pi))
        slope_ref[...] = share + hidden * bell
        if not whole_tiles:
            return
        far_ref, held, sems = rest
        held[i % 2] = active

        def copies(turn):
            out = []
            for k in range(inside):
                rank = rank_ref[turn * inside + k]
                start = pl.multiple_of(rank % (count // 2) * block, block)
                window = held.at[turn % 2, :, pl.ds(k * block, block)]
                out.append(pltpu.make_async_copy(window, far_ref.at[rank // (count // 2), :, pl.ds(start, block)], sems.at[turn % 2, k]))
            return out

        for copy in copies(i):
            copy.start()

        @pl.when(i > 0)
        def _():
            for copy in copies(i - 1):
                copy.wait()

        @pl.when(i == 3)
        def _():
            for copy in copies(i):
                copy.wait()

    shapes = [jax.ShapeDtypeStruct((PACKED, ff), bf16), jax.ShapeDtypeStruct((PACKED, ff), f32)]
    specs = [pl.BlockSpec((PACKED, step), lambda i, t: (0, i))] * 2
    scratch = []
    if whole_tiles:
        shapes.append(jax.ShapeDtypeStruct((2, PACKED, ff // 2), bf16))
        specs.append(pl.BlockSpec(memory_space=pl.ANY))
        scratch = [pltpu.VMEM((2, PACKED, step), bf16), pltpu.SemaphoreType.DMA((2, inside))]
    outs = pl.pallas_call(
        body,
        out_shape=shapes,
        grid_spec=pltpu.PrefetchScalarGridSpec(
            num_scalar_prefetch=1,
            grid=(4,),
            in_specs=[
                pl.BlockSpec((PACKED, width), lambda i, t: (0, 0)),
                pl.BlockSpec((width, step), lambda i, t: (0, i)),
                pl.BlockSpec((1, step), lambda i, t: (0, i)),
            ],
            out_specs=specs,
            scratch_shapes=scratch,
        ),
        compiler_params=room(),
        cost_estimate=cost(12e9, 30e6, PACKED * ff * 2),
        name="rise",
    )(ranks, normed, weights, bias.reshape(1, ff))
    return outs if whole_tiles else (outs[0], outs[1], None)


def fall_body(g_ref, w_ref, slope_ref, out_ref, sum_ref):
    grad = (contract_cols(g_ref[...], w_ref[...]) * slope_ref[...]).astype(bf16)
    out_ref[...] = grad
    sum_ref[...] = jnp.sum(grad.astype(f32), axis=0, keepdims=True)


def fall(grads, weights, slope):
    ff, width = weights.shape
    step = ff // 4
    return pl.pallas_call(
        fall_body,
        out_shape=[jax.ShapeDtypeStruct((PACKED, ff), bf16), jax.ShapeDtypeStruct((1, ff), f32)],
        grid=(4,),
        in_specs=[
            pl.BlockSpec((PACKED, width), lambda i: (0, 0)),
            pl.BlockSpec((step, width), lambda i: (i, 0)),
            pl.BlockSpec((PACKED, step), lambda i: (0, i)),
        ],
        out_specs=[pl.BlockSpec((PACKED, step), lambda i: (0, i)), pl.BlockSpec((1, step), lambda i: (0, i))],
        compiler_params=room(),
        cost_estimate=cost(10e9, 25e6),
        name="fall",
    )(grads, weights, slope)


def project_body(x_ref, w_ref, b_ref, out_ref):
    out_ref[...] = (dot_float(x_ref[...], w_ref[...]) + b_ref[...]).astype(bf16)


def project(left, weights, bias):
    width, columns = weights.shape
    step = columns // 3
    return pl.pallas_call(
        project_body,
        out_shape=jax.ShapeDtypeStruct((PACKED, columns), bf16),
        grid=(3,),
        in_specs=[
            pl.BlockSpec((PACKED, width), lambda i: (0, 0)),
            pl.BlockSpec((width, step), lambda i: (0, i)),
            pl.BlockSpec((1, step), lambda i: (0, i)),
        ],
        out_specs=pl.BlockSpec((PACKED, step), lambda i: (0, i)),
        compiler_params=room(),
        cost_estimate=cost(6e9, 12e6),
        name="project",
    )(left, weights, bias.reshape(1, columns))


def row(vector):
    return vector.reshape(1, -1)


def fixed(shape):
    return pl.BlockSpec(shape, lambda i: (0,) * len(shape))


def seed(weights, vectors, long):
    rows, width = weights.shape
    half = width // 6

    def body(w_ref, *refs):
        out_ref = refs[-1]
        for k in range(6):
            out_ref[:, k * half : (k + 1) * half] = w_ref[:, pl.ds((k % 3 * 2 + k // 3) * half, half)]
        out_ref[:, width:] = jnp.zeros((rows, SMALL), bf16)
        for k in range(len(vectors)):
            out_ref[k : k + 1, width : width + rows] = refs[k][...]
        out_ref[0:1, width + 128 : width + 128 + long.shape[0]] = refs[len(vectors)][...]

    return pl.pallas_call(
        body,
        out_shape=jax.ShapeDtypeStruct((rows, width + SMALL), bf16),
        cost_estimate=cost(0, 1e6),
        name="seed",
    )(weights, *[row(v) for v in vectors], row(long))


def pack_norm_body(p_ref, x_ref, g_ref, s_ref, t_ref, n_ref):
    tokens = dot_float(p_ref[...], x_ref[...])
    t_ref[...] = tokens
    n_ref[...] = norm_rows(tokens, g_ref[...], s_ref[...]).astype(bf16)


def pack_norm(packing, slots, gain, shift):
    count, width = slots.shape
    half = PACKED // 2
    by_row = pl.BlockSpec((half, width), lambda i: (i, 0))
    return pl.pallas_call(
        pack_norm_body,
        out_shape=[jax.ShapeDtypeStruct((PACKED, width), f32), jax.ShapeDtypeStruct((PACKED, width), bf16)],
        grid=(2,),
        in_specs=[pl.BlockSpec((half, count), lambda i: (i, 0)), fixed((count, width)), fixed((1, width)), fixed((1, width))],
        out_specs=[by_row, by_row],
        compiler_params=room(),
        cost_estimate=cost(1e9, 8e6),
        name="pack_norm",
    )(packing, slots, row(gain), row(shift))


def pack_body(p_ref, x_ref, o_ref, s_ref):
    low = dot_float(p_ref[...], x_ref[...]).astype(bf16)
    o_ref[...] = low
    s_ref[...] = jnp.sum(low.astype(f32), axis=0, keepdims=True)


def pack(packing, slots):
    count, width = slots.shape
    half = width // 2
    return pl.pallas_call(
        pack_body,
        out_shape=[jax.ShapeDtypeStruct((PACKED, width), bf16), jax.ShapeDtypeStruct((1, width), f32)],
        grid=(2,),
        in_specs=[fixed((PACKED, count)), pl.BlockSpec((count, half), lambda i: (0, i))],
        out_specs=[pl.BlockSpec((PACKED, half), lambda i: (0, i)), pl.BlockSpec((1, half), lambda i: (0, i))],
        compiler_params=room(),
        cost_estimate=cost(1e9, 4e6),
        name="pack",
    )(packing, slots)


def out_norm_body(m_ref, w_ref, t_ref, b_ref, g_ref, s_ref, r_ref, n_ref):
    residual = t_ref[...] + dot_float(m_ref[...], w_ref[...]) + b_ref[...]
    r_ref[...] = residual
    n_ref[...] = norm_rows(residual, g_ref[...], s_ref[...]).astype(bf16)


def out_norm(mixed, weights, tokens, bias, gain, shift):
    width = weights.shape[1]
    half = PACKED // 2
    by_row = pl.BlockSpec((half, width), lambda i: (i, 0))
    vec = fixed((1, width))
    return pl.pallas_call(
        out_norm_body,
        out_shape=[jax.ShapeDtypeStruct((PACKED, width), f32), jax.ShapeDtypeStruct((PACKED, width), bf16)],
        grid=(2,),
        in_specs=[by_row, fixed(weights.shape), by_row, vec, vec, vec],
        out_specs=[by_row, by_row],
        compiler_params=room(),
        cost_estimate=cost(2e9, 8e6),
        name="out_norm",
    )(mixed, weights, tokens, row(bias), row(gain), row(shift))


def land_body(a_ref, w_ref, r_ref, b_ref, p_ref, o_ref, sum_ref):
    i = pl.program_id(0)
    part = dot_float(a_ref[...], w_ref[...])

    @pl.when(i == 0)
    def _():
        sum_ref[...] = part + r_ref[...] + b_ref[...]

    @pl.when(i > 0)
    def _():
        sum_ref[...] += part

    @pl.when(i == pl.num_programs(0) - 1)
    def _():
        o_ref[...] = contract_rows(p_ref[...], sum_ref[...].astype(bf16)).astype(bf16)


def land(active, weights, residual, bias, packing):
    ff, width = weights.shape
    step = ff // 4
    count = packing.shape[1]
    return pl.pallas_call(
        land_body,
        out_shape=jax.ShapeDtypeStruct((count, width), bf16),
        grid=(4,),
        in_specs=[
            pl.BlockSpec((PACKED, step), lambda i: (0, i)),
            pl.BlockSpec((step, width), lambda i: (i, 0)),
            fixed((PACKED, width)),
            fixed((1, width)),
            fixed((PACKED, count)),
        ],
        out_specs=fixed((count, width)),
        scratch_shapes=[pltpu.VMEM((PACKED, width), f32)],
        compiler_params=room(),
        cost_estimate=cost(6e9, 14e6),
        name="land",
    )(active, weights, residual, row(bias), packing)


def back_norm(grads, weights, values, gain, added, packing=None):
    width = weights.shape[0]
    step = weights.shape[1] // (4 if len(grads) == 1 else len(grads))
    steps = weights.shape[1] // step
    count = len(grads)

    def body(*refs):
        g_refs, (w_ref, x_ref, gain_ref, add_ref), rest = refs[:count], refs[count : count + 4], refs[count + 4 :]
        sum_ref = rest[-1]
        i = pl.program_id(0)
        for k, g_ref in enumerate(g_refs):

            @pl.when((i == k) if count > 1 else (i >= 0))
            def _(g_ref=g_ref, k=k):
                part = contract_cols(g_ref[...], w_ref[...])

                @pl.when(i == 0)
                def _():
                    sum_ref[...] = part

                @pl.when(i > 0)
                def _():
                    sum_ref[...] += part

        @pl.when(i == steps - 1)
        def _():
            back = sum_ref[...]
            values = x_ref[...]
            centred = values - jnp.mean(values, axis=-1, keepdims=True)
            scale = lax.rsqrt(jnp.mean(centred * centred, axis=-1, keepdims=True) + EPSILON)
            normed = centred * scale
            scaled = back * gain_ref[...]
            inner = jnp.mean(scaled * normed, axis=-1, keepdims=True)
            out = (scaled - jnp.mean(scaled, axis=-1, keepdims=True) - normed * inner) * scale + add_ref[...].astype(f32)
            low = out.astype(bf16)
            if packing is None:
                out_ref, low_ref, sums_ref = rest[:3]
                out_ref[...] = out
                low_ref[...] = low
            else:
                p_ref, low_ref, sums_ref = rest[:3]
                low_ref[...] = contract_rows(p_ref[...], low).astype(bf16)
            sums = [jnp.sum(a, axis=0, keepdims=True) for a in (back * normed, back, low.astype(f32))]
            sums_ref[...] = jnp.concatenate(sums + [jnp.zeros((5, width), f32)], axis=0)

    full = fixed((PACKED, width))
    if packing is None:
        shapes = [jax.ShapeDtypeStruct((PACKED, width), f32), jax.ShapeDtypeStruct((PACKED, width), bf16)]
        out_specs, more_specs, more = [full, full], [], []
    else:
        shapes = [jax.ShapeDtypeStruct((packing.shape[1], width), bf16)]
        out_specs, more_specs, more = [fixed(shapes[0].shape)], [fixed(packing.shape)], [packing]
    g_spec = fixed((PACKED, step)) if count > 1 else pl.BlockSpec((PACKED, step), lambda i: (0, i))
    return pl.pallas_call(
        body,
        out_shape=shapes + [jax.ShapeDtypeStruct((8, width), f32)],
        grid=(steps,),
        in_specs=[g_spec] * count + [pl.BlockSpec((width, step), lambda i: (0, i)), full, fixed((1, width)), full] + more_specs,
        out_specs=out_specs + [fixed((8, width))],
        scratch_shapes=[pltpu.VMEM((PACKED, width), f32)],
        compiler_params=room(),
        cost_estimate=cost(6e9, 20e6),
        name="back_norm",
    )(*grads, weights, values, row(gain), added, *more)


def back_project_body(g_ref, w_ref, o_ref):
    o_ref[...] = contract_cols(g_ref[...], w_ref[...]).astype(bf16)


def back_project(grads, weights):
    rows, width = weights.shape
    half = rows // 2
    return pl.pallas_call(
        back_project_body,
        out_shape=jax.ShapeDtypeStruct((PACKED, rows), bf16),
        grid=(2,),
        in_specs=[fixed((PACKED, width)), pl.BlockSpec((half, width), lambda i: (i, 0))],
        out_specs=pl.BlockSpec((PACKED, half), lambda i: (0, i)),
        compiler_params=room(),
        cost_estimate=cost(2e9, 5e6),
        name="back_project",
    )(grads, weights)


def layer(ring, tokens, counts, w_qkv, bias_q, bias_v, w_out, bias_out, w_up, bias_up, w_down, bias_down, gain_one, shift_one, gain_two, shift_two, cotangent):
    images, slots, width = tokens.shape
    group = ring.sizes["sz"] * ring.sizes["sc"]
    twins = group // images
    rows = w_qkv.shape[0]
    wide = w_down.shape[0] // rows
    ff = w_up.shape[1]

    slot = lax.broadcasted_iota(jnp.int32, (images, slots, 1), 1)
    marked = jnp.where(slot < counts[:, :, None], tokens, jnp.asarray(ABSENT, bf16))

    def back_pieces(pieces, own):
        pieces = jnp.stack([own] + [pieces[k] for k in everything])
        return pieces[:, 0], ring.swap(pieces[:, 1])

    def slots_of(array):
        return array.reshape(depth, 2, slots, width)

    depth = ring.sizes["sz"]
    outer = [k for k in range(1, depth) if k in (1, depth - 1)]
    inner = [k for k in range(1, depth) if k not in outer]
    everything = list(range(1, depth))

    small = [bias_q, bias_v, bias_out, bias_down, gain_one, shift_one, gain_two, shift_two]

    def arrays_of(sources):
        return [source[0] for source in sources]

    def with_arrays(sources, arrays):
        return [(array,) + source[1:] for array, source in zip(arrays, sources)]

    one = seed(w_qkv, small, bias_up)
    column = ring.spread(one, everything)
    stay, go = ring.blocks_for(marked, twins)
    came = ring.swap(go)
    cot_stay, go = ring.blocks_for(cotangent, twins)
    cot_came = ring.swap(go)
    one = ring.along(one, column)
    two = jnp.concatenate([w_out, w_up], axis=1)
    one, two, stay, came, cot_stay, cot_came = tie(one, two, stay, came, cot_stay, cot_came)

    one = ring.across(one)
    column = ring.spread(two, outer)
    pieces = ring.paired(stay, came)
    cot_pieces = ring.paired(cot_stay, cot_came)
    one_near = ring.flat([[half] for half in one])
    target = ring.target(width)
    one, one_near, two, column, pieces, cot_pieces, target = tie(one, one_near, two, column, pieces, cot_pieces, target)

    one_more = ring.plane(one)
    one_core = ring.swap(one_near)
    rest = ring.send(pieces, outer[:1])
    column.update(ring.spread(two, inner))
    two = ring.along(two, column)
    one_near, one_more, one_core, two, pieces, rest, cot_pieces = tie(one_near, one_more, one_core, two, pieces, rest, cot_pieces)

    one_more_core = ring.to_core(one_more)
    two = ring.across(two)
    rest.update(ring.send(pieces, outer[1:]))
    one_near, one_more, one_core, one_more_core, two, pieces, rest, three = tie(
        one_near, one_more, one_core, one_more_core, two, pieces, rest, w_down
    )

    two_core = ring.to_core([[half] for half in two])
    two_more = ring.plane(two)
    rest.update(ring.send(pieces, inner))
    full_qkv, vectors = ring.assemble(ring.near_flat_sources(one_near, one_core, one_more, one_more_core), [3 * width, SMALL])
    two, two_core, two_more, rest, full_qkv, vectors, three = tie(two, two_core, two_more, rest, full_qkv, vectors, three)

    column = ring.spread(three, everything)
    two_more_core = ring.to_core(two_more)
    image_slots = jnp.concatenate([pieces[0]] + [rest[k] for k in everything]).reshape(group * slots, width)
    vectors = vectors.reshape(ring.count, rows, SMALL).astype(f32)
    bu = vectors[:, 0, 128 : 128 + wide * rows].reshape(ff)
    bq, bv, bo, bd, g1, s1, g2, s2 = [vectors[:, k, :rows].reshape(width) for k in range(8)]
    here = (image_slots[:, :1].astype(f32) < 0.5 * ABSENT).reshape(group, slots)
    held = jnp.sum(here.astype(f32), axis=1)
    before = jnp.sum(jnp.where(np.tril(np.ones((group, group), bool), -1), held[None, :], 0.0), axis=1)
    rank = before[:, None] + lax.broadcasted_iota(jnp.int32, (group, slots), 1).astype(f32)
    rank = jnp.where(here, rank, -1.0).reshape(1, group * slots).astype(jnp.int32)
    packing = (rank == lax.broadcasted_iota(jnp.int32, (PACKED, group * slots), 0)).astype(bf16)
    tokens_f, normed = pack_norm(packing, image_slots, g1, s1)
    qkv_bias = halved(jnp.concatenate([bq, jnp.zeros((width,), f32), bv]))
    qkv = project(normed, full_qkv, qkv_bias)
    mixed, logs = attend(qkv)
    three = ring.along(three, column)
    two_more_core, three, mixed = tie(two_more_core, three, mixed)

    three = ring.across(three)
    cot_rest = ring.send(cot_pieces, outer)
    full_out, full_up = ring.assemble(ring.sources(two, two_core, two_more, two_more_core), [width, ff])
    residual, normed_two = out_norm(mixed, full_out, tokens_f, bo, g2, s2)
    normed_far = ring.by_distance(normed, target)
    three, normed_two, normed_far, cot_rest = tie(three, normed_two, normed_far, cot_rest)

    three_more = ring.plane(three)
    three_core = ring.to_core([[half] for half in three])
    cot_rest.update(ring.send(cot_pieces, inner))
    ranks = ring.far(lax.broadcasted_iota(jnp.int32, (ring.count,), 0))
    active, slope, active_far = rise(normed_two, full_up, bu, ranks)
    if active_far is None:
        active_far = ring.by_distance(active, ring.target(ff))
    mixed_far = ring.by_distance(mixed, target)
    two_far = ring.by_distance(normed_two, target)
    three, three_more, three_core, active, active_far, mixed_far, two_far, cot_rest = tie(
        three, three_more, three_core, active, active_far, mixed_far, two_far, cot_rest
    )

    three_more_core = ring.to_core(three_more)
    share = (lax.axis_index(("sz", "sc")) % twins == 0).astype(f32) if twins > 1 else None
    cot_slots = jnp.concatenate([cot_pieces[0]] + [cot_rest[k] for k in everything]).reshape(group * slots, width)
    grad_low, grad_bd = pack(packing, cot_slots)
    sent = weight_grad(active_far, 1, grad_low, share)
    three_more_core, sent, grad_low = tie(three_more_core, sent, grad_low)

    d = ring.swap(sent)
    (full_down,) = ring.assemble(ring.sources(three, three_core, three_more, three_more_core), [width])
    d, full_down = tie(d, full_down)

    d = ring.kept(active_far, grad_low, share, d)
    result = slots_of(land(active, full_down, residual, bd, packing))
    d, result = tie(d, result)

    d = ring.first(d)
    back = ring.send(result, outer, -1)
    hidden_low, grad_bu = fall(grad_low, full_down, slope)
    sent = weight_grad(two_far, 1, hidden_low, share)
    d, sent, back = tie(d, sent, back)

    d = ring.again(d)
    d, sent = tie(d, sent)

    d = ring.second(d)
    u = ring.swap(sent)
    back.update(ring.send(result, inner, -1))
    grad_residual, residual_low, sums_two = back_norm([hidden_low], full_up, residual, g2, grad_low)
    d, u, residual_low, back = tie(d, u, residual_low, back)

    d = ring.last(d)
    u = ring.kept(two_far, hidden_low, share, u)
    sent = weight_grad(mixed_far, 1, residual_low, share)
    d, u, sent, residual_low = tie(d, u, sent, residual_low)

    u = ring.first(u)
    gone = ring.toward_some(d, outer)
    grad_mixed = back_project(residual_low, full_out)
    sent_out = sent
    half_grads = attend_back(qkv, logs, grad_mixed)
    u, sent_out, d, gone, grad_mixed, half_grads = tie(u, sent_out, d, gone, grad_mixed, half_grads)

    u = ring.again(u)
    u, sent_out, back, d, grad_mixed, half_grads = tie(u, sent_out, back, d, grad_mixed, half_grads)

    u = ring.second(u)
    gone.update(ring.toward_some(d, inner))
    o = ring.swap(sent_out)
    grads, grad_sums = attend_back(qkv, logs, grad_mixed, half_grads)
    sent = weight_grad(normed_far, 1, grads, share)
    u, o, sent, grads, back, d, gone = tie(u, o, sent, grads, back, d, gone)
    d = [d[0]] + [gone[k] for k in everything]

    u = ring.last(u)
    u, sent, grads = tie(u, sent, grads)

    later = ring.toward_some(u, outer)
    q = ring.swap(sent)
    grad_tokens, sums_one = back_norm([grads], full_qkv, tokens_f, g1, grad_residual, packing)
    grad_tokens = slots_of(grad_tokens)
    u, later, o, q, grads, grad_tokens, sums_one, back, d = tie(u, later, o, q, grads, grad_tokens, sums_one, back, d)

    sent_back = ring.send(grad_tokens, outer, -1)
    q = ring.kept(normed_far, grads, share, q)
    o = ring.reshaped(weight_grad(mixed_far, 0, residual_low, share, o))
    joined_sum = whole(grad_sums[0])
    grad_bq, grad_bv = joined_sum[:width], joined_sum[2 * width :]
    small = [grad_bq, grad_bv, sums_two[2], grad_bd, sums_one[0], sums_one[1], sums_two[0], sums_two[1]]
    small = [array.reshape(ring.count, rows) for array in small] + [grad_bu.reshape(ring.count, wide * rows)]
    small = jnp.concatenate(small, axis=1)
    small = (small if share is None else small * share).astype(bf16)
    near_first = (ranks[None, :] == lax.broadcasted_iota(jnp.int32, (ring.count, 1), 0)).astype(bf16)
    small = dot_float(near_first, small).astype(bf16)
    small = jnp.pad(small, ((0, 0), (0, rows * SMALL - small.shape[1]))).reshape(2, ring.count // 2 * rows, SMALL)
    q, o, small, u, sent_back, grad_tokens, back, d = tie(q, o, small, u, sent_back, grad_tokens, back, d)

    q = ring.first(q)
    sent_back.update(ring.send(grad_tokens, inner, -1))
    came = ring.swap(small[1])
    own = jnp.stack([result[0]] + [back[k] for k in everything])
    other = ring.swap(own[:, 1])
    q, came, sent_back, u, back, d, own, other = tie(q, came, sent_back, u, back, d, own, other)

    q = ring.again(q)
    small = ring.reshaped(total([small[0], came]).astype(bf16))
    o = ring.ready(jnp.concatenate([o, small], axis=-1))
    q, o, u, own, d = tie(q, o, u, own, d)

    q = ring.second(q)
    o = ring.first(o)
    later.update(ring.toward_some(u, inner))
    result = ring.images_of(own[:, 0], other, images, twins)
    result = jnp.where(slot < counts[:, :, None], result, jnp.asarray(0, bf16))
    o, later, result, q, d = tie(o, later, result, q, d)

    q = ring.last(q)
    o = ring.again(o)
    o, q, d = tie(o, q, d)

    q = ring.third(q)
    o = ring.second(o)
    u = [u[0]] + [later[k] for k in everything]
    grad_tokens, came = back_pieces(sent_back, grad_tokens[0])
    q, o, grad_tokens, came = tie(q, o, grad_tokens, came)

    o = ring.third(ring.last(o))
    grad_tokens = ring.images_of(grad_tokens, came, images, twins).astype(f32)

    sum_down, sum_up = total(d), total(u)
    o = total(o)
    sum_out = o[:, :width]
    sum_qkv = whole(total(q))
    small = o[:, width:].reshape(rows * SMALL)
    sum_bq, sum_bv, sum_bo, sum_bd, sum_g1, sum_s1, sum_g2, sum_s2 = [small[k * rows : (k + 1) * rows] for k in range(8)]
    sum_bu = small[8 * rows : (8 + wide) * rows]
    return (result, grad_tokens, sum_qkv, sum_bq, sum_bv, sum_out, sum_bo, sum_up, sum_bu, sum_down, sum_bd, sum_g1, sum_s1, sum_g2, sum_s2)


def solution(mesh):
    n_grp, n_seq = mesh.shape["grp"], mesh.shape["seq"]
    sizes = (n_grp // 2, 2, n_seq // 2, 2)
    fine = Mesh(mesh.devices.reshape(sizes), AXES)
    ring = Ring(sizes)
    grp, seq = AXES[:2], AXES[2:]
    by_token = P(grp, seq, None)
    rows, vec = P(AXES, None), P(AXES)
    in_specs = (by_token, P(grp, seq), rows, vec, vec, rows, vec, rows, vec, rows, vec, vec, vec, vec, vec, by_token)
    out_specs = (by_token, by_token, rows, vec, vec, rows, vec, rows, vec, rows, vec, vec, vec, vec, vec)

    def shards(*args):
        return layer(ring, *args)

    return jax.shard_map(shards, mesh=fine, in_specs=in_specs, out_specs=out_specs, check_vma=False)
```

```python
import jax
import jax.numpy as jnp
import numpy as np
from jax import lax
from jax.experimental import pallas as pl
from jax.experimental.pallas import tpu as pltpu
from jax.sharding import Mesh
from jax.sharding import PartitionSpec as P

H = 16
HD = 64
LENGTH = 577
PACKED = 592
EPSILON = 1e-06
NEGATIVE = -1e30
ABSENT = 100.0
SMALL = 256
AXES = ("gy", "gx", "sz", "sc")
ORDERS = (("gx", "gy"), ("gy", "gx"))

bf16 = jnp.bfloat16
f32 = jnp.float32


def norm_rows(values, gain_vec, shift_vec):
    row_mean = jnp.mean(values, axis=-1, keepdims=True)
    centred = values - row_mean
    row_var = jnp.mean(centred * centred, axis=-1, keepdims=True)
    return centred * lax.rsqrt(row_var + EPSILON) * gain_vec + shift_vec


def dot_float(left, right):
    return jnp.dot(left, right, preferred_element_type=f32)


def contract_rows(left, right):
    return lax.dot_general(left, right, (((0,), (0,)), ((), ())), preferred_element_type=f32)


def contract_cols(left, right):
    return lax.dot_general(left, right, (((1,), (1,)), ((), ())), preferred_element_type=f32)


def room(mib=50):
    return pltpu.CompilerParams(vmem_limit_bytes=mib * 2**20)


HINT = 0.02


def cost(flops, bytes_accessed, transcendentals=0):
    return pl.CostEstimate(
        flops=int(HINT * flops), bytes_accessed=int(HINT * bytes_accessed), transcendentals=int(HINT * transcendentals)
    )


def shifted(array, axis, size, step):
    return lax.ppermute(array, axis, [(i, (i + step) % size) for i in range(size)])


def pick(array, index, axis):
    return lax.dynamic_index_in_dim(array, index, axis, keepdims=False)


class Ring:
    def __init__(self, sizes):
        self.sizes = dict(zip(AXES, sizes))
        self.count = int(np.prod(sizes))

    def place(self):
        return {axis: lax.axis_index(axis) for axis in AXES}

    def others(self, array, axis):
        size = self.sizes[axis]
        return [shifted(array, axis, size, step) for step in range(1, size)]

    def others_from(self, array, axis, steps):
        size = self.sizes[axis]
        return [shifted(array, axis, size, step) for step in steps]

    def along(self, shard, columns):
        cut = shard.shape[0] // 2
        size = self.sizes["sz"]
        columns = [shard] + [columns[k] for k in range(1, size)]
        here = lax.axis_index("sz")
        ordered = [lax.select_n((here - k) % size, *columns) if size > 2 else jnp.where(here == k, *columns) for k in range(size)]
        return [jnp.stack([c[:cut] for c in ordered]), jnp.stack([c[cut:] for c in ordered])]

    def spread(self, shard, steps):
        return {k: shifted(shard, "sz", self.sizes["sz"], k) for k in steps}

    def across(self, halves):
        return [jnp.stack([half] + self.others(half, order[0])) for half, order in zip(halves, ORDERS)]

    def plane(self, halves):
        return [self.others(half, order[1]) for half, order in zip(halves, ORDERS)]

    def to_core(self, groups):
        return [[shifted(group, "sc", 2, 1) for group in part] for part in groups]

    def sources(self, first, traded_first, second, traded_second):
        found = []
        for part in range(2):
            kinds = ([first[part]] + second[part], traded_first[part] + traded_second[part])
            for turn, groups in enumerate(kinds):
                found += [(g, turn, [(part, step, one) for one in range(g.shape[0])]) for step, g in enumerate(groups)]
        return found

    def flat(self, groups):
        return jnp.concatenate([group for part in groups for group in part], axis=0)

    def labels(self, far):
        sizes = self.sizes
        found = []
        for part in range(2):
            for step in range(1, sizes[ORDERS[part][1]]) if far else [0]:
                found += [(part, step, one) for one in range(sizes[ORDERS[part][0]])]
        return found

    def near_flat_sources(self, near, near_core, second, traded_second):
        found = [(near, 0, self.labels(False)), (near_core, 1, self.labels(False))]
        for turn, groups in enumerate((second, traded_second)):
            for part in range(2):
                for step, g in enumerate(groups[part]):
                    found.append((g, turn, [(part, step + 1, one) for one in range(g.shape[0])]))
        return found

    def assemble(self, sources, widths):
        place = self.place()
        sizes = self.sizes
        cut, width = sources[0][0].shape[-2:]
        depth = sizes["sz"]
        planes, kinds, parts, arrays, counts = [], [], [], [], []
        for group, turn, labels in sources:
            arrays.append(group)
            counts.append(len(labels))
            for part, step, one in labels:
                order = ORDERS[part]
                at = {order[1]: (place[order[1]] - step) % sizes[order[1]], order[0]: (place[order[0]] - one) % sizes[order[0]]}
                planes.append(at["gy"] * sizes["gx"] + at["gx"])
                kinds.append((place["sc"] - turn) % 2)
                parts.append(part)
        table = jnp.stack(planes + kinds).astype(jnp.int32)
        many = len(planes)
        starts = np.concatenate([[0], np.cumsum(widths)])

        def body(table_ref, *refs):
            ins = refs[: len(counts)]
            outs = refs[len(counts) : -3]
            held, came, left = refs[-3:]
            arrivals = []
            for ref, count in zip(ins, counts):
                for k in range(count):
                    n = len(arrivals)
                    arrivals.append(pltpu.make_async_copy(ref.at[k], held.at[n], came.at[n]))
            for copy in arrivals:
                copy.start()
            departures = []
            for n, copy in enumerate(arrivals):
                copy.wait()
                for i, out in enumerate(outs):
                    window = held.at[n, :, :, pl.ds(int(starts[i]), widths[i])]
                    target = out.at[table_ref[n], :, table_ref[many + n], parts[n]]
                    leave = pltpu.make_async_copy(window, target, left.at[n, i])
                    leave.start()
                    departures.append(leave)
            for copy in departures:
                copy.wait()

        planes_all = sizes["gy"] * sizes["gx"]
        outs = pl.pallas_call(
            body,
            out_shape=[jax.ShapeDtypeStruct((planes_all, depth, 2, 2, cut, w), bf16) for w in widths],
            grid_spec=pltpu.PrefetchScalarGridSpec(
                num_scalar_prefetch=1,
                grid=(1,),
                in_specs=[pl.BlockSpec(memory_space=pl.ANY)] * len(counts),
                out_specs=[pl.BlockSpec(memory_space=pl.ANY)] * len(widths),
                scratch_shapes=[
                    pltpu.VMEM((many, depth, cut, width), bf16),
                    pltpu.SemaphoreType.DMA((many,)),
                    pltpu.SemaphoreType.DMA((many, len(widths))),
                ],
            ),
            compiler_params=room(),
            cost_estimate=cost(0, 4 * self.count * 2 * cut * width),
            name="assemble",
        )(table, *arrays)
        return [out.reshape(self.count * 2 * cut, w) for out, w in zip(outs, widths)]

    def far(self, device):
        place = self.place()
        sizes = self.sizes
        index, out = device, {}
        for axis in AXES[::-1]:
            out[axis] = (index % sizes[axis] - place[axis]) % sizes[axis]
            index = index // sizes[axis]
        return ((out["sc"] * sizes["gy"] + out["gy"]) * sizes["gx"] + out["gx"]) * sizes["sz"] + out["sz"]

    def target(self, width):
        block = width // self.count
        row = lax.broadcasted_iota(jnp.int32, (width, 1), 0)
        return self.far(row // block) * block + row % block

    def by_distance(self, array, target):
        tokens, width = array.shape
        half = width // 2

        def body(x_ref, t_ref, o_ref):
            columns = lax.broadcasted_iota(jnp.int32, (width, half), 1) + half * pl.program_id(0)
            pick_columns = jnp.where(t_ref[...] == columns, 1.0, 0.0).astype(bf16)
            o_ref[0] = dot_float(x_ref[...], pick_columns).astype(bf16)

        return pl.pallas_call(
            body,
            out_shape=jax.ShapeDtypeStruct((2, tokens, half), bf16),
            grid=(2,),
            in_specs=[pl.BlockSpec((tokens, width), lambda i: (0, 0)), pl.BlockSpec((width, 1), lambda i: (0, 0))],
            out_specs=pl.BlockSpec((1, tokens, half), lambda i: (i, 0, 0)),
            compiler_params=room(),
            cost_estimate=cost(2 * tokens * width * width, 4 * tokens * width),
            name="by_distance",
        )(array, target)

    def blocks_for(self, array, twins):
        place = self.place()
        size = self.sizes["sz"]
        out = []
        for turn in range(2):
            found = [((place["sz"] + k) % size * 2 + (place["sc"] + turn) % 2) // twins for k in range(size)]
            out.append(jnp.stack([pick(array, image, 0) for image in found]))
        return out

    def paired(self, stay, came):
        return [jnp.stack([stay[k], came[k]]) for k in range(self.sizes["sz"])]

    def send(self, pieces, steps, sign=1):
        return {k: shifted(pieces[k], "sz", self.sizes["sz"], sign * k) for k in steps}

    def images_of(self, own, came, images, twins):
        place = self.place()
        size = self.sizes["sz"]
        both = jnp.stack([own, came])
        both = both.reshape((2 * size,) + both.shape[2:])
        out = []
        for image in range(images):
            device = image * twins
            out.append(pick(both, (device % 2 - place["sc"]) % 2 * size + (device // 2 - place["sz"]) % size, 0))
        return jnp.stack(out)

    def swap(self, sent):
        return shifted(sent, "sc", 2, 1)

    def reshaped(self, out):
        sizes = self.sizes
        return out.reshape(sizes["gy"], sizes["gx"], sizes["sz"], out.shape[0] // (self.count // 2), out.shape[1])

    def kept(self, left, right, share, came):
        cut = left.shape[2] // (self.count // 2) // 2
        if cut % 16 == 0:
            return weight_grad(left, 0, right, share, came, self.sizes)
        return self.ready(self.reshaped(weight_grad(left, 0, right, share, came)))

    def toward(self, arrays, axis):
        size = self.sizes[axis]
        return [arrays[0]] + [shifted(arrays[k], axis, size, k) for k in range(1, size)]

    def toward_some(self, parts, steps):
        return {k: shifted(parts[k], "sz", self.sizes["sz"], k) for k in steps}

    def ready(self, sums):
        cut = sums.shape[3] // 2
        upper = [sums[k, :, :, :cut] for k in range(self.sizes["gy"])]
        lower = [sums[:, k, :, cut:] for k in range(self.sizes["gx"])]
        return upper, lower

    def first(self, pair):
        return self.toward(pair[0], "gy"), self.toward(pair[1], "gx")

    def again(self, pair):
        return tuple(
            [total([t[k] for t in terms]).astype(bf16) for k in range(self.sizes[axis])]
            for terms, axis in zip(pair, ("gx", "gy"))
        )

    def second(self, pair):
        return self.toward(pair[0], "gx"), self.toward(pair[1], "gy")

    def last(self, pair):
        return [
            jnp.concatenate([total([t[k] for t in terms]) for terms in pair], axis=0).astype(bf16)
            for k in range(self.sizes["sz"])
        ]

    def third(self, parts):
        return self.toward(parts, "sz")


def weight_grad(left, kind, right, share, came=None, sizes=None):
    tokens, columns = right.shape
    rows = left.shape[2]
    tiled = rows > 512
    parts = 1
    if sizes is not None:
        ny, nx, nz = sizes["gy"], sizes["gx"], sizes["sz"]
        parts = ny * nx
        block = rows // (parts * nz)
        cut = block // 2
    if tiled:
        tall, broad = rows // (parts if sizes is not None else rows // 512), columns
        steps = rows // tall
        at = lambda i: (i, 0)
        left_at, right_at = (lambda i: (kind, 0, i)), (lambda i: (0, 0))
    else:
        tall, broad = rows, next(w for w in (1024, 768, 512, 128) if columns % w == 0)
        steps = columns // broad
        at = lambda i: (0, i)
        left_at, right_at = (lambda i: (kind, 0, 0)), (lambda i: (0, i))
    others = [] if came is None else [came.reshape(rows, columns)]
    if share is not None:
        others.append(share.reshape(1, 1))
    given = 2 + len(others)

    def body(*refs):
        outs = refs[given:]
        out = contract_rows(refs[0][0], refs[1][...])
        if share is not None:
            out = out * refs[given - 1][...]
        if came is not None:
            out = out + refs[2][...].astype(f32)
        if sizes is None:
            outs[0][...] = out.astype(bf16)
        elif tiled:
            i = pl.program_id(0)
            out = out.astype(bf16).reshape(nz, block, broad)
            for k in range(ny):

                @pl.when(i // nx == k)
                def _(k=k):
                    outs[k][0] = out[:, :cut]

            for k in range(nx):

                @pl.when(i % nx == k)
                def _(k=k):
                    outs[ny + k][0] = out[:, cut:]

        else:
            out = out.astype(bf16).reshape(ny, nx, nz, block, broad)
            for k in range(ny):
                outs[k][...] = out[k, :, :, :cut]
            for k in range(nx):
                outs[ny + k][...] = out[:, k, :, cut:]

    specs = [pl.BlockSpec((1, tokens, tall), left_at), pl.BlockSpec((tokens, broad), right_at)]
    if came is not None:
        specs.append(pl.BlockSpec((tall, broad), at))
    if share is not None:
        specs.append(pl.BlockSpec((1, 1), lambda i: (0, 0)))
    if sizes is None:
        shapes, out_specs = [(rows, columns)], [pl.BlockSpec((tall, broad), at)]
    else:
        shapes = [(nx, nz, cut, columns)] * ny + [(ny, nz, cut, columns)] * nx
        if tiled:
            out_specs = [
                pl.BlockSpec((1, nz, cut, broad), lambda i, k=k: (jnp.clip(i - k * nx, 0, nx - 1), 0, 0, 0)) for k in range(ny)
            ]
            out_specs += [pl.BlockSpec((1, nz, cut, broad), lambda i, k=k: (jnp.maximum(i - k, 0) // nx, 0, 0, 0)) for k in range(nx)]
        else:
            out_specs = [pl.BlockSpec(shape[:3] + (broad,), lambda i: (0, 0, 0, i)) for shape in shapes]
    outs = pl.pallas_call(
        body,
        out_shape=[jax.ShapeDtypeStruct(shape, bf16) for shape in shapes],
        grid=(steps,),
        in_specs=specs,
        out_specs=out_specs,
        compiler_params=room(),
        cost_estimate=cost(2 * tokens * rows * columns, 4 * rows * columns),
        name="weight_grad",
    )(left, right, *others)
    return outs[0] if sizes is None else (outs[:ny], outs[ny:])


def total(arrays):
    out = arrays[0].astype(f32)
    for array in arrays[1:]:
        out = out + array.astype(f32)
    return out


def tie(*values):
    return lax.optimization_barrier(values)


def of_head(part):
    return lax.broadcasted_iota(jnp.int32, (1, 2 * HD), 1) // HD == part


def mask_tail(scores, fill):
    start = LENGTH // 8 * 8
    row = lax.broadcasted_iota(jnp.int32, (PACKED - start, PACKED), 0)
    tail = jnp.where(row < LENGTH - start, scores[start:], fill)
    return jnp.concatenate([scores[:start], tail], axis=0)


def flip(array):
    return array.astype(f32).T.astype(bf16)


def attend_body(q_ref, k_ref, v_ref, o_ref, l_ref):
    query, key = q_ref[...] * jnp.asarray(HD**-0.5, bf16), k_ref[...]
    value_t = flip(v_ref[...])
    mixed, logs = [], []
    for part in range(2):
        scores = contract_cols(jnp.where(of_head(part), key, 0), query)
        scores = mask_tail(scores, NEGATIVE)
        top = jnp.max(scores, axis=0, keepdims=True)
        exponent = jnp.exp(scores - top)
        total = jnp.sum(exponent, axis=0, keepdims=True)
        out = dot_float(value_t[HD * part : HD * (part + 1)], exponent.astype(bf16))
        mixed.append(out * (1.0 / total))
        logs.append(top + jnp.log(total))
    o_ref[...] = jnp.concatenate(mixed, axis=0).T.astype(bf16)
    l_ref[...] = jnp.concatenate(logs + [jnp.zeros((6, PACKED), f32)], axis=0)


PAIR = (PACKED, 2 * HD)
PAIRS = H // 2
CUT = PAIRS // 2


def kind_spec(kind, base=0):
    return pl.BlockSpec(PAIR, lambda i: (0, (i + base) // CUT * 3 * CUT + (i + base) % CUT + kind * CUT))


def pair_spec(base=0):
    return pl.BlockSpec(PAIR, lambda i: (0, i + base))


def log_spec(base=0):
    return pl.BlockSpec((8, PACKED), lambda i: (i + base, 0))


def halved(array):
    return array.reshape(-1, 3, 2, H * HD // 2).swapaxes(1, 2).reshape(array.shape)


def whole(array):
    return array.reshape(-1, 2, 3, H * HD // 2).swapaxes(1, 2).reshape(array.shape)


def attend(qkv):
    return pl.pallas_call(
        attend_body,
        out_shape=[
            jax.ShapeDtypeStruct((PACKED, H * HD), bf16),
            jax.ShapeDtypeStruct((8 * PAIRS, PACKED), f32),
        ],
        grid=(PAIRS,),
        in_specs=[kind_spec(0), kind_spec(1), kind_spec(2)],
        out_specs=[pair_spec(), log_spec()],
        compiler_params=room(),
        cost_estimate=cost(12e9, 8 * qkv.size, PACKED * PACKED * H),
        name="attend",
    )(qkv, qkv, qkv)


def attend_back_body(q_ref, k_ref, v_ref, l_ref, g_ref, *rest):
    d_ref, s_ref = rest[-2:]
    base = 0
    if len(rest) == 4:
        base = rest[0].shape[1]

        @pl.when(pl.program_id(0) == 0)
        def _():
            d_ref[:, :base] = rest[0][...]
            s_ref[:, :base] = rest[1][...]

    scale = jnp.asarray(HD**-0.5, bf16)
    query, key, value, grad = q_ref[...] * scale, k_ref[...], v_ref[...], g_ref[...]
    key_t = flip(key)
    grad_query, grad_key, grad_value = [], [], []
    for part in range(2):
        mask = of_head(part)
        scores = contract_cols(jnp.where(mask, key, 0), query)
        soft = mask_tail(jnp.exp(scores - l_ref[part : part + 1]), 0.0)
        grad_soft = contract_cols(jnp.where(mask, value, 0), grad)
        delta = jnp.sum(soft * grad_soft, axis=0, keepdims=True)
        grad_scores = (soft * (grad_soft - delta)).astype(bf16)
        grad_value.append(dot_float(soft.astype(bf16), grad))
        grad_key.append(dot_float(grad_scores, query))
        grad_query.append(dot_float(key_t[HD * part : HD * (part + 1)], grad_scores))
    first = of_head(0)
    grads = (
        jnp.concatenate(grad_query, axis=0).T * HD**-0.5,
        jnp.where(first, grad_key[0], grad_key[1]),
        jnp.where(first, grad_value[0], grad_value[1]),
    )
    for kind, array in enumerate(grads):
        start = pl.multiple_of(base + (pl.program_id(0) + kind * CUT) * 2 * HD, 2 * HD)
        low = array.astype(bf16)
        d_ref[:, pl.ds(start, 2 * HD)] = low
        s_ref[:, pl.ds(start, 2 * HD)] = jnp.sum(low.astype(f32), axis=0, keepdims=True)


def attend_back(qkv, logs, grad_mixed, before=()):
    base = CUT if before else 0
    width = qkv.shape[1] // (1 if before else 2)
    return pl.pallas_call(
        attend_back_body,
        out_shape=[jax.ShapeDtypeStruct((PACKED, width), bf16), jax.ShapeDtypeStruct((1, width), f32)],
        grid=(CUT,),
        in_specs=[kind_spec(0, base), kind_spec(1, base), kind_spec(2, base), log_spec(base), pair_spec(base)]
        + [pl.BlockSpec(array.shape, lambda i: (0, 0)) for array in before],
        out_specs=[pl.BlockSpec((PACKED, width), lambda i: (0, 0)), pl.BlockSpec((1, width), lambda i: (0, 0))],
        compiler_params=room(),
        cost_estimate=cost(12e9, 8 * qkv.size, PACKED * PACKED * H // 2),
        name="attend_back",
    )(qkv, qkv, qkv, logs, grad_mixed, *before)


def rise(normed, weights, bias, ranks):
    width, ff = weights.shape
    step = ff // 4
    count = ranks.shape[0]
    block = ff // count
    inside = step // block
    whole_tiles = block % 128 == 0

    def body(rank_ref, x_ref, w_ref, b_ref, active_ref, slope_ref, *rest):
        i = pl.program_id(0)
        hidden = dot_float(x_ref[...], w_ref[...]) + b_ref[...]
        share = 0.5 * (1.0 + lax.erf(hidden * np.float32(np.sqrt(0.5))))
        active = (hidden * share).astype(bf16)
        active_ref[...] = active
        bell = jnp.exp(hidden * hidden * -0.5) * np.float32(1.0 / np.sqrt(2.0 * np.pi))
        slope_ref[...] = share + hidden * bell
        if not whole_tiles:
            return
        far_ref, held, sems = rest
        held[i % 2] = active

        def copies(turn):
            out = []
            for k in range(inside):
                rank = rank_ref[turn * inside + k]
                start = pl.multiple_of(rank % (count // 2) * block, block)
                window = held.at[turn % 2, :, pl.ds(k * block, block)]
                out.append(pltpu.make_async_copy(window, far_ref.at[rank // (count // 2), :, pl.ds(start, block)], sems.at[turn % 2, k]))
            return out

        for copy in copies(i):
            copy.start()

        @pl.when(i > 0)
        def _():
            for copy in copies(i - 1):
                copy.wait()

        @pl.when(i == 3)
        def _():
            for copy in copies(i):
                copy.wait()

    shapes = [jax.ShapeDtypeStruct((PACKED, ff), bf16), jax.ShapeDtypeStruct((PACKED, ff), f32)]
    specs = [pl.BlockSpec((PACKED, step), lambda i, t: (0, i))] * 2
    scratch = []
    if whole_tiles:
        shapes.append(jax.ShapeDtypeStruct((2, PACKED, ff // 2), bf16))
        specs.append(pl.BlockSpec(memory_space=pl.ANY))
        scratch = [pltpu.VMEM((2, PACKED, step), bf16), pltpu.SemaphoreType.DMA((2, inside))]
    outs = pl.pallas_call(
        body,
        out_shape=shapes,
        grid_spec=pltpu.PrefetchScalarGridSpec(
            num_scalar_prefetch=1,
            grid=(4,),
            in_specs=[
                pl.BlockSpec((PACKED, width), lambda i, t: (0, 0)),
                pl.BlockSpec((width, step), lambda i, t: (0, i)),
                pl.BlockSpec((1, step), lambda i, t: (0, i)),
            ],
            out_specs=specs,
            scratch_shapes=scratch,
        ),
        compiler_params=room(),
        cost_estimate=cost(12e9, 30e6, PACKED * ff * 2),
        name="rise",
    )(ranks, normed, weights, bias.reshape(1, ff))
    return outs if whole_tiles else (outs[0], outs[1], None)


def fall_body(g_ref, w_ref, slope_ref, out_ref, sum_ref):
    grad = (contract_cols(g_ref[...], w_ref[...]) * slope_ref[...]).astype(bf16)
    out_ref[...] = grad
    sum_ref[...] = jnp.sum(grad.astype(f32), axis=0, keepdims=True)


def fall(grads, weights, slope):
    ff, width = weights.shape
    step = ff // 4
    return pl.pallas_call(
        fall_body,
        out_shape=[jax.ShapeDtypeStruct((PACKED, ff), bf16), jax.ShapeDtypeStruct((1, ff), f32)],
        grid=(4,),
        in_specs=[
            pl.BlockSpec((PACKED, width), lambda i: (0, 0)),
            pl.BlockSpec((step, width), lambda i: (i, 0)),
            pl.BlockSpec((PACKED, step), lambda i: (0, i)),
        ],
        out_specs=[pl.BlockSpec((PACKED, step), lambda i: (0, i)), pl.BlockSpec((1, step), lambda i: (0, i))],
        compiler_params=room(),
        cost_estimate=cost(10e9, 25e6),
        name="fall",
    )(grads, weights, slope)


def project_body(x_ref, w_ref, b_ref, out_ref):
    out_ref[...] = (dot_float(x_ref[...], w_ref[...]) + b_ref[...]).astype(bf16)


def project(left, weights, bias):
    width, columns = weights.shape
    step = columns // 3
    return pl.pallas_call(
        project_body,
        out_shape=jax.ShapeDtypeStruct((PACKED, columns), bf16),
        grid=(3,),
        in_specs=[
            pl.BlockSpec((PACKED, width), lambda i: (0, 0)),
            pl.BlockSpec((width, step), lambda i: (0, i)),
            pl.BlockSpec((1, step), lambda i: (0, i)),
        ],
        out_specs=pl.BlockSpec((PACKED, step), lambda i: (0, i)),
        compiler_params=room(),
        cost_estimate=cost(6e9, 12e6),
        name="project",
    )(left, weights, bias.reshape(1, columns))


def row(vector):
    return vector.reshape(1, -1)


def fixed(shape):
    return pl.BlockSpec(shape, lambda i: (0,) * len(shape))


def seed(weights, vectors, long):
    rows, width = weights.shape
    half = width // 6

    def body(w_ref, *refs):
        out_ref = refs[-1]
        for k in range(6):
            out_ref[:, k * half : (k + 1) * half] = w_ref[:, pl.ds((k % 3 * 2 + k // 3) * half, half)]
        out_ref[:, width:] = jnp.zeros((rows, SMALL), bf16)
        for k in range(len(vectors)):
            out_ref[k : k + 1, width : width + rows] = refs[k][...]
        out_ref[0:1, width + 128 : width + 128 + long.shape[0]] = refs[len(vectors)][...]

    return pl.pallas_call(
        body,
        out_shape=jax.ShapeDtypeStruct((rows, width + SMALL), bf16),
        cost_estimate=cost(0, 1e6),
        name="seed",
    )(weights, *[row(v) for v in vectors], row(long))


def pack_norm_body(p_ref, x_ref, g_ref, s_ref, t_ref, n_ref):
    tokens = dot_float(p_ref[...], x_ref[...])
    t_ref[...] = tokens
    n_ref[...] = norm_rows(tokens, g_ref[...], s_ref[...]).astype(bf16)


def pack_norm(packing, slots, gain, shift):
    count, width = slots.shape
    half = PACKED // 2
    by_row = pl.BlockSpec((half, width), lambda i: (i, 0))
    return pl.pallas_call(
        pack_norm_body,
        out_shape=[jax.ShapeDtypeStruct((PACKED, width), f32), jax.ShapeDtypeStruct((PACKED, width), bf16)],
        grid=(2,),
        in_specs=[pl.BlockSpec((half, count), lambda i: (i, 0)), fixed((count, width)), fixed((1, width)), fixed((1, width))],
        out_specs=[by_row, by_row],
        compiler_params=room(),
        cost_estimate=cost(1e9, 8e6),
        name="pack_norm",
    )(packing, slots, row(gain), row(shift))


def pack_body(p_ref, x_ref, o_ref, s_ref):
    low = dot_float(p_ref[...], x_ref[...]).astype(bf16)
    o_ref[...] = low
    s_ref[...] = jnp.sum(low.astype(f32), axis=0, keepdims=True)


def pack(packing, slots):
    count, width = slots.shape
    half = width // 2
    return pl.pallas_call(
        pack_body,
        out_shape=[jax.ShapeDtypeStruct((PACKED, width), bf16), jax.ShapeDtypeStruct((1, width), f32)],
        grid=(2,),
        in_specs=[fixed((PACKED, count)), pl.BlockSpec((count, half), lambda i: (0, i))],
        out_specs=[pl.BlockSpec((PACKED, half), lambda i: (0, i)), pl.BlockSpec((1, half), lambda i: (0, i))],
        compiler_params=room(),
        cost_estimate=cost(1e9, 4e6),
        name="pack",
    )(packing, slots)


def out_norm_body(m_ref, w_ref, t_ref, b_ref, g_ref, s_ref, r_ref, n_ref):
    residual = t_ref[...] + dot_float(m_ref[...], w_ref[...]) + b_ref[...]
    r_ref[...] = residual
    n_ref[...] = norm_rows(residual, g_ref[...], s_ref[...]).astype(bf16)


def out_norm(mixed, weights, tokens, bias, gain, shift):
    width = weights.shape[1]
    half = PACKED // 2
    by_row = pl.BlockSpec((half, width), lambda i: (i, 0))
    vec = fixed((1, width))
    return pl.pallas_call(
        out_norm_body,
        out_shape=[jax.ShapeDtypeStruct((PACKED, width), f32), jax.ShapeDtypeStruct((PACKED, width), bf16)],
        grid=(2,),
        in_specs=[by_row, fixed(weights.shape), by_row, vec, vec, vec],
        out_specs=[by_row, by_row],
        compiler_params=room(),
        cost_estimate=cost(2e9, 8e6),
        name="out_norm",
    )(mixed, weights, tokens, row(bias), row(gain), row(shift))


def land_body(a_ref, w_ref, r_ref, b_ref, p_ref, o_ref, sum_ref):
    i = pl.program_id(0)
    part = dot_float(a_ref[...], w_ref[...])

    @pl.when(i == 0)
    def _():
        sum_ref[...] = part + r_ref[...] + b_ref[...]

    @pl.when(i > 0)
    def _():
        sum_ref[...] += part

    @pl.when(i == pl.num_programs(0) - 1)
    def _():
        o_ref[...] = contract_rows(p_ref[...], sum_ref[...].astype(bf16)).astype(bf16)


def land(active, weights, residual, bias, packing):
    ff, width = weights.shape
    step = ff // 4
    count = packing.shape[1]
    return pl.pallas_call(
        land_body,
        out_shape=jax.ShapeDtypeStruct((count, width), bf16),
        grid=(4,),
        in_specs=[
            pl.BlockSpec((PACKED, step), lambda i: (0, i)),
            pl.BlockSpec((step, width), lambda i: (i, 0)),
            fixed((PACKED, width)),
            fixed((1, width)),
            fixed((PACKED, count)),
        ],
        out_specs=fixed((count, width)),
        scratch_shapes=[pltpu.VMEM((PACKED, width), f32)],
        compiler_params=room(),
        cost_estimate=cost(6e9, 14e6),
        name="land",
    )(active, weights, residual, row(bias), packing)


def back_norm(grads, weights, values, gain, added, packing=None):
    width = weights.shape[0]
    step = weights.shape[1] // (4 if len(grads) == 1 else len(grads))
    steps = weights.shape[1] // step
    count = len(grads)

    def body(*refs):
        g_refs, (w_ref, x_ref, gain_ref, add_ref), rest = refs[:count], refs[count : count + 4], refs[count + 4 :]
        sum_ref = rest[-1]
        i = pl.program_id(0)
        for k, g_ref in enumerate(g_refs):

            @pl.when((i == k) if count > 1 else (i >= 0))
            def _(g_ref=g_ref, k=k):
                part = contract_cols(g_ref[...], w_ref[...])

                @pl.when(i == 0)
                def _():
                    sum_ref[...] = part

                @pl.when(i > 0)
                def _():
                    sum_ref[...] += part

        @pl.when(i == steps - 1)
        def _():
            back = sum_ref[...]
            values = x_ref[...]
            centred = values - jnp.mean(values, axis=-1, keepdims=True)
            scale = lax.rsqrt(jnp.mean(centred * centred, axis=-1, keepdims=True) + EPSILON)
            normed = centred * scale
            scaled = back * gain_ref[...]
            inner = jnp.mean(scaled * normed, axis=-1, keepdims=True)
            out = (scaled - jnp.mean(scaled, axis=-1, keepdims=True) - normed * inner) * scale + add_ref[...].astype(f32)
            low = out.astype(bf16)
            if packing is None:
                out_ref, low_ref, sums_ref = rest[:3]
                out_ref[...] = out
                low_ref[...] = low
            else:
                p_ref, low_ref, sums_ref = rest[:3]
                low_ref[...] = contract_rows(p_ref[...], low).astype(bf16)
            sums = [jnp.sum(a, axis=0, keepdims=True) for a in (back * normed, back, low.astype(f32))]
            sums_ref[...] = jnp.concatenate(sums + [jnp.zeros((5, width), f32)], axis=0)

    full = fixed((PACKED, width))
    if packing is None:
        shapes = [jax.ShapeDtypeStruct((PACKED, width), f32), jax.ShapeDtypeStruct((PACKED, width), bf16)]
        out_specs, more_specs, more = [full, full], [], []
    else:
        shapes = [jax.ShapeDtypeStruct((packing.shape[1], width), bf16)]
        out_specs, more_specs, more = [fixed(shapes[0].shape)], [fixed(packing.shape)], [packing]
    g_spec = fixed((PACKED, step)) if count > 1 else pl.BlockSpec((PACKED, step), lambda i: (0, i))
    return pl.pallas_call(
        body,
        out_shape=shapes + [jax.ShapeDtypeStruct((8, width), f32)],
        grid=(steps,),
        in_specs=[g_spec] * count + [pl.BlockSpec((width, step), lambda i: (0, i)), full, fixed((1, width)), full] + more_specs,
        out_specs=out_specs + [fixed((8, width))],
        scratch_shapes=[pltpu.VMEM((PACKED, width), f32)],
        compiler_params=room(),
        cost_estimate=cost(6e9, 20e6),
        name="back_norm",
    )(*grads, weights, values, row(gain), added, *more)


def back_project_body(g_ref, w_ref, o_ref):
    o_ref[...] = contract_cols(g_ref[...], w_ref[...]).astype(bf16)


def back_project(grads, weights):
    rows, width = weights.shape
    half = rows // 2
    return pl.pallas_call(
        back_project_body,
        out_shape=jax.ShapeDtypeStruct((PACKED, rows), bf16),
        grid=(2,),
        in_specs=[fixed((PACKED, width)), pl.BlockSpec((half, width), lambda i: (i, 0))],
        out_specs=pl.BlockSpec((PACKED, half), lambda i: (0, i)),
        compiler_params=room(),
        cost_estimate=cost(2e9, 5e6),
        name="back_project",
    )(grads, weights)


def layer(ring, tokens, counts, w_qkv, bias_q, bias_v, w_out, bias_out, w_up, bias_up, w_down, bias_down, gain_one, shift_one, gain_two, shift_two, cotangent):
    images, slots, width = tokens.shape
    group = ring.sizes["sz"] * ring.sizes["sc"]
    twins = group // images
    rows = w_qkv.shape[0]
    wide = w_down.shape[0] // rows
    ff = w_up.shape[1]

    slot = lax.broadcasted_iota(jnp.int32, (images, slots, 1), 1)
    marked = jnp.where(slot < counts[:, :, None], tokens, jnp.asarray(ABSENT, bf16))

    def back_pieces(pieces, own):
        pieces = jnp.stack([own] + [pieces[k] for k in everything])
        return pieces[:, 0], ring.swap(pieces[:, 1])

    def slots_of(array):
        return array.reshape(depth, 2, slots, width)

    depth = ring.sizes["sz"]
    outer = [k for k in range(1, depth) if k in (1, depth - 1)]
    inner = [k for k in range(1, depth) if k not in outer]
    everything = list(range(1, depth))

    small = [bias_q, bias_v, bias_out, bias_down, gain_one, shift_one, gain_two, shift_two]

    def arrays_of(sources):
        return [source[0] for source in sources]

    def with_arrays(sources, arrays):
        return [(array,) + source[1:] for array, source in zip(arrays, sources)]

    one = seed(w_qkv, small, bias_up)
    column = ring.spread(one, everything)
    stay, go = ring.blocks_for(marked, twins)
    came = ring.swap(go)
    cot_stay, go = ring.blocks_for(cotangent, twins)
    cot_came = ring.swap(go)
    one = ring.along(one, column)
    two = jnp.concatenate([w_out, w_up], axis=1)
    one, two, stay, came, cot_stay, cot_came = tie(one, two, stay, came, cot_stay, cot_came)

    one = ring.across(one)
    column = ring.spread(two, outer)
    pieces = ring.paired(stay, came)
    cot_pieces = ring.paired(cot_stay, cot_came)
    one_near = ring.flat([[half] for half in one])
    target = ring.target(width)
    one, one_near, two, column, pieces, cot_pieces, target = tie(one, one_near, two, column, pieces, cot_pieces, target)

    one_more = ring.plane(one)
    one_core = ring.swap(one_near)
    rest = ring.send(pieces, outer[:1])
    column.update(ring.spread(two, inner))
    two = ring.along(two, column)
    one_near, one_more, one_core, two, pieces, rest, cot_pieces = tie(one_near, one_more, one_core, two, pieces, rest, cot_pieces)

    one_more_core = ring.to_core(one_more)
    two = ring.across(two)
    rest.update(ring.send(pieces, outer[1:]))
    one_near, one_more, one_core, one_more_core, two, pieces, rest, three = tie(
        one_near, one_more, one_core, one_more_core, two, pieces, rest, w_down
    )

    two_core = ring.to_core([[half] for half in two])
    two_more = ring.plane(two)
    rest.update(ring.send(pieces, inner))
    full_qkv, vectors = ring.assemble(ring.near_flat_sources(one_near, one_core, one_more, one_more_core), [3 * width, SMALL])
    two, two_core, two_more, rest, full_qkv, vectors, three = tie(two, two_core, two_more, rest, full_qkv, vectors, three)

    column = ring.spread(three, everything)
    two_more_core = ring.to_core(two_more)
    image_slots = jnp.concatenate([pieces[0]] + [rest[k] for k in everything]).reshape(group * slots, width)
    vectors = vectors.reshape(ring.count, rows, SMALL).astype(f32)
    bu = vectors[:, 0, 128 : 128 + wide * rows].reshape(ff)
    bq, bv, bo, bd, g1, s1, g2, s2 = [vectors[:, k, :rows].reshape(width) for k in range(8)]
    here = (image_slots[:, :1].astype(f32) < 0.5 * ABSENT).reshape(group, slots)
    held = jnp.sum(here.astype(f32), axis=1)
    before = jnp.sum(jnp.where(np.tril(np.ones((group, group), bool), -1), held[None, :], 0.0), axis=1)
    rank = before[:, None] + lax.broadcasted_iota(jnp.int32, (group, slots), 1).astype(f32)
    rank = jnp.where(here, rank, -1.0).reshape(1, group * slots).astype(jnp.int32)
    packing = (rank == lax.broadcasted_iota(jnp.int32, (PACKED, group * slots), 0)).astype(bf16)
    tokens_f, normed = pack_norm(packing, image_slots, g1, s1)
    qkv_bias = halved(jnp.concatenate([bq, jnp.zeros((width,), f32), bv]))
    qkv = project(normed, full_qkv, qkv_bias)
    mixed, logs = attend(qkv)
    three = ring.along(three, column)
    two_more_core, three, mixed = tie(two_more_core, three, mixed)

    three = ring.across(three)
    cot_rest = ring.send(cot_pieces, outer)
    full_out, full_up = ring.assemble(ring.sources(two, two_core, two_more, two_more_core), [width, ff])
    residual, normed_two = out_norm(mixed, full_out, tokens_f, bo, g2, s2)
    normed_far = ring.by_distance(normed, target)
    three, normed_two, normed_far, cot_rest = tie(three, normed_two, normed_far, cot_rest)

    three_more = ring.plane(three)
    three_core = ring.to_core([[half] for half in three])
    cot_rest.update(ring.send(cot_pieces, inner))
    ranks = ring.far(lax.broadcasted_iota(jnp.int32, (ring.count,), 0))
    active, slope, active_far = rise(normed_two, full_up, bu, ranks)
    if active_far is None:
        active_far = ring.by_distance(active, ring.target(ff))
    mixed_far = ring.by_distance(mixed, target)
    two_far = ring.by_distance(normed_two, target)
    three, three_more, three_core, active, active_far, mixed_far, two_far, cot_rest = tie(
        three, three_more, three_core, active, active_far, mixed_far, two_far, cot_rest
    )

    three_more_core = ring.to_core(three_more)
    share = (lax.axis_index(("sz", "sc")) % twins == 0).astype(f32) if twins > 1 else None
    cot_slots = jnp.concatenate([cot_pieces[0]] + [cot_rest[k] for k in everything]).reshape(group * slots, width)
    grad_low, grad_bd = pack(packing, cot_slots)
    sent = weight_grad(active_far, 1, grad_low, share)
    three_more_core, sent, grad_low = tie(three_more_core, sent, grad_low)

    d = ring.swap(sent)
    (full_down,) = ring.assemble(ring.sources(three, three_core, three_more, three_more_core), [width])
    d, full_down = tie(d, full_down)

    d = ring.kept(active_far, grad_low, share, d)
    result = slots_of(land(active, full_down, residual, bd, packing))
    d, result = tie(d, result)

    d = ring.first(d)
    back = ring.send(result, inner, -1)
    hidden_low, grad_bu = fall(grad_low, full_down, slope)
    sent = weight_grad(two_far, 1, hidden_low, share)
    d, sent, back = tie(d, sent, back)

    d = ring.again(d)
    d, sent = tie(d, sent)

    d = ring.second(d)
    u = ring.swap(sent)
    back.update(ring.send(result, outer[:1], -1))
    grad_residual, residual_low, sums_two = back_norm([hidden_low], full_up, residual, g2, grad_low)
    d, u, residual_low, back = tie(d, u, residual_low, back)

    d = ring.last(d)
    u = ring.kept(two_far, hidden_low, share, u)
    sent = weight_grad(mixed_far, 1, residual_low, share)
    d, u, sent, residual_low = tie(d, u, sent, residual_low)

    u = ring.first(u)
    gone = ring.toward_some(d, outer)
    back.update(ring.send(result, outer[1:], -1))
    grad_mixed = back_project(residual_low, full_out)
    sent_out = sent
    half_grads = attend_back(qkv, logs, grad_mixed)
    u, sent_out, d, gone, grad_mixed, half_grads, back = tie(u, sent_out, d, gone, grad_mixed, half_grads, back)

    u = ring.again(u)
    u, sent_out, back, d, grad_mixed, half_grads = tie(u, sent_out, back, d, grad_mixed, half_grads)

    u = ring.second(u)
    gone.update(ring.toward_some(d, inner))
    o = ring.swap(sent_out)
    grads, grad_sums = attend_back(qkv, logs, grad_mixed, half_grads)
    sent = weight_grad(normed_far, 1, grads, share)
    u, o, sent, grads, back, d, gone = tie(u, o, sent, grads, back, d, gone)
    d = [d[0]] + [gone[k] for k in everything]

    u = ring.last(u)
    u, sent, grads = tie(u, sent, grads)

    later = ring.toward_some(u, outer)
    q = ring.swap(sent)
    grad_tokens, sums_one = back_norm([grads], full_qkv, tokens_f, g1, grad_residual, packing)
    grad_tokens = slots_of(grad_tokens)
    u, later, o, q, grads, grad_tokens, sums_one, back, d = tie(u, later, o, q, grads, grad_tokens, sums_one, back, d)

    sent_back = ring.send(grad_tokens, outer, -1)
    q = ring.kept(normed_far, grads, share, q)
    o = ring.reshaped(weight_grad(mixed_far, 0, residual_low, share, o))
    joined_sum = whole(grad_sums[0])
    grad_bq, grad_bv = joined_sum[:width], joined_sum[2 * width :]
    small = [grad_bq, grad_bv, sums_two[2], grad_bd, sums_one[0], sums_one[1], sums_two[0], sums_two[1]]
    small = [array.reshape(ring.count, rows) for array in small] + [grad_bu.reshape(ring.count, wide * rows)]
    small = jnp.concatenate(small, axis=1)
    small = (small if share is None else small * share).astype(bf16)
    near_first = (ranks[None, :] == lax.broadcasted_iota(jnp.int32, (ring.count, 1), 0)).astype(bf16)
    small = dot_float(near_first, small).astype(bf16)
    small = jnp.pad(small, ((0, 0), (0, rows * SMALL - small.shape[1]))).reshape(2, ring.count // 2 * rows, SMALL)
    q, o, small, u, sent_back, grad_tokens, back, d = tie(q, o, small, u, sent_back, grad_tokens, back, d)

    q = ring.first(q)
    sent_back.update(ring.send(grad_tokens, inner, -1))
    came = ring.swap(small[1])
    own = jnp.stack([result[0]] + [back[k] for k in everything])
    other = ring.swap(own[:, 1])
    q, came, sent_back, u, back, d, own, other = tie(q, came, sent_back, u, back, d, own, other)

    q = ring.again(q)
    small = ring.reshaped(total([small[0], came]).astype(bf16))
    o = ring.ready(jnp.concatenate([o, small], axis=-1))
    q, o, u, own, d = tie(q, o, u, own, d)

    q = ring.second(q)
    o = ring.first(o)
    later.update(ring.toward_some(u, inner))
    result = ring.images_of(own[:, 0], other, images, twins)
    result = jnp.where(slot < counts[:, :, None], result, jnp.asarray(0, bf16))
    o, later, result, q, d = tie(o, later, result, q, d)

    q = ring.last(q)
    o = ring.again(o)
    o, q, d = tie(o, q, d)

    q = ring.third(q)
    o = ring.second(o)
    u = [u[0]] + [later[k] for k in everything]
    grad_tokens, came = back_pieces(sent_back, grad_tokens[0])
    q, o, grad_tokens, came = tie(q, o, grad_tokens, came)

    o = ring.third(ring.last(o))
    grad_tokens = ring.images_of(grad_tokens, came, images, twins).astype(f32)

    sum_down, sum_up = total(d), total(u)
    o = total(o)
    sum_out = o[:, :width]
    sum_qkv = whole(total(q))
    small = o[:, width:].reshape(rows * SMALL)
    sum_bq, sum_bv, sum_bo, sum_bd, sum_g1, sum_s1, sum_g2, sum_s2 = [small[k * rows : (k + 1) * rows] for k in range(8)]
    sum_bu = small[8 * rows : (8 + wide) * rows]
    return (result, grad_tokens, sum_qkv, sum_bq, sum_bv, sum_out, sum_bo, sum_up, sum_bu, sum_down, sum_bd, sum_g1, sum_s1, sum_g2, sum_s2)


def solution(mesh):
    n_grp, n_seq = mesh.shape["grp"], mesh.shape["seq"]
    sizes = (n_grp // 2, 2, n_seq // 2, 2)
    fine = Mesh(mesh.devices.reshape(sizes), AXES)
    ring = Ring(sizes)
    grp, seq = AXES[:2], AXES[2:]
    by_token = P(grp, seq, None)
    rows, vec = P(AXES, None), P(AXES)
    in_specs = (by_token, P(grp, seq), rows, vec, vec, rows, vec, rows, vec, rows, vec, vec, vec, vec, vec, by_token)
    out_specs = (by_token, by_token, rows, vec, vec, rows, vec, rows, vec, rows, vec, vec, vec, vec, vec)

    def shards(*args):
        return layer(ring, *args)

    return jax.shard_map(shards, mesh=fine, in_specs=in_specs, out_specs=out_specs, check_vma=False)
```

```python
import jax
import jax.numpy as jnp
import numpy as np
from jax import lax
from jax.experimental import pallas as pl
from jax.experimental.pallas import tpu as pltpu
from jax.sharding import Mesh
from jax.sharding import PartitionSpec as P

H = 16
HD = 64
LENGTH = 577
PACKED = 592
EPSILON = 1e-06
NEGATIVE = -1e30
ABSENT = 100.0
SMALL = 256
AXES = ("gy", "gx", "sz", "sc")
ORDERS = (("gx", "gy"), ("gy", "gx"))

bf16 = jnp.bfloat16
f32 = jnp.float32


def norm_rows(values, gain_vec, shift_vec):
    row_mean = jnp.mean(values, axis=-1, keepdims=True)
    centred = values - row_mean
    row_var = jnp.mean(centred * centred, axis=-1, keepdims=True)
    return centred * lax.rsqrt(row_var + EPSILON) * gain_vec + shift_vec


def dot_float(left, right):
    return jnp.dot(left, right, preferred_element_type=f32)


def contract_rows(left, right):
    return lax.dot_general(left, right, (((0,), (0,)), ((), ())), preferred_element_type=f32)


def contract_cols(left, right):
    return lax.dot_general(left, right, (((1,), (1,)), ((), ())), preferred_element_type=f32)


def room(mib=50):
    return pltpu.CompilerParams(vmem_limit_bytes=mib * 2**20)


HINT = 0.02


def cost(flops, bytes_accessed, transcendentals=0):
    return pl.CostEstimate(
        flops=int(HINT * flops), bytes_accessed=int(HINT * bytes_accessed), transcendentals=int(HINT * transcendentals)
    )


def shifted(array, axis, size, step):
    return lax.ppermute(array, axis, [(i, (i + step) % size) for i in range(size)])


def pick(array, index, axis):
    return lax.dynamic_index_in_dim(array, index, axis, keepdims=False)


class Ring:
    def __init__(self, sizes):
        self.sizes = dict(zip(AXES, sizes))
        self.count = int(np.prod(sizes))

    def place(self):
        return {axis: lax.axis_index(axis) for axis in AXES}

    def others(self, array, axis):
        size = self.sizes[axis]
        return [shifted(array, axis, size, step) for step in range(1, size)]

    def others_from(self, array, axis, steps):
        size = self.sizes[axis]
        return [shifted(array, axis, size, step) for step in steps]

    def along(self, shard, columns):
        cut = shard.shape[0] // 2
        size = self.sizes["sz"]
        columns = [shard] + [columns[k] for k in range(1, size)]
        here = lax.axis_index("sz")
        ordered = [lax.select_n((here - k) % size, *columns) if size > 2 else jnp.where(here == k, *columns) for k in range(size)]
        return [jnp.stack([c[:cut] for c in ordered]), jnp.stack([c[cut:] for c in ordered])]

    def spread(self, shard, steps):
        return {k: shifted(shard, "sz", self.sizes["sz"], k) for k in steps}

    def across(self, halves):
        return [jnp.stack([half] + self.others(half, order[0])) for half, order in zip(halves, ORDERS)]

    def plane(self, halves):
        return [self.others(half, order[1]) for half, order in zip(halves, ORDERS)]

    def to_core(self, groups):
        return [[shifted(group, "sc", 2, 1) for group in part] for part in groups]

    def sources(self, first, traded_first, second, traded_second):
        found = []
        for part in range(2):
            kinds = ([first[part]] + second[part], traded_first[part] + traded_second[part])
            for turn, groups in enumerate(kinds):
                found += [(g, turn, [(part, step, one) for one in range(g.shape[0])]) for step, g in enumerate(groups)]
        return found

    def flat(self, groups):
        return jnp.concatenate([group for part in groups for group in part], axis=0)

    def labels(self, far):
        sizes = self.sizes
        found = []
        for part in range(2):
            for step in range(1, sizes[ORDERS[part][1]]) if far else [0]:
                found += [(part, step, one) for one in range(sizes[ORDERS[part][0]])]
        return found

    def near_flat_sources(self, near, near_core, second, traded_second):
        found = [(near, 0, self.labels(False)), (near_core, 1, self.labels(False))]
        for turn, groups in enumerate((second, traded_second)):
            for part in range(2):
                for step, g in enumerate(groups[part]):
                    found.append((g, turn, [(part, step + 1, one) for one in range(g.shape[0])]))
        return found

    def assemble(self, sources, widths):
        place = self.place()
        sizes = self.sizes
        cut, width = sources[0][0].shape[-2:]
        depth = sizes["sz"]
        planes, kinds, parts, arrays, counts = [], [], [], [], []
        for group, turn, labels in sources:
            arrays.append(group)
            counts.append(len(labels))
            for part, step, one in labels:
                order = ORDERS[part]
                at = {order[1]: (place[order[1]] - step) % sizes[order[1]], order[0]: (place[order[0]] - one) % sizes[order[0]]}
                planes.append(at["gy"] * sizes["gx"] + at["gx"])
                kinds.append((place["sc"] - turn) % 2)
                parts.append(part)
        table = jnp.stack(planes + kinds).astype(jnp.int32)
        many = len(planes)
        starts = np.concatenate([[0], np.cumsum(widths)])

        def body(table_ref, *refs):
            ins = refs[: len(counts)]
            outs = refs[len(counts) : -3]
            held, came, left = refs[-3:]
            arrivals = []
            for ref, count in zip(ins, counts):
                for k in range(count):
                    n = len(arrivals)
                    arrivals.append(pltpu.make_async_copy(ref.at[k], held.at[n], came.at[n]))
            for copy in arrivals:
                copy.start()
            departures = []
            for n, copy in enumerate(arrivals):
                copy.wait()
                for i, out in enumerate(outs):
                    window = held.at[n, :, :, pl.ds(int(starts[i]), widths[i])]
                    target = out.at[table_ref[n], :, table_ref[many + n], parts[n]]
                    leave = pltpu.make_async_copy(window, target, left.at[n, i])
                    leave.start()
                    departures.append(leave)
            for copy in departures:
                copy.wait()

        planes_all = sizes["gy"] * sizes["gx"]
        outs = pl.pallas_call(
            body,
            out_shape=[jax.ShapeDtypeStruct((planes_all, depth, 2, 2, cut, w), bf16) for w in widths],
            grid_spec=pltpu.PrefetchScalarGridSpec(
                num_scalar_prefetch=1,
                grid=(1,),
                in_specs=[pl.BlockSpec(memory_space=pl.ANY)] * len(counts),
                out_specs=[pl.BlockSpec(memory_space=pl.ANY)] * len(widths),
                scratch_shapes=[
                    pltpu.VMEM((many, depth, cut, width), bf16),
                    pltpu.SemaphoreType.DMA((many,)),
                    pltpu.SemaphoreType.DMA((many, len(widths))),
                ],
            ),
            compiler_params=room(),
            cost_estimate=cost(0, 4 * self.count * 2 * cut * width),
            name="assemble",
        )(table, *arrays)
        return [out.reshape(self.count * 2 * cut, w) for out, w in zip(outs, widths)]

    def far(self, device):
        place = self.place()
        sizes = self.sizes
        index, out = device, {}
        for axis in AXES[::-1]:
            out[axis] = (index % sizes[axis] - place[axis]) % sizes[axis]
            index = index // sizes[axis]
        return ((out["sc"] * sizes["gy"] + out["gy"]) * sizes["gx"] + out["gx"]) * sizes["sz"] + out["sz"]

    def target(self, width):
        block = width // self.count
        row = lax.broadcasted_iota(jnp.int32, (width, 1), 0)
        return self.far(row // block) * block + row % block

    def by_distance(self, array, target):
        tokens, width = array.shape
        half = width // 2

        def body(x_ref, t_ref, o_ref):
            columns = lax.broadcasted_iota(jnp.int32, (width, half), 1) + half * pl.program_id(0)
            pick_columns = jnp.where(t_ref[...] == columns, 1.0, 0.0).astype(bf16)
            o_ref[0] = dot_float(x_ref[...], pick_columns).astype(bf16)

        return pl.pallas_call(
            body,
            out_shape=jax.ShapeDtypeStruct((2, tokens, half), bf16),
            grid=(2,),
            in_specs=[pl.BlockSpec((tokens, width), lambda i: (0, 0)), pl.BlockSpec((width, 1), lambda i: (0, 0))],
            out_specs=pl.BlockSpec((1, tokens, half), lambda i: (i, 0, 0)),
            compiler_params=room(),
            cost_estimate=cost(2 * tokens * width * width, 4 * tokens * width),
            name="by_distance",
        )(array, target)

    def blocks_for(self, array, twins):
        place = self.place()
        size = self.sizes["sz"]
        out = []
        for turn in range(2):
            found = [((place["sz"] + k) % size * 2 + (place["sc"] + turn) % 2) // twins for k in range(size)]
            out.append(jnp.stack([pick(array, image, 0) for image in found]))
        return out

    def paired(self, stay, came):
        return [jnp.stack([stay[k], came[k]]) for k in range(self.sizes["sz"])]

    def send(self, pieces, steps, sign=1):
        return {k: shifted(pieces[k], "sz", self.sizes["sz"], sign * k) for k in steps}

    def images_of(self, own, came, images, twins):
        place = self.place()
        size = self.sizes["sz"]
        both = jnp.stack([own, came])
        both = both.reshape((2 * size,) + both.shape[2:])
        out = []
        for image in range(images):
            device = image * twins
            out.append(pick(both, (device % 2 - place["sc"]) % 2 * size + (device // 2 - place["sz"]) % size, 0))
        return jnp.stack(out)

    def swap(self, sent):
        return shifted(sent, "sc", 2, 1)

    def reshaped(self, out):
        sizes = self.sizes
        return out.reshape(sizes["gy"], sizes["gx"], sizes["sz"], out.shape[0] // (self.count // 2), out.shape[1])

    def kept(self, left, right, share, came):
        cut = left.shape[2] // (self.count // 2) // 2
        if cut % 16 == 0:
            return weight_grad(left, 0, right, share, came, self.sizes)
        return self.ready(self.reshaped(weight_grad(left, 0, right, share, came)))

    def toward(self, arrays, axis):
        size = self.sizes[axis]
        return [arrays[0]] + [shifted(arrays[k], axis, size, k) for k in range(1, size)]

    def toward_some(self, parts, steps):
        return {k: shifted(parts[k], "sz", self.sizes["sz"], k) for k in steps}

    def ready(self, sums):
        cut = sums.shape[3] // 2
        upper = [sums[k, :, :, :cut] for k in range(self.sizes["gy"])]
        lower = [sums[:, k, :, cut:] for k in range(self.sizes["gx"])]
        return upper, lower

    def first(self, pair):
        return self.toward(pair[0], "gy"), self.toward(pair[1], "gx")

    def again(self, pair):
        return tuple(
            [total([t[k] for t in terms]).astype(bf16) for k in range(self.sizes[axis])]
            for terms, axis in zip(pair, ("gx", "gy"))
        )

    def second(self, pair):
        return self.toward(pair[0], "gx"), self.toward(pair[1], "gy")

    def last(self, pair):
        return [
            jnp.concatenate([total([t[k] for t in terms]) for terms in pair], axis=0).astype(bf16)
            for k in range(self.sizes["sz"])
        ]

    def third(self, parts):
        return self.toward(parts, "sz")


def weight_grad(left, kind, right, share, came=None, sizes=None):
    tokens, columns = right.shape
    rows = left.shape[2]
    tiled = rows > 512
    parts = 1
    if sizes is not None:
        ny, nx, nz = sizes["gy"], sizes["gx"], sizes["sz"]
        parts = ny * nx
        block = rows // (parts * nz)
        cut = block // 2
    if tiled:
        tall, broad = rows // (parts if sizes is not None else rows // 512), columns
        steps = rows // tall
        at = lambda i: (i, 0)
        left_at, right_at = (lambda i: (kind, 0, i)), (lambda i: (0, 0))
    else:
        tall, broad = rows, next(w for w in (1024, 768, 512, 128) if columns % w == 0)
        steps = columns // broad
        at = lambda i: (0, i)
        left_at, right_at = (lambda i: (kind, 0, 0)), (lambda i: (0, i))
    others = [] if came is None else [came.reshape(rows, columns)]
    if share is not None:
        others.append(share.reshape(1, 1))
    given = 2 + len(others)

    def body(*refs):
        outs = refs[given:]
        out = contract_rows(refs[0][0], refs[1][...])
        if share is not None:
            out = out * refs[given - 1][...]
        if came is not None:
            out = out + refs[2][...].astype(f32)
        if sizes is None:
            outs[0][...] = out.astype(bf16)
        elif tiled:
            i = pl.program_id(0)
            out = out.astype(bf16).reshape(nz, block, broad)
            for k in range(ny):

                @pl.when(i // nx == k)
                def _(k=k):
                    outs[k][0] = out[:, :cut]

            for k in range(nx):

                @pl.when(i % nx == k)
                def _(k=k):
                    outs[ny + k][0] = out[:, cut:]

        else:
            out = out.astype(bf16).reshape(ny, nx, nz, block, broad)
            for k in range(ny):
                outs[k][...] = out[k, :, :, :cut]
            for k in range(nx):
                outs[ny + k][...] = out[:, k, :, cut:]

    specs = [pl.BlockSpec((1, tokens, tall), left_at), pl.BlockSpec((tokens, broad), right_at)]
    if came is not None:
        specs.append(pl.BlockSpec((tall, broad), at))
    if share is not None:
        specs.append(pl.BlockSpec((1, 1), lambda i: (0, 0)))
    if sizes is None:
        shapes, out_specs = [(rows, columns)], [pl.BlockSpec((tall, broad), at)]
    else:
        shapes = [(nx, nz, cut, columns)] * ny + [(ny, nz, cut, columns)] * nx
        if tiled:
            out_specs = [
                pl.BlockSpec((1, nz, cut, broad), lambda i, k=k: (jnp.clip(i - k * nx, 0, nx - 1), 0, 0, 0)) for k in range(ny)
            ]
            out_specs += [pl.BlockSpec((1, nz, cut, broad), lambda i, k=k: (jnp.maximum(i - k, 0) // nx, 0, 0, 0)) for k in range(nx)]
        else:
            out_specs = [pl.BlockSpec(shape[:3] + (broad,), lambda i: (0, 0, 0, i)) for shape in shapes]
    outs = pl.pallas_call(
        body,
        out_shape=[jax.ShapeDtypeStruct(shape, bf16) for shape in shapes],
        grid=(steps,),
        in_specs=specs,
        out_specs=out_specs,
        compiler_params=room(),
        cost_estimate=cost(2 * tokens * rows * columns, 4 * rows * columns),
        name="weight_grad",
    )(left, right, *others)
    return outs[0] if sizes is None else (outs[:ny], outs[ny:])


def total(arrays):
    out = arrays[0].astype(f32)
    for array in arrays[1:]:
        out = out + array.astype(f32)
    return out


def tie(*values):
    return lax.optimization_barrier(values)


def of_head(part):
    return lax.broadcasted_iota(jnp.int32, (1, 2 * HD), 1) // HD == part


def mask_tail(scores, fill):
    start = LENGTH // 8 * 8
    row = lax.broadcasted_iota(jnp.int32, (PACKED - start, PACKED), 0)
    tail = jnp.where(row < LENGTH - start, scores[start:], fill)
    return jnp.concatenate([scores[:start], tail], axis=0)


def flip(array):
    return array.astype(f32).T.astype(bf16)


def attend_body(q_ref, k_ref, v_ref, o_ref, l_ref):
    query, key = q_ref[...] * jnp.asarray(HD**-0.5, bf16), k_ref[...]
    value_t = flip(v_ref[...])
    mixed, logs = [], []
    for part in range(2):
        scores = contract_cols(jnp.where(of_head(part), key, 0), query)
        scores = mask_tail(scores, NEGATIVE)
        top = jnp.max(scores, axis=0, keepdims=True)
        exponent = jnp.exp(scores - top)
        total = jnp.sum(exponent, axis=0, keepdims=True)
        out = dot_float(value_t[HD * part : HD * (part + 1)], exponent.astype(bf16))
        mixed.append(out * (1.0 / total))
        logs.append(top + jnp.log(total))
    o_ref[...] = jnp.concatenate(mixed, axis=0).T.astype(bf16)
    l_ref[...] = jnp.concatenate(logs + [jnp.zeros((6, PACKED), f32)], axis=0)


PAIR = (PACKED, 2 * HD)
PAIRS = H // 2
CUT = PAIRS // 2


def kind_spec(kind, base=0):
    return pl.BlockSpec(PAIR, lambda i: (0, (i + base) // CUT * 3 * CUT + (i + base) % CUT + kind * CUT))


def pair_spec(base=0):
    return pl.BlockSpec(PAIR, lambda i: (0, i + base))


def log_spec(base=0):
    return pl.BlockSpec((8, PACKED), lambda i: (i + base, 0))


def halved(array):
    return array.reshape(-1, 3, 2, H * HD // 2).swapaxes(1, 2).reshape(array.shape)


def whole(array):
    return array.reshape(-1, 2, 3, H * HD // 2).swapaxes(1, 2).reshape(array.shape)


def attend(qkv):
    return pl.pallas_call(
        attend_body,
        out_shape=[
            jax.ShapeDtypeStruct((PACKED, H * HD), bf16),
            jax.ShapeDtypeStruct((8 * PAIRS, PACKED), f32),
        ],
        grid=(PAIRS,),
        in_specs=[kind_spec(0), kind_spec(1), kind_spec(2)],
        out_specs=[pair_spec(), log_spec()],
        compiler_params=room(),
        cost_estimate=cost(12e9, 8 * qkv.size, PACKED * PACKED * H),
        name="attend",
    )(qkv, qkv, qkv)


def attend_back_body(q_ref, k_ref, v_ref, l_ref, g_ref, *rest):
    d_ref, s_ref = rest[-2:]
    base = 0
    if len(rest) == 4:
        base = rest[0].shape[1]

        @pl.when(pl.program_id(0) == 0)
        def _():
            d_ref[:, :base] = rest[0][...]
            s_ref[:, :base] = rest[1][...]

    scale = jnp.asarray(HD**-0.5, bf16)
    query, key, value, grad = q_ref[...] * scale, k_ref[...], v_ref[...], g_ref[...]
    key_t = flip(key)
    grad_query, grad_key, grad_value = [], [], []
    for part in range(2):
        mask = of_head(part)
        scores = contract_cols(jnp.where(mask, key, 0), query)
        soft = mask_tail(jnp.exp(scores - l_ref[part : part + 1]), 0.0)
        grad_soft = contract_cols(jnp.where(mask, value, 0), grad)
        delta = jnp.sum(soft * grad_soft, axis=0, keepdims=True)
        grad_scores = (soft * (grad_soft - delta)).astype(bf16)
        grad_value.append(dot_float(soft.astype(bf16), grad))
        grad_key.append(dot_float(grad_scores, query))
        grad_query.append(dot_float(key_t[HD * part : HD * (part + 1)], grad_scores))
    first = of_head(0)
    grads = (
        jnp.concatenate(grad_query, axis=0).T * HD**-0.5,
        jnp.where(first, grad_key[0], grad_key[1]),
        jnp.where(first, grad_value[0], grad_value[1]),
    )
    for kind, array in enumerate(grads):
        start = pl.multiple_of(base + (pl.program_id(0) + kind * CUT) * 2 * HD, 2 * HD)
        low = array.astype(bf16)
        d_ref[:, pl.ds(start, 2 * HD)] = low
        s_ref[:, pl.ds(start, 2 * HD)] = jnp.sum(low.astype(f32), axis=0, keepdims=True)


def attend_back(qkv, logs, grad_mixed, before=()):
    base = CUT if before else 0
    width = qkv.shape[1] // (1 if before else 2)
    return pl.pallas_call(
        attend_back_body,
        out_shape=[jax.ShapeDtypeStruct((PACKED, width), bf16), jax.ShapeDtypeStruct((1, width), f32)],
        grid=(CUT,),
        in_specs=[kind_spec(0, base), kind_spec(1, base), kind_spec(2, base), log_spec(base), pair_spec(base)]
        + [pl.BlockSpec(array.shape, lambda i: (0, 0)) for array in before],
        out_specs=[pl.BlockSpec((PACKED, width), lambda i: (0, 0)), pl.BlockSpec((1, width), lambda i: (0, 0))],
        compiler_params=room(),
        cost_estimate=cost(12e9, 8 * qkv.size, PACKED * PACKED * H // 2),
        name="attend_back",
    )(qkv, qkv, qkv, logs, grad_mixed, *before)


def rise(normed, weights, bias, ranks):
    width, ff = weights.shape
    step = ff // 4
    count = ranks.shape[0]
    block = ff // count
    inside = step // block
    whole_tiles = block % 128 == 0

    def body(rank_ref, x_ref, w_ref, b_ref, active_ref, slope_ref, *rest):
        i = pl.program_id(0)
        hidden = dot_float(x_ref[...], w_ref[...]) + b_ref[...]
        share = 0.5 * (1.0 + lax.erf(hidden * np.float32(np.sqrt(0.5))))
        active = (hidden * share).astype(bf16)
        active_ref[...] = active
        bell = jnp.exp(hidden * hidden * -0.5) * np.float32(1.0 / np.sqrt(2.0 * np.pi))
        slope_ref[...] = share + hidden * bell
        if not whole_tiles:
            return
        far_ref, held, sems = rest
        held[i % 2] = active

        def copies(turn):
            out = []
            for k in range(inside):
                rank = rank_ref[turn * inside + k]
                start = pl.multiple_of(rank % (count // 2) * block, block)
                window = held.at[turn % 2, :, pl.ds(k * block, block)]
                out.append(pltpu.make_async_copy(window, far_ref.at[rank // (count // 2), :, pl.ds(start, block)], sems.at[turn % 2, k]))
            return out

        for copy in copies(i):
            copy.start()

        @pl.when(i > 0)
        def _():
            for copy in copies(i - 1):
                copy.wait()

        @pl.when(i == 3)
        def _():
            for copy in copies(i):
                copy.wait()

    shapes = [jax.ShapeDtypeStruct((PACKED, ff), bf16), jax.ShapeDtypeStruct((PACKED, ff), f32)]
    specs = [pl.BlockSpec((PACKED, step), lambda i, t: (0, i))] * 2
    scratch = []
    if whole_tiles:
        shapes.append(jax.ShapeDtypeStruct((2, PACKED, ff // 2), bf16))
        specs.append(pl.BlockSpec(memory_space=pl.ANY))
        scratch = [pltpu.VMEM((2, PACKED, step), bf16), pltpu.SemaphoreType.DMA((2, inside))]
    outs = pl.pallas_call(
        body,
        out_shape=shapes,
        grid_spec=pltpu.PrefetchScalarGridSpec(
            num_scalar_prefetch=1,
            grid=(4,),
            in_specs=[
                pl.BlockSpec((PACKED, width), lambda i, t: (0, 0)),
                pl.BlockSpec((width, step), lambda i, t: (0, i)),
                pl.BlockSpec((1, step), lambda i, t: (0, i)),
            ],
            out_specs=specs,
            scratch_shapes=scratch,
        ),
        compiler_params=room(),
        cost_estimate=cost(12e9, 30e6, PACKED * ff * 2),
        name="rise",
    )(ranks, normed, weights, bias.reshape(1, ff))
    return outs if whole_tiles else (outs[0], outs[1], None)


def fall_body(g_ref, w_ref, slope_ref, out_ref, sum_ref):
    grad = (contract_cols(g_ref[...], w_ref[...]) * slope_ref[...]).astype(bf16)
    out_ref[...] = grad
    sum_ref[...] = jnp.sum(grad.astype(f32), axis=0, keepdims=True)


def fall(grads, weights, slope):
    ff, width = weights.shape
    step = ff // 4
    return pl.pallas_call(
        fall_body,
        out_shape=[jax.ShapeDtypeStruct((PACKED, ff), bf16), jax.ShapeDtypeStruct((1, ff), f32)],
        grid=(4,),
        in_specs=[
            pl.BlockSpec((PACKED, width), lambda i: (0, 0)),
            pl.BlockSpec((step, width), lambda i: (i, 0)),
            pl.BlockSpec((PACKED, step), lambda i: (0, i)),
        ],
        out_specs=[pl.BlockSpec((PACKED, step), lambda i: (0, i)), pl.BlockSpec((1, step), lambda i: (0, i))],
        compiler_params=room(),
        cost_estimate=cost(10e9, 25e6),
        name="fall",
    )(grads, weights, slope)


def project_body(x_ref, w_ref, b_ref, out_ref):
    out_ref[...] = (dot_float(x_ref[...], w_ref[...]) + b_ref[...]).astype(bf16)


def project(left, weights, bias):
    width, columns = weights.shape
    step = columns // 3
    return pl.pallas_call(
        project_body,
        out_shape=jax.ShapeDtypeStruct((PACKED, columns), bf16),
        grid=(3,),
        in_specs=[
            pl.BlockSpec((PACKED, width), lambda i: (0, 0)),
            pl.BlockSpec((width, step), lambda i: (0, i)),
            pl.BlockSpec((1, step), lambda i: (0, i)),
        ],
        out_specs=pl.BlockSpec((PACKED, step), lambda i: (0, i)),
        compiler_params=room(),
        cost_estimate=cost(6e9, 12e6),
        name="project",
    )(left, weights, bias.reshape(1, columns))


def row(vector):
    return vector.reshape(1, -1)


def fixed(shape):
    return pl.BlockSpec(shape, lambda i: (0,) * len(shape))


def seed(weights, vectors, long):
    rows, width = weights.shape
    half = width // 6

    def body(w_ref, *refs):
        out_ref = refs[-1]
        for k in range(6):
            out_ref[:, k * half : (k + 1) * half] = w_ref[:, pl.ds((k % 3 * 2 + k // 3) * half, half)]
        out_ref[:, width:] = jnp.zeros((rows, SMALL), bf16)
        for k in range(len(vectors)):
            out_ref[k : k + 1, width : width + rows] = refs[k][...]
        out_ref[0:1, width + 128 : width + 128 + long.shape[0]] = refs[len(vectors)][...]

    return pl.pallas_call(
        body,
        out_shape=jax.ShapeDtypeStruct((rows, width + SMALL), bf16),
        cost_estimate=cost(0, 1e6),
        name="seed",
    )(weights, *[row(v) for v in vectors], row(long))


def pack_norm_body(p_ref, x_ref, g_ref, s_ref, t_ref, n_ref):
    tokens = dot_float(p_ref[...], x_ref[...])
    t_ref[...] = tokens
    n_ref[...] = norm_rows(tokens, g_ref[...], s_ref[...]).astype(bf16)


def pack_norm(packing, slots, gain, shift):
    count, width = slots.shape
    half = PACKED // 2
    by_row = pl.BlockSpec((half, width), lambda i: (i, 0))
    return pl.pallas_call(
        pack_norm_body,
        out_shape=[jax.ShapeDtypeStruct((PACKED, width), f32), jax.ShapeDtypeStruct((PACKED, width), bf16)],
        grid=(2,),
        in_specs=[pl.BlockSpec((half, count), lambda i: (i, 0)), fixed((count, width)), fixed((1, width)), fixed((1, width))],
        out_specs=[by_row, by_row],
        compiler_params=room(),
        cost_estimate=cost(1e9, 8e6),
        name="pack_norm",
    )(packing, slots, row(gain), row(shift))


def pack_body(p_ref, x_ref, o_ref, s_ref):
    low = dot_float(p_ref[...], x_ref[...]).astype(bf16)
    o_ref[...] = low
    s_ref[...] = jnp.sum(low.astype(f32), axis=0, keepdims=True)


def pack(packing, slots):
    count, width = slots.shape
    half = width // 2
    return pl.pallas_call(
        pack_body,
        out_shape=[jax.ShapeDtypeStruct((PACKED, width), bf16), jax.ShapeDtypeStruct((1, width), f32)],
        grid=(2,),
        in_specs=[fixed((PACKED, count)), pl.BlockSpec((count, half), lambda i: (0, i))],
        out_specs=[pl.BlockSpec((PACKED, half), lambda i: (0, i)), pl.BlockSpec((1, half), lambda i: (0, i))],
        compiler_params=room(),
        cost_estimate=cost(1e9, 4e6),
        name="pack",
    )(packing, slots)


def out_norm_body(m_ref, w_ref, t_ref, b_ref, g_ref, s_ref, r_ref, n_ref):
    residual = t_ref[...] + dot_float(m_ref[...], w_ref[...]) + b_ref[...]
    r_ref[...] = residual
    n_ref[...] = norm_rows(residual, g_ref[...], s_ref[...]).astype(bf16)


def out_norm(mixed, weights, tokens, bias, gain, shift):
    width = weights.shape[1]
    half = PACKED // 2
    by_row = pl.BlockSpec((half, width), lambda i: (i, 0))
    vec = fixed((1, width))
    return pl.pallas_call(
        out_norm_body,
        out_shape=[jax.ShapeDtypeStruct((PACKED, width), f32), jax.ShapeDtypeStruct((PACKED, width), bf16)],
        grid=(2,),
        in_specs=[by_row, fixed(weights.shape), by_row, vec, vec, vec],
        out_specs=[by_row, by_row],
        compiler_params=room(),
        cost_estimate=cost(2e9, 8e6),
        name="out_norm",
    )(mixed, weights, tokens, row(bias), row(gain), row(shift))


def land_body(a_ref, w_ref, r_ref, b_ref, p_ref, o_ref, sum_ref):
    i = pl.program_id(0)
    part = dot_float(a_ref[...], w_ref[...])

    @pl.when(i == 0)
    def _():
        sum_ref[...] = part + r_ref[...] + b_ref[...]

    @pl.when(i > 0)
    def _():
        sum_ref[...] += part

    @pl.when(i == pl.num_programs(0) - 1)
    def _():
        o_ref[...] = contract_rows(p_ref[...], sum_ref[...].astype(bf16)).astype(bf16)


def land(active, weights, residual, bias, packing):
    ff, width = weights.shape
    step = ff // 4
    count = packing.shape[1]
    return pl.pallas_call(
        land_body,
        out_shape=jax.ShapeDtypeStruct((count, width), bf16),
        grid=(4,),
        in_specs=[
            pl.BlockSpec((PACKED, step), lambda i: (0, i)),
            pl.BlockSpec((step, width), lambda i: (i, 0)),
            fixed((PACKED, width)),
            fixed((1, width)),
            fixed((PACKED, count)),
        ],
        out_specs=fixed((count, width)),
        scratch_shapes=[pltpu.VMEM((PACKED, width), f32)],
        compiler_params=room(),
        cost_estimate=cost(6e9, 14e6),
        name="land",
    )(active, weights, residual, row(bias), packing)


def back_norm(grads, weights, values, gain, added, packing=None):
    width = weights.shape[0]
    step = weights.shape[1] // (4 if len(grads) == 1 else len(grads))
    steps = weights.shape[1] // step
    count = len(grads)

    def body(*refs):
        g_refs, (w_ref, x_ref, gain_ref, add_ref), rest = refs[:count], refs[count : count + 4], refs[count + 4 :]
        sum_ref = rest[-1]
        i = pl.program_id(0)
        for k, g_ref in enumerate(g_refs):

            @pl.when((i == k) if count > 1 else (i >= 0))
            def _(g_ref=g_ref, k=k):
                part = contract_cols(g_ref[...], w_ref[...])

                @pl.when(i == 0)
                def _():
                    sum_ref[...] = part

                @pl.when(i > 0)
                def _():
                    sum_ref[...] += part

        @pl.when(i == steps - 1)
        def _():
            back = sum_ref[...]
            values = x_ref[...]
            centred = values - jnp.mean(values, axis=-1, keepdims=True)
            scale = lax.rsqrt(jnp.mean(centred * centred, axis=-1, keepdims=True) + EPSILON)
            normed = centred * scale
            scaled = back * gain_ref[...]
            inner = jnp.mean(scaled * normed, axis=-1, keepdims=True)
            out = (scaled - jnp.mean(scaled, axis=-1, keepdims=True) - normed * inner) * scale + add_ref[...].astype(f32)
            low = out.astype(bf16)
            if packing is None:
                out_ref, low_ref, sums_ref = rest[:3]
                out_ref[...] = out
                low_ref[...] = low
            else:
                p_ref, low_ref, sums_ref = rest[:3]
                low_ref[...] = contract_rows(p_ref[...], low).astype(bf16)
            sums = [jnp.sum(a, axis=0, keepdims=True) for a in (back * normed, back, low.astype(f32))]
            sums_ref[...] = jnp.concatenate(sums + [jnp.zeros((5, width), f32)], axis=0)

    full = fixed((PACKED, width))
    if packing is None:
        shapes = [jax.ShapeDtypeStruct((PACKED, width), f32), jax.ShapeDtypeStruct((PACKED, width), bf16)]
        out_specs, more_specs, more = [full, full], [], []
    else:
        shapes = [jax.ShapeDtypeStruct((packing.shape[1], width), bf16)]
        out_specs, more_specs, more = [fixed(shapes[0].shape)], [fixed(packing.shape)], [packing]
    g_spec = fixed((PACKED, step)) if count > 1 else pl.BlockSpec((PACKED, step), lambda i: (0, i))
    return pl.pallas_call(
        body,
        out_shape=shapes + [jax.ShapeDtypeStruct((8, width), f32)],
        grid=(steps,),
        in_specs=[g_spec] * count + [pl.BlockSpec((width, step), lambda i: (0, i)), full, fixed((1, width)), full] + more_specs,
        out_specs=out_specs + [fixed((8, width))],
        scratch_shapes=[pltpu.VMEM((PACKED, width), f32)],
        compiler_params=room(),
        cost_estimate=cost(6e9, 20e6),
        name="back_norm",
    )(*grads, weights, values, row(gain), added, *more)


def back_project_body(g_ref, w_ref, o_ref):
    o_ref[...] = contract_cols(g_ref[...], w_ref[...]).astype(bf16)


def back_project(grads, weights):
    rows, width = weights.shape
    half = rows // 2
    return pl.pallas_call(
        back_project_body,
        out_shape=jax.ShapeDtypeStruct((PACKED, rows), bf16),
        grid=(2,),
        in_specs=[fixed((PACKED, width)), pl.BlockSpec((half, width), lambda i: (i, 0))],
        out_specs=pl.BlockSpec((PACKED, half), lambda i: (0, i)),
        compiler_params=room(),
        cost_estimate=cost(2e9, 5e6),
        name="back_project",
    )(grads, weights)


def layer(ring, tokens, counts, w_qkv, bias_q, bias_v, w_out, bias_out, w_up, bias_up, w_down, bias_down, gain_one, shift_one, gain_two, shift_two, cotangent):
    images, slots, width = tokens.shape
    group = ring.sizes["sz"] * ring.sizes["sc"]
    twins = group // images
    rows = w_qkv.shape[0]
    wide = w_down.shape[0] // rows
    ff = w_up.shape[1]

    slot = lax.broadcasted_iota(jnp.int32, (images, slots, 1), 1)
    marked = jnp.where(slot < counts[:, :, None], tokens, jnp.asarray(ABSENT, bf16))

    def back_pieces(pieces, own):
        pieces = jnp.stack([own] + [pieces[k] for k in everything])
        return pieces[:, 0], ring.swap(pieces[:, 1])

    def slots_of(array):
        return array.reshape(depth, 2, slots, width)

    depth = ring.sizes["sz"]
    outer = [k for k in range(1, depth) if k in (1, depth - 1)]
    inner = [k for k in range(1, depth) if k not in outer]
    everything = list(range(1, depth))

    small = [bias_q, bias_v, bias_out, bias_down, gain_one, shift_one, gain_two, shift_two]

    def arrays_of(sources):
        return [source[0] for source in sources]

    def with_arrays(sources, arrays):
        return [(array,) + source[1:] for array, source in zip(arrays, sources)]

    one = seed(w_qkv, small, bias_up)
    column = ring.spread(one, everything)
    stay, go = ring.blocks_for(marked, twins)
    came = ring.swap(go)
    cot_stay, go = ring.blocks_for(cotangent, twins)
    cot_came = ring.swap(go)
    one = ring.along(one, column)
    two = jnp.concatenate([w_out, w_up], axis=1)
    one, two, stay, came, cot_stay, cot_came = tie(one, two, stay, came, cot_stay, cot_came)

    one = ring.across(one)
    column = ring.spread(two, outer)
    pieces = ring.paired(stay, came)
    cot_pieces = ring.paired(cot_stay, cot_came)
    one_near = ring.flat([[half] for half in one])
    target = ring.target(width)
    one, one_near, two, column, pieces, cot_pieces, target = tie(one, one_near, two, column, pieces, cot_pieces, target)

    one_more = ring.plane(one)
    one_core = ring.swap(one_near)
    rest = ring.send(pieces, outer[:1])
    column.update(ring.spread(two, inner))
    two = ring.along(two, column)
    one_near, one_more, one_core, two, pieces, rest, cot_pieces = tie(one_near, one_more, one_core, two, pieces, rest, cot_pieces)

    one_more_core = ring.to_core(one_more)
    two = ring.across(two)
    rest.update(ring.send(pieces, outer[1:]))
    one_near, one_more, one_core, one_more_core, two, pieces, rest, three = tie(
        one_near, one_more, one_core, one_more_core, two, pieces, rest, w_down
    )

    two_core = ring.to_core([[half] for half in two])
    two_more = ring.plane(two)
    rest.update(ring.send(pieces, inner))
    full_qkv, vectors = ring.assemble(ring.near_flat_sources(one_near, one_core, one_more, one_more_core), [3 * width, SMALL])
    two, two_core, two_more, rest, full_qkv, vectors, three = tie(two, two_core, two_more, rest, full_qkv, vectors, three)

    column = ring.spread(three, everything)
    two_more_core = ring.to_core(two_more)
    image_slots = jnp.concatenate([pieces[0]] + [rest[k] for k in everything]).reshape(group * slots, width)
    vectors = vectors.reshape(ring.count, rows, SMALL).astype(f32)
    bu = vectors[:, 0, 128 : 128 + wide * rows].reshape(ff)
    bq, bv, bo, bd, g1, s1, g2, s2 = [vectors[:, k, :rows].reshape(width) for k in range(8)]
    here = (image_slots[:, :1].astype(f32) < 0.5 * ABSENT).reshape(group, slots)
    held = jnp.sum(here.astype(f32), axis=1)
    before = jnp.sum(jnp.where(np.tril(np.ones((group, group), bool), -1), held[None, :], 0.0), axis=1)
    rank = before[:, None] + lax.broadcasted_iota(jnp.int32, (group, slots), 1).astype(f32)
    rank = jnp.where(here, rank, -1.0).reshape(1, group * slots).astype(jnp.int32)
    packing = (rank == lax.broadcasted_iota(jnp.int32, (PACKED, group * slots), 0)).astype(bf16)
    tokens_f, normed = pack_norm(packing, image_slots, g1, s1)
    qkv_bias = halved(jnp.concatenate([bq, jnp.zeros((width,), f32), bv]))
    qkv = project(normed, full_qkv, qkv_bias)
    mixed, logs = attend(qkv)
    three = ring.along(three, column)
    two_more_core, three, mixed = tie(two_more_core, three, mixed)

    three = ring.across(three)
    cot_rest = ring.send(cot_pieces, outer)
    full_out, full_up = ring.assemble(ring.sources(two, two_core, two_more, two_more_core), [width, ff])
    residual, normed_two = out_norm(mixed, full_out, tokens_f, bo, g2, s2)
    three, normed_two, cot_rest = tie(three, normed_two, cot_rest)

    three_more = ring.plane(three)
    three_core = ring.to_core([[half] for half in three])
    cot_rest.update(ring.send(cot_pieces, inner))
    ranks = ring.far(lax.broadcasted_iota(jnp.int32, (ring.count,), 0))
    active, slope, active_far = rise(normed_two, full_up, bu, ranks)
    if active_far is None:
        active_far = ring.by_distance(active, ring.target(ff))
    mixed_far = ring.by_distance(mixed, target)
    two_far = ring.by_distance(normed_two, target)
    three, three_more, three_core, active, active_far, mixed_far, two_far, cot_rest = tie(
        three, three_more, three_core, active, active_far, mixed_far, two_far, cot_rest
    )

    three_more_core = ring.to_core(three_more)
    share = (lax.axis_index(("sz", "sc")) % twins == 0).astype(f32) if twins > 1 else None
    cot_slots = jnp.concatenate([cot_pieces[0]] + [cot_rest[k] for k in everything]).reshape(group * slots, width)
    grad_low, grad_bd = pack(packing, cot_slots)
    sent = weight_grad(active_far, 1, grad_low, share)
    three_more_core, sent, grad_low = tie(three_more_core, sent, grad_low)

    d = ring.swap(sent)
    (full_down,) = ring.assemble(ring.sources(three, three_core, three_more, three_more_core), [width])
    d, full_down = tie(d, full_down)

    d = ring.kept(active_far, grad_low, share, d)
    result = slots_of(land(active, full_down, residual, bd, packing))
    d, result = tie(d, result)

    d = ring.first(d)
    back = ring.send(result, inner, -1)
    hidden_low, grad_bu = fall(grad_low, full_down, slope)
    sent = weight_grad(two_far, 1, hidden_low, share)
    d, sent, back = tie(d, sent, back)

    d = ring.again(d)
    d, sent = tie(d, sent)

    d = ring.second(d)
    u = ring.swap(sent)
    back.update(ring.send(result, outer[:1], -1))
    grad_residual, residual_low, sums_two = back_norm([hidden_low], full_up, residual, g2, grad_low)
    d, u, residual_low, back = tie(d, u, residual_low, back)

    d = ring.last(d)
    u = ring.kept(two_far, hidden_low, share, u)
    sent = weight_grad(mixed_far, 1, residual_low, share)
    d, u, sent, residual_low, normed = tie(d, u, sent, residual_low, normed)

    u = ring.first(u)
    gone = ring.toward_some(d, outer)
    back.update(ring.send(result, outer[1:], -1))
    grad_mixed = back_project(residual_low, full_out)
    sent_out = sent
    half_grads = attend_back(qkv, logs, grad_mixed)
    normed_far = ring.by_distance(normed, target)
    u, sent_out, d, gone, grad_mixed, half_grads, back, normed_far = tie(
        u, sent_out, d, gone, grad_mixed, half_grads, back, normed_far
    )

    u = ring.again(u)
    u, sent_out, back, d, grad_mixed, half_grads = tie(u, sent_out, back, d, grad_mixed, half_grads)

    u = ring.second(u)
    gone.update(ring.toward_some(d, inner))
    o = ring.swap(sent_out)
    grads, grad_sums = attend_back(qkv, logs, grad_mixed, half_grads)
    sent = weight_grad(normed_far, 1, grads, share)
    u, o, sent, grads, back, d, gone = tie(u, o, sent, grads, back, d, gone)
    d = [d[0]] + [gone[k] for k in everything]

    u = ring.last(u)
    u, sent, grads = tie(u, sent, grads)

    later = ring.toward_some(u, outer)
    q = ring.swap(sent)
    grad_tokens, sums_one = back_norm([grads], full_qkv, tokens_f, g1, grad_residual, packing)
    grad_tokens = slots_of(grad_tokens)
    u, later, o, q, grads, grad_tokens, sums_one, back, d = tie(u, later, o, q, grads, grad_tokens, sums_one, back, d)

    sent_back = ring.send(grad_tokens, outer, -1)
    q = ring.kept(normed_far, grads, share, q)
    o = ring.reshaped(weight_grad(mixed_far, 0, residual_low, share, o))
    joined_sum = whole(grad_sums[0])
    grad_bq, grad_bv = joined_sum[:width], joined_sum[2 * width :]
    small = [grad_bq, grad_bv, sums_two[2], grad_bd, sums_one[0], sums_one[1], sums_two[0], sums_two[1]]
    small = [array.reshape(ring.count, rows) for array in small] + [grad_bu.reshape(ring.count, wide * rows)]
    small = jnp.concatenate(small, axis=1)
    small = (small if share is None else small * share).astype(bf16)
    near_first = (ranks[None, :] == lax.broadcasted_iota(jnp.int32, (ring.count, 1), 0)).astype(bf16)
    small = dot_float(near_first, small).astype(bf16)
    small = jnp.pad(small, ((0, 0), (0, rows * SMALL - small.shape[1]))).reshape(2, ring.count // 2 * rows, SMALL)
    q, o, small, u, sent_back, grad_tokens, back, d = tie(q, o, small, u, sent_back, grad_tokens, back, d)

    q = ring.first(q)
    sent_back.update(ring.send(grad_tokens, inner, -1))
    came = ring.swap(small[1])
    own = jnp.stack([result[0]] + [back[k] for k in everything])
    other = ring.swap(own[:, 1])
    q, came, sent_back, u, back, d, own, other = tie(q, came, sent_back, u, back, d, own, other)

    q = ring.again(q)
    small = ring.reshaped(total([small[0], came]).astype(bf16))
    o = ring.ready(jnp.concatenate([o, small], axis=-1))
    q, o, u, own, d = tie(q, o, u, own, d)

    q = ring.second(q)
    o = ring.first(o)
    later.update(ring.toward_some(u, inner))
    result = ring.images_of(own[:, 0], other, images, twins)
    result = jnp.where(slot < counts[:, :, None], result, jnp.asarray(0, bf16))
    o, later, result, q, d = tie(o, later, result, q, d)

    q = ring.last(q)
    o = ring.again(o)
    o, q, d = tie(o, q, d)

    q = ring.third(q)
    o = ring.second(o)
    u = [u[0]] + [later[k] for k in everything]
    grad_tokens, came = back_pieces(sent_back, grad_tokens[0])
    q, o, grad_tokens, came = tie(q, o, grad_tokens, came)

    o = ring.third(ring.last(o))
    grad_tokens = ring.images_of(grad_tokens, came, images, twins).astype(f32)

    sum_down, sum_up = total(d), total(u)
    o = total(o)
    sum_out = o[:, :width]
    sum_qkv = whole(total(q))
    small = o[:, width:].reshape(rows * SMALL)
    sum_bq, sum_bv, sum_bo, sum_bd, sum_g1, sum_s1, sum_g2, sum_s2 = [small[k * rows : (k + 1) * rows] for k in range(8)]
    sum_bu = small[8 * rows : (8 + wide) * rows]
    return (result, grad_tokens, sum_qkv, sum_bq, sum_bv, sum_out, sum_bo, sum_up, sum_bu, sum_down, sum_bd, sum_g1, sum_s1, sum_g2, sum_s2)


def solution(mesh):
    n_grp, n_seq = mesh.shape["grp"], mesh.shape["seq"]
    sizes = (n_grp // 2, 2, n_seq // 2, 2)
    fine = Mesh(mesh.devices.reshape(sizes), AXES)
    ring = Ring(sizes)
    grp, seq = AXES[:2], AXES[2:]
    by_token = P(grp, seq, None)
    rows, vec = P(AXES, None), P(AXES)
    in_specs = (by_token, P(grp, seq), rows, vec, vec, rows, vec, rows, vec, rows, vec, vec, vec, vec, vec, by_token)
    out_specs = (by_token, by_token, rows, vec, vec, rows, vec, rows, vec, rows, vec, vec, vec, vec, vec)

    def shards(*args):
        return layer(ring, *args)

    return jax.shard_map(shards, mesh=fine, in_specs=in_specs, out_specs=out_specs, check_vma=False)
```

```python
import jax
import jax.numpy as jnp
import numpy as np
from jax import lax
from jax.experimental import pallas as pl
from jax.experimental.pallas import tpu as pltpu
from jax.sharding import Mesh
from jax.sharding import PartitionSpec as P

H = 16
HD = 64
LENGTH = 577
PACKED = 592
EPSILON = 1e-06
NEGATIVE = -1e30
ABSENT = 100.0
SMALL = 256
AXES = ("gy", "gx", "sz", "sc")
ORDERS = (("gx", "gy"), ("gy", "gx"))

bf16 = jnp.bfloat16
f32 = jnp.float32


def norm_rows(values, gain_vec, shift_vec):
    row_mean = jnp.mean(values, axis=-1, keepdims=True)
    centred = values - row_mean
    row_var = jnp.mean(centred * centred, axis=-1, keepdims=True)
    return centred * lax.rsqrt(row_var + EPSILON) * gain_vec + shift_vec


def dot_float(left, right):
    return jnp.dot(left, right, preferred_element_type=f32)


def contract_rows(left, right):
    return lax.dot_general(left, right, (((0,), (0,)), ((), ())), preferred_element_type=f32)


def contract_cols(left, right):
    return lax.dot_general(left, right, (((1,), (1,)), ((), ())), preferred_element_type=f32)


def room(mib=50):
    return pltpu.CompilerParams(vmem_limit_bytes=mib * 2**20)


HINT = 0.02


def cost(flops, bytes_accessed, transcendentals=0):
    return pl.CostEstimate(
        flops=int(HINT * flops), bytes_accessed=int(HINT * bytes_accessed), transcendentals=int(HINT * transcendentals)
    )


def shifted(array, axis, size, step):
    return lax.ppermute(array, axis, [(i, (i + step) % size) for i in range(size)])


def pick(array, index, axis):
    return lax.dynamic_index_in_dim(array, index, axis, keepdims=False)


class Ring:
    def __init__(self, sizes):
        self.sizes = dict(zip(AXES, sizes))
        self.count = int(np.prod(sizes))

    def place(self):
        return {axis: lax.axis_index(axis) for axis in AXES}

    def others(self, array, axis):
        size = self.sizes[axis]
        return [shifted(array, axis, size, step) for step in range(1, size)]

    def others_from(self, array, axis, steps):
        size = self.sizes[axis]
        return [shifted(array, axis, size, step) for step in steps]

    def along(self, shard, columns):
        cut = shard.shape[0] // 2
        size = self.sizes["sz"]
        columns = [shard] + [columns[k] for k in range(1, size)]
        here = lax.axis_index("sz")
        ordered = [lax.select_n((here - k) % size, *columns) if size > 2 else jnp.where(here == k, *columns) for k in range(size)]
        return [jnp.stack([c[:cut] for c in ordered]), jnp.stack([c[cut:] for c in ordered])]

    def spread(self, shard, steps):
        return {k: shifted(shard, "sz", self.sizes["sz"], k) for k in steps}

    def across(self, halves):
        return [jnp.stack([half] + self.others(half, order[0])) for half, order in zip(halves, ORDERS)]

    def plane(self, halves):
        return [self.others(half, order[1]) for half, order in zip(halves, ORDERS)]

    def to_core(self, groups):
        return [[shifted(group, "sc", 2, 1) for group in part] for part in groups]

    def sources(self, first, traded_first, second, traded_second):
        found = []
        for part in range(2):
            kinds = ([first[part]] + second[part], traded_first[part] + traded_second[part])
            for turn, groups in enumerate(kinds):
                found += [(g, turn, [(part, step, one) for one in range(g.shape[0])]) for step, g in enumerate(groups)]
        return found

    def flat(self, groups):
        return jnp.concatenate([group for part in groups for group in part], axis=0)

    def labels(self, far):
        sizes = self.sizes
        found = []
        for part in range(2):
            for step in range(1, sizes[ORDERS[part][1]]) if far else [0]:
                found += [(part, step, one) for one in range(sizes[ORDERS[part][0]])]
        return found

    def near_flat_sources(self, near, near_core, second, traded_second):
        found = [(near, 0, self.labels(False)), (near_core, 1, self.labels(False))]
        for turn, groups in enumerate((second, traded_second)):
            for part in range(2):
                for step, g in enumerate(groups[part]):
                    found.append((g, turn, [(part, step + 1, one) for one in range(g.shape[0])]))
        return found

    def assemble(self, sources, widths):
        place = self.place()
        sizes = self.sizes
        cut, width = sources[0][0].shape[-2:]
        depth = sizes["sz"]
        planes, kinds, parts, arrays, counts = [], [], [], [], []
        for group, turn, labels in sources:
            arrays.append(group)
            counts.append(len(labels))
            for part, step, one in labels:
                order = ORDERS[part]
                at = {order[1]: (place[order[1]] - step) % sizes[order[1]], order[0]: (place[order[0]] - one) % sizes[order[0]]}
                planes.append(at["gy"] * sizes["gx"] + at["gx"])
                kinds.append((place["sc"] - turn) % 2)
                parts.append(part)
        table = jnp.stack(planes + kinds).astype(jnp.int32)
        many = len(planes)
        starts = np.concatenate([[0], np.cumsum(widths)])

        def body(table_ref, *refs):
            ins = refs[: len(counts)]
            outs = refs[len(counts) : -3]
            held, came, left = refs[-3:]
            arrivals = []
            for ref, count in zip(ins, counts):
                for k in range(count):
                    n = len(arrivals)
                    arrivals.append(pltpu.make_async_copy(ref.at[k], held.at[n], came.at[n]))
            for copy in arrivals:
                copy.start()
            departures = []
            for n, copy in enumerate(arrivals):
                copy.wait()
                for i, out in enumerate(outs):
                    window = held.at[n, :, :, pl.ds(int(starts[i]), widths[i])]
                    target = out.at[table_ref[n], :, table_ref[many + n], parts[n]]
                    leave = pltpu.make_async_copy(window, target, left.at[n, i])
                    leave.start()
                    departures.append(leave)
            for copy in departures:
                copy.wait()

        planes_all = sizes["gy"] * sizes["gx"]
        outs = pl.pallas_call(
            body,
            out_shape=[jax.ShapeDtypeStruct((planes_all, depth, 2, 2, cut, w), bf16) for w in widths],
            grid_spec=pltpu.PrefetchScalarGridSpec(
                num_scalar_prefetch=1,
                grid=(1,),
                in_specs=[pl.BlockSpec(memory_space=pl.ANY)] * len(counts),
                out_specs=[pl.BlockSpec(memory_space=pl.ANY)] * len(widths),
                scratch_shapes=[
                    pltpu.VMEM((many, depth, cut, width), bf16),
                    pltpu.SemaphoreType.DMA((many,)),
                    pltpu.SemaphoreType.DMA((many, len(widths))),
                ],
            ),
            compiler_params=room(),
            cost_estimate=cost(0, 4 * self.count * 2 * cut * width),
            name="assemble",
        )(table, *arrays)
        return [out.reshape(self.count * 2 * cut, w) for out, w in zip(outs, widths)]

    def far(self, device):
        place = self.place()
        sizes = self.sizes
        index, out = device, {}
        for axis in AXES[::-1]:
            out[axis] = (index % sizes[axis] - place[axis]) % sizes[axis]
            index = index // sizes[axis]
        return ((out["sc"] * sizes["gy"] + out["gy"]) * sizes["gx"] + out["gx"]) * sizes["sz"] + out["sz"]

    def target(self, width):
        block = width // self.count
        row = lax.broadcasted_iota(jnp.int32, (width, 1), 0)
        return self.far(row // block) * block + row % block

    def by_distance(self, array, target):
        tokens, width = array.shape
        half = width // 2

        def body(x_ref, t_ref, o_ref):
            columns = lax.broadcasted_iota(jnp.int32, (width, half), 1) + half * pl.program_id(0)
            pick_columns = jnp.where(t_ref[...] == columns, 1.0, 0.0).astype(bf16)
            o_ref[0] = dot_float(x_ref[...], pick_columns).astype(bf16)

        return pl.pallas_call(
            body,
            out_shape=jax.ShapeDtypeStruct((2, tokens, half), bf16),
            grid=(2,),
            in_specs=[pl.BlockSpec((tokens, width), lambda i: (0, 0)), pl.BlockSpec((width, 1), lambda i: (0, 0))],
            out_specs=pl.BlockSpec((1, tokens, half), lambda i: (i, 0, 0)),
            compiler_params=room(),
            cost_estimate=cost(2 * tokens * width * width, 4 * tokens * width),
            name="by_distance",
        )(array, target)

    def blocks_for(self, array, twins):
        place = self.place()
        size = self.sizes["sz"]
        out = []
        for turn in range(2):
            found = [((place["sz"] + k) % size * 2 + (place["sc"] + turn) % 2) // twins for k in range(size)]
            out.append(jnp.stack([pick(array, image, 0) for image in found]))
        return out

    def paired(self, stay, came):
        return [jnp.stack([stay[k], came[k]]) for k in range(self.sizes["sz"])]

    def send(self, pieces, steps, sign=1):
        return {k: shifted(pieces[k], "sz", self.sizes["sz"], sign * k) for k in steps}

    def images_of(self, own, came, images, twins):
        place = self.place()
        size = self.sizes["sz"]
        both = jnp.stack([own, came])
        both = both.reshape((2 * size,) + both.shape[2:])
        out = []
        for image in range(images):
            device = image * twins
            out.append(pick(both, (device % 2 - place["sc"]) % 2 * size + (device // 2 - place["sz"]) % size, 0))
        return jnp.stack(out)

    def swap(self, sent):
        return shifted(sent, "sc", 2, 1)

    def reshaped(self, out):
        sizes = self.sizes
        return out.reshape(sizes["gy"], sizes["gx"], sizes["sz"], out.shape[0] // (self.count // 2), out.shape[1])

    def kept(self, left, right, share, came):
        cut = left.shape[2] // (self.count // 2) // 2
        if cut % 16 == 0:
            return weight_grad(left, 0, right, share, came, self.sizes)
        return self.ready(self.reshaped(weight_grad(left, 0, right, share, came)))

    def toward(self, arrays, axis):
        size = self.sizes[axis]
        return [arrays[0]] + [shifted(arrays[k], axis, size, k) for k in range(1, size)]

    def toward_some(self, parts, steps):
        return {k: shifted(parts[k], "sz", self.sizes["sz"], k) for k in steps}

    def ready(self, sums):
        cut = sums.shape[3] // 2
        upper = [sums[k, :, :, :cut] for k in range(self.sizes["gy"])]
        lower = [sums[:, k, :, cut:] for k in range(self.sizes["gx"])]
        return upper, lower

    def first(self, pair):
        return self.toward(pair[0], "gy"), self.toward(pair[1], "gx")

    def again(self, pair):
        return tuple(
            [total([t[k] for t in terms]).astype(bf16) for k in range(self.sizes[axis])]
            for terms, axis in zip(pair, ("gx", "gy"))
        )

    def second(self, pair):
        return self.toward(pair[0], "gx"), self.toward(pair[1], "gy")

    def last(self, pair):
        return [
            jnp.concatenate([total([t[k] for t in terms]) for terms in pair], axis=0).astype(bf16)
            for k in range(self.sizes["sz"])
        ]

    def third(self, parts):
        return self.toward(parts, "sz")


def weight_grad(left, kind, right, share, came=None, sizes=None):
    tokens, columns = right.shape
    rows = left.shape[2]
    tiled = rows > 512
    parts = 1
    if sizes is not None:
        ny, nx, nz = sizes["gy"], sizes["gx"], sizes["sz"]
        parts = ny * nx
        block = rows // (parts * nz)
        cut = block // 2
    if tiled:
        tall, broad = rows // (parts if sizes is not None else rows // 512), columns
        steps = rows // tall
        at = lambda i: (i, 0)
        left_at, right_at = (lambda i: (kind, 0, i)), (lambda i: (0, 0))
    else:
        tall, broad = rows, next(w for w in (1024, 768, 512, 128) if columns % w == 0)
        steps = columns // broad
        at = lambda i: (0, i)
        left_at, right_at = (lambda i: (kind, 0, 0)), (lambda i: (0, i))
    others = [] if came is None else [came.reshape(rows, columns)]
    if share is not None:
        others.append(share.reshape(1, 1))
    given = 2 + len(others)

    def body(*refs):
        outs = refs[given:]
        out = contract_rows(refs[0][0], refs[1][...])
        if share is not None:
            out = out * refs[given - 1][...]
        if came is not None:
            out = out + refs[2][...].astype(f32)
        if sizes is None:
            outs[0][...] = out.astype(bf16)
        elif tiled:
            i = pl.program_id(0)
            out = out.astype(bf16).reshape(nz, block, broad)
            for k in range(ny):

                @pl.when(i // nx == k)
                def _(k=k):
                    outs[k][0] = out[:, :cut]

            for k in range(nx):

                @pl.when(i % nx == k)
                def _(k=k):
                    outs[ny + k][0] = out[:, cut:]

        else:
            out = out.astype(bf16).reshape(ny, nx, nz, block, broad)
            for k in range(ny):
                outs[k][...] = out[k, :, :, :cut]
            for k in range(nx):
                outs[ny + k][...] = out[:, k, :, cut:]

    specs = [pl.BlockSpec((1, tokens, tall), left_at), pl.BlockSpec((tokens, broad), right_at)]
    if came is not None:
        specs.append(pl.BlockSpec((tall, broad), at))
    if share is not None:
        specs.append(pl.BlockSpec((1, 1), lambda i: (0, 0)))
    if sizes is None:
        shapes, out_specs = [(rows, columns)], [pl.BlockSpec((tall, broad), at)]
    else:
        shapes = [(nx, nz, cut, columns)] * ny + [(ny, nz, cut, columns)] * nx
        if tiled:
            out_specs = [
                pl.BlockSpec((1, nz, cut, broad), lambda i, k=k: (jnp.clip(i - k * nx, 0, nx - 1), 0, 0, 0)) for k in range(ny)
            ]
            out_specs += [pl.BlockSpec((1, nz, cut, broad), lambda i, k=k: (jnp.maximum(i - k, 0) // nx, 0, 0, 0)) for k in range(nx)]
        else:
            out_specs = [pl.BlockSpec(shape[:3] + (broad,), lambda i: (0, 0, 0, i)) for shape in shapes]
    outs = pl.pallas_call(
        body,
        out_shape=[jax.ShapeDtypeStruct(shape, bf16) for shape in shapes],
        grid=(steps,),
        in_specs=specs,
        out_specs=out_specs,
        compiler_params=room(),
        cost_estimate=cost(2 * tokens * rows * columns, 4 * rows * columns),
        name="weight_grad",
    )(left, right, *others)
    return outs[0] if sizes is None else (outs[:ny], outs[ny:])


def total(arrays):
    out = arrays[0].astype(f32)
    for array in arrays[1:]:
        out = out + array.astype(f32)
    return out


def tie(*values):
    return lax.optimization_barrier(values)


def of_head(part):
    return lax.broadcasted_iota(jnp.int32, (1, 2 * HD), 1) // HD == part


def mask_tail(scores, fill):
    start = LENGTH // 8 * 8
    row = lax.broadcasted_iota(jnp.int32, (PACKED - start, PACKED), 0)
    tail = jnp.where(row < LENGTH - start, scores[start:], fill)
    return jnp.concatenate([scores[:start], tail], axis=0)


def flip(array):
    return array.astype(f32).T.astype(bf16)


def attend_body(q_ref, k_ref, v_ref, o_ref, l_ref):
    query, key = q_ref[...] * jnp.asarray(HD**-0.5, bf16), k_ref[...]
    value_t = flip(v_ref[...])
    mixed, logs = [], []
    for part in range(2):
        scores = contract_cols(jnp.where(of_head(part), key, 0), query)
        scores = mask_tail(scores, NEGATIVE)
        top = jnp.max(scores, axis=0, keepdims=True)
        exponent = jnp.exp(scores - top)
        total = jnp.sum(exponent, axis=0, keepdims=True)
        out = dot_float(value_t[HD * part : HD * (part + 1)], exponent.astype(bf16))
        mixed.append(out * (1.0 / total))
        logs.append(top + jnp.log(total))
    o_ref[...] = jnp.concatenate(mixed, axis=0).T.astype(bf16)
    l_ref[...] = jnp.concatenate(logs + [jnp.zeros((6, PACKED), f32)], axis=0)


PAIR = (PACKED, 2 * HD)
PAIRS = H // 2
CUT = PAIRS // 2


def kind_spec(kind, base=0):
    return pl.BlockSpec(PAIR, lambda i: (0, (i + base) // CUT * 3 * CUT + (i + base) % CUT + kind * CUT))


def pair_spec(base=0):
    return pl.BlockSpec(PAIR, lambda i: (0, i + base))


def log_spec(base=0):
    return pl.BlockSpec((8, PACKED), lambda i: (i + base, 0))


def halved(array):
    return array.reshape(-1, 3, 2, H * HD // 2).swapaxes(1, 2).reshape(array.shape)


def whole(array):
    return array.reshape(-1, 2, 3, H * HD // 2).swapaxes(1, 2).reshape(array.shape)


def attend(qkv):
    return pl.pallas_call(
        attend_body,
        out_shape=[
            jax.ShapeDtypeStruct((PACKED, H * HD), bf16),
            jax.ShapeDtypeStruct((8 * PAIRS, PACKED), f32),
        ],
        grid=(PAIRS,),
        in_specs=[kind_spec(0), kind_spec(1), kind_spec(2)],
        out_specs=[pair_spec(), log_spec()],
        compiler_params=room(),
        cost_estimate=cost(12e9, 8 * qkv.size, PACKED * PACKED * H),
        name="attend",
    )(qkv, qkv, qkv)


def attend_back_body(q_ref, k_ref, v_ref, l_ref, g_ref, *rest):
    d_ref, s_ref = rest[-2:]
    base = 0
    if len(rest) == 4:
        base = rest[0].shape[1]

        @pl.when(pl.program_id(0) == 0)
        def _():
            d_ref[:, :base] = rest[0][...]
            s_ref[:, :base] = rest[1][...]

    scale = jnp.asarray(HD**-0.5, bf16)
    query, key, value, grad = q_ref[...] * scale, k_ref[...], v_ref[...], g_ref[...]
    key_t = flip(key)
    grad_query, grad_key, grad_value = [], [], []
    for part in range(2):
        mask = of_head(part)
        scores = contract_cols(jnp.where(mask, key, 0), query)
        soft = mask_tail(jnp.exp(scores - l_ref[part : part + 1]), 0.0)
        grad_soft = contract_cols(jnp.where(mask, value, 0), grad)
        delta = jnp.sum(soft * grad_soft, axis=0, keepdims=True)
        grad_scores = (soft * (grad_soft - delta)).astype(bf16)
        grad_value.append(dot_float(soft.astype(bf16), grad))
        grad_key.append(dot_float(grad_scores, query))
        grad_query.append(dot_float(key_t[HD * part : HD * (part + 1)], grad_scores))
    first = of_head(0)
    grads = (
        jnp.concatenate(grad_query, axis=0).T * HD**-0.5,
        jnp.where(first, grad_key[0], grad_key[1]),
        jnp.where(first, grad_value[0], grad_value[1]),
    )
    for kind, array in enumerate(grads):
        start = pl.multiple_of(base + (pl.program_id(0) + kind * CUT) * 2 * HD, 2 * HD)
        low = array.astype(bf16)
        d_ref[:, pl.ds(start, 2 * HD)] = low
        s_ref[:, pl.ds(start, 2 * HD)] = jnp.sum(low.astype(f32), axis=0, keepdims=True)


def attend_back(qkv, logs, grad_mixed, before=()):
    base = CUT if before else 0
    width = qkv.shape[1] // (1 if before else 2)
    return pl.pallas_call(
        attend_back_body,
        out_shape=[jax.ShapeDtypeStruct((PACKED, width), bf16), jax.ShapeDtypeStruct((1, width), f32)],
        grid=(CUT,),
        in_specs=[kind_spec(0, base), kind_spec(1, base), kind_spec(2, base), log_spec(base), pair_spec(base)]
        + [pl.BlockSpec(array.shape, lambda i: (0, 0)) for array in before],
        out_specs=[pl.BlockSpec((PACKED, width), lambda i: (0, 0)), pl.BlockSpec((1, width), lambda i: (0, 0))],
        compiler_params=room(),
        cost_estimate=cost(12e9, 8 * qkv.size, PACKED * PACKED * H // 2),
        name="attend_back",
    )(qkv, qkv, qkv, logs, grad_mixed, *before)


def rise(normed, weights, bias, ranks):
    width, ff = weights.shape
    step = ff // 4
    count = ranks.shape[0]
    block = ff // count
    inside = step // block
    whole_tiles = block % 128 == 0

    def body(rank_ref, x_ref, w_ref, b_ref, active_ref, slope_ref, *rest):
        i = pl.program_id(0)
        hidden = dot_float(x_ref[...], w_ref[...]) + b_ref[...]
        share = 0.5 * (1.0 + lax.erf(hidden * np.float32(np.sqrt(0.5))))
        active = (hidden * share).astype(bf16)
        active_ref[...] = active
        bell = jnp.exp(hidden * hidden * -0.5) * np.float32(1.0 / np.sqrt(2.0 * np.pi))
        slope_ref[...] = share + hidden * bell
        if not whole_tiles:
            return
        far_ref, held, sems = rest
        held[i % 2] = active

        def copies(turn):
            out = []
            for k in range(inside):
                rank = rank_ref[turn * inside + k]
                start = pl.multiple_of(rank % (count // 2) * block, block)
                window = held.at[turn % 2, :, pl.ds(k * block, block)]
                out.append(pltpu.make_async_copy(window, far_ref.at[rank // (count // 2), :, pl.ds(start, block)], sems.at[turn % 2, k]))
            return out

        for copy in copies(i):
            copy.start()

        @pl.when(i > 0)
        def _():
            for copy in copies(i - 1):
                copy.wait()

        @pl.when(i == 3)
        def _():
            for copy in copies(i):
                copy.wait()

    shapes = [jax.ShapeDtypeStruct((PACKED, ff), bf16), jax.ShapeDtypeStruct((PACKED, ff), f32)]
    specs = [pl.BlockSpec((PACKED, step), lambda i, t: (0, i))] * 2
    scratch = []
    if whole_tiles:
        shapes.append(jax.ShapeDtypeStruct((2, PACKED, ff // 2), bf16))
        specs.append(pl.BlockSpec(memory_space=pl.ANY))
        scratch = [pltpu.VMEM((2, PACKED, step), bf16), pltpu.SemaphoreType.DMA((2, inside))]
    outs = pl.pallas_call(
        body,
        out_shape=shapes,
        grid_spec=pltpu.PrefetchScalarGridSpec(
            num_scalar_prefetch=1,
            grid=(4,),
            in_specs=[
                pl.BlockSpec((PACKED, width), lambda i, t: (0, 0)),
                pl.BlockSpec((width, step), lambda i, t: (0, i)),
                pl.BlockSpec((1, step), lambda i, t: (0, i)),
            ],
            out_specs=specs,
            scratch_shapes=scratch,
        ),
        compiler_params=room(),
        cost_estimate=cost(12e9, 30e6, PACKED * ff * 2),
        name="rise",
    )(ranks, normed, weights, bias.reshape(1, ff))
    return outs if whole_tiles else (outs[0], outs[1], None)


def fall_body(g_ref, w_ref, slope_ref, out_ref, sum_ref):
    grad = (contract_cols(g_ref[...], w_ref[...]) * slope_ref[...]).astype(bf16)
    out_ref[...] = grad
    sum_ref[...] = jnp.sum(grad.astype(f32), axis=0, keepdims=True)


def fall(grads, weights, slope):
    ff, width = weights.shape
    step = ff // 4
    return pl.pallas_call(
        fall_body,
        out_shape=[jax.ShapeDtypeStruct((PACKED, ff), bf16), jax.ShapeDtypeStruct((1, ff), f32)],
        grid=(4,),
        in_specs=[
            pl.BlockSpec((PACKED, width), lambda i: (0, 0)),
            pl.BlockSpec((step, width), lambda i: (i, 0)),
            pl.BlockSpec((PACKED, step), lambda i: (0, i)),
        ],
        out_specs=[pl.BlockSpec((PACKED, step), lambda i: (0, i)), pl.BlockSpec((1, step), lambda i: (0, i))],
        compiler_params=room(),
        cost_estimate=cost(10e9, 25e6),
        name="fall",
    )(grads, weights, slope)


def project_body(x_ref, w_ref, b_ref, out_ref):
    out_ref[...] = (dot_float(x_ref[...], w_ref[...]) + b_ref[...]).astype(bf16)


def project(left, weights, bias):
    width, columns = weights.shape
    step = columns // 3
    return pl.pallas_call(
        project_body,
        out_shape=jax.ShapeDtypeStruct((PACKED, columns), bf16),
        grid=(3,),
        in_specs=[
            pl.BlockSpec((PACKED, width), lambda i: (0, 0)),
            pl.BlockSpec((width, step), lambda i: (0, i)),
            pl.BlockSpec((1, step), lambda i: (0, i)),
        ],
        out_specs=pl.BlockSpec((PACKED, step), lambda i: (0, i)),
        compiler_params=room(),
        cost_estimate=cost(6e9, 12e6),
        name="project",
    )(left, weights, bias.reshape(1, columns))


def row(vector):
    return vector.reshape(1, -1)


def fixed(shape):
    return pl.BlockSpec(shape, lambda i: (0,) * len(shape))


def seed(weights, vectors, long):
    rows, width = weights.shape
    half = width // 6

    def body(w_ref, *refs):
        out_ref = refs[-1]
        for k in range(6):
            out_ref[:, k * half : (k + 1) * half] = w_ref[:, pl.ds((k % 3 * 2 + k // 3) * half, half)]
        out_ref[:, width:] = jnp.zeros((rows, SMALL), bf16)
        for k in range(len(vectors)):
            out_ref[k : k + 1, width : width + rows] = refs[k][...]
        out_ref[0:1, width + 128 : width + 128 + long.shape[0]] = refs[len(vectors)][...]

    return pl.pallas_call(
        body,
        out_shape=jax.ShapeDtypeStruct((rows, width + SMALL), bf16),
        cost_estimate=cost(0, 1e6),
        name="seed",
    )(weights, *[row(v) for v in vectors], row(long))


def pack_norm_body(p_ref, x_ref, g_ref, s_ref, t_ref, n_ref):
    tokens = dot_float(p_ref[...], x_ref[...])
    t_ref[...] = tokens
    n_ref[...] = norm_rows(tokens, g_ref[...], s_ref[...]).astype(bf16)


def pack_norm(packing, slots, gain, shift):
    count, width = slots.shape
    half = PACKED // 2
    by_row = pl.BlockSpec((half, width), lambda i: (i, 0))
    return pl.pallas_call(
        pack_norm_body,
        out_shape=[jax.ShapeDtypeStruct((PACKED, width), f32), jax.ShapeDtypeStruct((PACKED, width), bf16)],
        grid=(2,),
        in_specs=[pl.BlockSpec((half, count), lambda i: (i, 0)), fixed((count, width)), fixed((1, width)), fixed((1, width))],
        out_specs=[by_row, by_row],
        compiler_params=room(),
        cost_estimate=cost(1e9, 8e6),
        name="pack_norm",
    )(packing, slots, row(gain), row(shift))


def pack_body(p_ref, x_ref, o_ref, s_ref):
    low = dot_float(p_ref[...], x_ref[...]).astype(bf16)
    o_ref[...] = low
    s_ref[...] = jnp.sum(low.astype(f32), axis=0, keepdims=True)


def pack(packing, slots):
    count, width = slots.shape
    half = width // 2
    return pl.pallas_call(
        pack_body,
        out_shape=[jax.ShapeDtypeStruct((PACKED, width), bf16), jax.ShapeDtypeStruct((1, width), f32)],
        grid=(2,),
        in_specs=[fixed((PACKED, count)), pl.BlockSpec((count, half), lambda i: (0, i))],
        out_specs=[pl.BlockSpec((PACKED, half), lambda i: (0, i)), pl.BlockSpec((1, half), lambda i: (0, i))],
        compiler_params=room(),
        cost_estimate=cost(1e9, 4e6),
        name="pack",
    )(packing, slots)


def out_norm_body(m_ref, w_ref, t_ref, b_ref, g_ref, s_ref, r_ref, n_ref):
    residual = t_ref[...] + dot_float(m_ref[...], w_ref[...]) + b_ref[...]
    r_ref[...] = residual
    n_ref[...] = norm_rows(residual, g_ref[...], s_ref[...]).astype(bf16)


def out_norm(mixed, weights, tokens, bias, gain, shift):
    width = weights.shape[1]
    half = PACKED // 2
    by_row = pl.BlockSpec((half, width), lambda i: (i, 0))
    vec = fixed((1, width))
    return pl.pallas_call(
        out_norm_body,
        out_shape=[jax.ShapeDtypeStruct((PACKED, width), f32), jax.ShapeDtypeStruct((PACKED, width), bf16)],
        grid=(2,),
        in_specs=[by_row, fixed(weights.shape), by_row, vec, vec, vec],
        out_specs=[by_row, by_row],
        compiler_params=room(),
        cost_estimate=cost(2e9, 8e6),
        name="out_norm",
    )(mixed, weights, tokens, row(bias), row(gain), row(shift))


def land_body(a_ref, w_ref, r_ref, b_ref, p_ref, o_ref, sum_ref):
    i = pl.program_id(0)
    part = dot_float(a_ref[...], w_ref[...])

    @pl.when(i == 0)
    def _():
        sum_ref[...] = part + r_ref[...] + b_ref[...]

    @pl.when(i > 0)
    def _():
        sum_ref[...] += part

    @pl.when(i == pl.num_programs(0) - 1)
    def _():
        o_ref[...] = contract_rows(p_ref[...], sum_ref[...].astype(bf16)).astype(bf16)


def land(active, weights, residual, bias, packing):
    ff, width = weights.shape
    step = ff // 4
    count = packing.shape[1]
    return pl.pallas_call(
        land_body,
        out_shape=jax.ShapeDtypeStruct((count, width), bf16),
        grid=(4,),
        in_specs=[
            pl.BlockSpec((PACKED, step), lambda i: (0, i)),
            pl.BlockSpec((step, width), lambda i: (i, 0)),
            fixed((PACKED, width)),
            fixed((1, width)),
            fixed((PACKED, count)),
        ],
        out_specs=fixed((count, width)),
        scratch_shapes=[pltpu.VMEM((PACKED, width), f32)],
        compiler_params=room(),
        cost_estimate=cost(6e9, 14e6),
        name="land",
    )(active, weights, residual, row(bias), packing)


def back_norm(grads, weights, values, gain, added, packing=None):
    width = weights.shape[0]
    step = weights.shape[1] // (4 if len(grads) == 1 else len(grads))
    steps = weights.shape[1] // step
    count = len(grads)

    def body(*refs):
        g_refs, (w_ref, x_ref, gain_ref, add_ref), rest = refs[:count], refs[count : count + 4], refs[count + 4 :]
        sum_ref = rest[-1]
        i = pl.program_id(0)
        for k, g_ref in enumerate(g_refs):

            @pl.when((i == k) if count > 1 else (i >= 0))
            def _(g_ref=g_ref, k=k):
                part = contract_cols(g_ref[...], w_ref[...])

                @pl.when(i == 0)
                def _():
                    sum_ref[...] = part

                @pl.when(i > 0)
                def _():
                    sum_ref[...] += part

        @pl.when(i == steps - 1)
        def _():
            back = sum_ref[...]
            values = x_ref[...]
            centred = values - jnp.mean(values, axis=-1, keepdims=True)
            scale = lax.rsqrt(jnp.mean(centred * centred, axis=-1, keepdims=True) + EPSILON)
            normed = centred * scale
            scaled = back * gain_ref[...]
            inner = jnp.mean(scaled * normed, axis=-1, keepdims=True)
            out = (scaled - jnp.mean(scaled, axis=-1, keepdims=True) - normed * inner) * scale + add_ref[...].astype(f32)
            low = out.astype(bf16)
            if packing is None:
                out_ref, low_ref, sums_ref = rest[:3]
                out_ref[...] = out
                low_ref[...] = low
            else:
                p_ref, low_ref, sums_ref = rest[:3]
                low_ref[...] = contract_rows(p_ref[...], low).astype(bf16)
            sums = [jnp.sum(a, axis=0, keepdims=True) for a in (back * normed, back, low.astype(f32))]
            sums_ref[...] = jnp.concatenate(sums + [jnp.zeros((5, width), f32)], axis=0)

    full = fixed((PACKED, width))
    if packing is None:
        shapes = [jax.ShapeDtypeStruct((PACKED, width), f32), jax.ShapeDtypeStruct((PACKED, width), bf16)]
        out_specs, more_specs, more = [full, full], [], []
    else:
        shapes = [jax.ShapeDtypeStruct((packing.shape[1], width), bf16)]
        out_specs, more_specs, more = [fixed(shapes[0].shape)], [fixed(packing.shape)], [packing]
    g_spec = fixed((PACKED, step)) if count > 1 else pl.BlockSpec((PACKED, step), lambda i: (0, i))
    return pl.pallas_call(
        body,
        out_shape=shapes + [jax.ShapeDtypeStruct((8, width), f32)],
        grid=(steps,),
        in_specs=[g_spec] * count + [pl.BlockSpec((width, step), lambda i: (0, i)), full, fixed((1, width)), full] + more_specs,
        out_specs=out_specs + [fixed((8, width))],
        scratch_shapes=[pltpu.VMEM((PACKED, width), f32)],
        compiler_params=room(),
        cost_estimate=cost(6e9, 20e6),
        name="back_norm",
    )(*grads, weights, values, row(gain), added, *more)


def back_project_body(g_ref, w_ref, o_ref):
    o_ref[...] = contract_cols(g_ref[...], w_ref[...]).astype(bf16)


def back_project(grads, weights):
    rows, width = weights.shape
    half = rows // 2
    return pl.pallas_call(
        back_project_body,
        out_shape=jax.ShapeDtypeStruct((PACKED, rows), bf16),
        grid=(2,),
        in_specs=[fixed((PACKED, width)), pl.BlockSpec((half, width), lambda i: (i, 0))],
        out_specs=pl.BlockSpec((PACKED, half), lambda i: (0, i)),
        compiler_params=room(),
        cost_estimate=cost(2e9, 5e6),
        name="back_project",
    )(grads, weights)


def layer(ring, tokens, counts, w_qkv, bias_q, bias_v, w_out, bias_out, w_up, bias_up, w_down, bias_down, gain_one, shift_one, gain_two, shift_two, cotangent):
    images, slots, width = tokens.shape
    group = ring.sizes["sz"] * ring.sizes["sc"]
    twins = group // images
    rows = w_qkv.shape[0]
    wide = w_down.shape[0] // rows
    ff = w_up.shape[1]

    slot = lax.broadcasted_iota(jnp.int32, (images, slots, 1), 1)
    marked = jnp.where(slot < counts[:, :, None], tokens, jnp.asarray(ABSENT, bf16))

    def back_pieces(pieces, own):
        pieces = jnp.stack([own] + [pieces[k] for k in everything])
        return pieces[:, 0], ring.swap(pieces[:, 1])

    def slots_of(array):
        return array.reshape(depth, 2, slots, width)

    depth = ring.sizes["sz"]
    outer = [k for k in range(1, depth) if k in (1, depth - 1)]
    inner = [k for k in range(1, depth) if k not in outer]
    everything = list(range(1, depth))

    small = [bias_q, bias_v, bias_out, bias_down, gain_one, shift_one, gain_two, shift_two]

    def arrays_of(sources):
        return [source[0] for source in sources]

    def with_arrays(sources, arrays):
        return [(array,) + source[1:] for array, source in zip(arrays, sources)]

    one = seed(w_qkv, small, bias_up)
    column = ring.spread(one, everything)
    stay, go = ring.blocks_for(marked, twins)
    came = ring.swap(go)
    cot_stay, go = ring.blocks_for(cotangent, twins)
    cot_came = ring.swap(go)
    one = ring.along(one, column)
    two = jnp.concatenate([w_out, w_up], axis=1)
    one, two, stay, came, cot_stay, cot_came = tie(one, two, stay, came, cot_stay, cot_came)

    one = ring.across(one)
    column = ring.spread(two, outer)
    pieces = ring.paired(stay, came)
    cot_pieces = ring.paired(cot_stay, cot_came)
    one_near = ring.flat([[half] for half in one])
    target = ring.target(width)
    one, one_near, two, column, pieces, cot_pieces, target = tie(one, one_near, two, column, pieces, cot_pieces, target)

    one_more = ring.plane(one)
    one_core = ring.swap(one_near)
    rest = ring.send(pieces, outer[:1])
    column.update(ring.spread(two, inner))
    two = ring.along(two, column)
    one_near, one_more, one_core, two, pieces, rest, cot_pieces = tie(one_near, one_more, one_core, two, pieces, rest, cot_pieces)

    one_more_core = ring.to_core(one_more)
    two = ring.across(two)
    rest.update(ring.send(pieces, outer[1:]))
    one_near, one_more, one_core, one_more_core, two, pieces, rest, three = tie(
        one_near, one_more, one_core, one_more_core, two, pieces, rest, w_down
    )

    two_core = ring.to_core([[half] for half in two])
    two_more = ring.plane(two)
    rest.update(ring.send(pieces, inner))
    full_qkv, vectors = ring.assemble(ring.near_flat_sources(one_near, one_core, one_more, one_more_core), [3 * width, SMALL])
    two, two_core, two_more, rest, full_qkv, vectors, three = tie(two, two_core, two_more, rest, full_qkv, vectors, three)

    column = ring.spread(three, everything)
    two_more_core = ring.to_core(two_more)
    image_slots = jnp.concatenate([pieces[0]] + [rest[k] for k in everything]).reshape(group * slots, width)
    vectors = vectors.reshape(ring.count, rows, SMALL).astype(f32)
    bu = vectors[:, 0, 128 : 128 + wide * rows].reshape(ff)
    bq, bv, bo, bd, g1, s1, g2, s2 = [vectors[:, k, :rows].reshape(width) for k in range(8)]
    here = (image_slots[:, :1].astype(f32) < 0.5 * ABSENT).reshape(group, slots)
    held = jnp.sum(here.astype(f32), axis=1)
    before = jnp.sum(jnp.where(np.tril(np.ones((group, group), bool), -1), held[None, :], 0.0), axis=1)
    rank = before[:, None] + lax.broadcasted_iota(jnp.int32, (group, slots), 1).astype(f32)
    rank = jnp.where(here, rank, -1.0).reshape(1, group * slots).astype(jnp.int32)
    packing = (rank == lax.broadcasted_iota(jnp.int32, (PACKED, group * slots), 0)).astype(bf16)
    tokens_f, normed = pack_norm(packing, image_slots, g1, s1)
    qkv_bias = halved(jnp.concatenate([bq, jnp.zeros((width,), f32), bv]))
    qkv = project(normed, full_qkv, qkv_bias)
    mixed, logs = attend(qkv)
    three = ring.along(three, column)
    two_more_core, three, mixed = tie(two_more_core, three, mixed)

    three = ring.across(three)
    cot_rest = ring.send(cot_pieces, outer)
    full_out, full_up = ring.assemble(ring.sources(two, two_core, two_more, two_more_core), [width, ff])
    residual, normed_two = out_norm(mixed, full_out, tokens_f, bo, g2, s2)
    three, normed_two, cot_rest = tie(three, normed_two, cot_rest)

    three_more = ring.plane(three)
    three_core = ring.to_core([[half] for half in three])
    cot_rest.update(ring.send(cot_pieces, inner))
    ranks = ring.far(lax.broadcasted_iota(jnp.int32, (ring.count,), 0))
    active, slope, active_far = rise(normed_two, full_up, bu, ranks)
    if active_far is None:
        active_far = ring.by_distance(active, ring.target(ff))
    two_far = ring.by_distance(normed_two, target)
    three, three_more, three_core, active, active_far, two_far, cot_rest = tie(
        three, three_more, three_core, active, active_far, two_far, cot_rest
    )

    three_more_core = ring.to_core(three_more)
    share = (lax.axis_index(("sz", "sc")) % twins == 0).astype(f32) if twins > 1 else None
    cot_slots = jnp.concatenate([cot_pieces[0]] + [cot_rest[k] for k in everything]).reshape(group * slots, width)
    grad_low, grad_bd = pack(packing, cot_slots)
    sent = weight_grad(active_far, 1, grad_low, share)
    three_more_core, sent, grad_low = tie(three_more_core, sent, grad_low)

    d = ring.swap(sent)
    (full_down,) = ring.assemble(ring.sources(three, three_core, three_more, three_more_core), [width])
    d, full_down = tie(d, full_down)

    d = ring.kept(active_far, grad_low, share, d)
    result = slots_of(land(active, full_down, residual, bd, packing))
    d, result, mixed = tie(d, result, mixed)

    d = ring.first(d)
    mixed_far = ring.by_distance(mixed, target)
    back = ring.send(result, inner, -1)
    hidden_low, grad_bu = fall(grad_low, full_down, slope)
    sent = weight_grad(two_far, 1, hidden_low, share)
    d, sent, back, mixed_far = tie(d, sent, back, mixed_far)

    d = ring.again(d)
    d, sent = tie(d, sent)

    d = ring.second(d)
    u = ring.swap(sent)
    back.update(ring.send(result, outer[:1], -1))
    grad_residual, residual_low, sums_two = back_norm([hidden_low], full_up, residual, g2, grad_low)
    d, u, residual_low, back = tie(d, u, residual_low, back)

    d = ring.last(d)
    u = ring.kept(two_far, hidden_low, share, u)
    sent = weight_grad(mixed_far, 1, residual_low, share)
    d, u, sent, residual_low, normed = tie(d, u, sent, residual_low, normed)

    u = ring.first(u)
    gone = ring.toward_some(d, outer)
    back.update(ring.send(result, outer[1:], -1))
    grad_mixed = back_project(residual_low, full_out)
    sent_out = sent
    half_grads = attend_back(qkv, logs, grad_mixed)
    normed_far = ring.by_distance(normed, target)
    u, sent_out, d, gone, grad_mixed, half_grads, back, normed_far = tie(
        u, sent_out, d, gone, grad_mixed, half_grads, back, normed_far
    )

    u = ring.again(u)
    u, sent_out, back, d, grad_mixed, half_grads = tie(u, sent_out, back, d, grad_mixed, half_grads)

    u = ring.second(u)
    gone.update(ring.toward_some(d, inner))
    o = ring.swap(sent_out)
    grads, grad_sums = attend_back(qkv, logs, grad_mixed, half_grads)
    sent = weight_grad(normed_far, 1, grads, share)
    u, o, sent, grads, back, d, gone = tie(u, o, sent, grads, back, d, gone)
    d = [d[0]] + [gone[k] for k in everything]

    u = ring.last(u)
    u, sent, grads = tie(u, sent, grads)

    later = ring.toward_some(u, outer)
    q = ring.swap(sent)
    grad_tokens, sums_one = back_norm([grads], full_qkv, tokens_f, g1, grad_residual, packing)
    grad_tokens = slots_of(grad_tokens)
    u, later, o, q, grads, grad_tokens, sums_one, back, d = tie(u, later, o, q, grads, grad_tokens, sums_one, back, d)

    sent_back = ring.send(grad_tokens, outer, -1)
    q = ring.kept(normed_far, grads, share, q)
    o = ring.reshaped(weight_grad(mixed_far, 0, residual_low, share, o))
    joined_sum = whole(grad_sums[0])
    grad_bq, grad_bv = joined_sum[:width], joined_sum[2 * width :]
    small = [grad_bq, grad_bv, sums_two[2], grad_bd, sums_one[0], sums_one[1], sums_two[0], sums_two[1]]
    small = [array.reshape(ring.count, rows) for array in small] + [grad_bu.reshape(ring.count, wide * rows)]
    small = jnp.concatenate(small, axis=1)
    small = (small if share is None else small * share).astype(bf16)
    near_first = (ranks[None, :] == lax.broadcasted_iota(jnp.int32, (ring.count, 1), 0)).astype(bf16)
    small = dot_float(near_first, small).astype(bf16)
    small = jnp.pad(small, ((0, 0), (0, rows * SMALL - small.shape[1]))).reshape(2, ring.count // 2 * rows, SMALL)
    q, o, small, u, sent_back, grad_tokens, back, d = tie(q, o, small, u, sent_back, grad_tokens, back, d)

    q = ring.first(q)
    sent_back.update(ring.send(grad_tokens, inner, -1))
    came = ring.swap(small[1])
    own = jnp.stack([result[0]] + [back[k] for k in everything])
    other = ring.swap(own[:, 1])
    q, came, sent_back, u, back, d, own, other = tie(q, came, sent_back, u, back, d, own, other)

    q = ring.again(q)
    small = ring.reshaped(total([small[0], came]).astype(bf16))
    o = ring.ready(jnp.concatenate([o, small], axis=-1))
    q, o, u, own, d = tie(q, o, u, own, d)

    q = ring.second(q)
    o = ring.first(o)
    later.update(ring.toward_some(u, inner))
    result = ring.images_of(own[:, 0], other, images, twins)
    result = jnp.where(slot < counts[:, :, None], result, jnp.asarray(0, bf16))
    o, later, result, q, d = tie(o, later, result, q, d)

    q = ring.last(q)
    o = ring.again(o)
    o, q, d = tie(o, q, d)

    q = ring.third(q)
    o = ring.second(o)
    u = [u[0]] + [later[k] for k in everything]
    grad_tokens, came = back_pieces(sent_back, grad_tokens[0])
    q, o, grad_tokens, came = tie(q, o, grad_tokens, came)

    o = ring.third(ring.last(o))
    grad_tokens = ring.images_of(grad_tokens, came, images, twins).astype(f32)

    sum_down, sum_up = total(d), total(u)
    o = total(o)
    sum_out = o[:, :width]
    sum_qkv = whole(total(q))
    small = o[:, width:].reshape(rows * SMALL)
    sum_bq, sum_bv, sum_bo, sum_bd, sum_g1, sum_s1, sum_g2, sum_s2 = [small[k * rows : (k + 1) * rows] for k in range(8)]
    sum_bu = small[8 * rows : (8 + wide) * rows]
    return (result, grad_tokens, sum_qkv, sum_bq, sum_bv, sum_out, sum_bo, sum_up, sum_bu, sum_down, sum_bd, sum_g1, sum_s1, sum_g2, sum_s2)


def solution(mesh):
    n_grp, n_seq = mesh.shape["grp"], mesh.shape["seq"]
    sizes = (n_grp // 2, 2, n_seq // 2, 2)
    fine = Mesh(mesh.devices.reshape(sizes), AXES)
    ring = Ring(sizes)
    grp, seq = AXES[:2], AXES[2:]
    by_token = P(grp, seq, None)
    rows, vec = P(AXES, None), P(AXES)
    in_specs = (by_token, P(grp, seq), rows, vec, vec, rows, vec, rows, vec, rows, vec, vec, vec, vec, vec, by_token)
    out_specs = (by_token, by_token, rows, vec, vec, rows, vec, rows, vec, rows, vec, vec, vec, vec, vec)

    def shards(*args):
        return layer(ring, *args)

    return jax.shard_map(shards, mesh=fine, in_specs=in_specs, out_specs=out_specs, check_vma=False)
```
